128 devices in a mesh: pb: 8 (over z, core), pa: 16 (over y, x).
Axes of the slice: x: 4, y: 4, z: 4, core: 2. Of those that a mesh axis runs over, the one named last changes fastest.
Arguments:
- queries: bfloat16 [16384, 3584], P(('pb', 'pa')), may hold values from -16 to 16
- passages: bfloat16 [65536, 3584], P(('pb', 'pa')), may hold values from -16 to 16
- hard_block_offsets: int32 [4096, 4], P(('pb', 'pa')), may hold values from 0 to 126, all different within a row; in each aligned block of 32 rows (0 to 31, 32 to 63, ...) at most 2 rows name the same one
- positive: int32 [16384], P(('pb', 'pa')), may hold values from 0 to 511
- context: bfloat16 [65536, 3584], P(('pb', 'pa')), may hold values from -24 to 24
- residual: bfloat16 [65536, 3584], P(('pb', 'pa')), may hold values from -6 to 6
- output_weight: bfloat16 [3584, 3584], P(('pb', 'pa')), may hold values from -0.09375 to 0.09375
- adapter_down_weight: bfloat16 [3584, 16], replicated, may hold values from -0.09375 to 0.09375
- adapter_up_weight: bfloat16 [16, 3584], replicated, may hold values from -1.5 to 1.5
- final_norm_weight: bfloat16 [3584], replicated, may hold values from 0.099609375 to 1.8984375
Outputs:
- query_gradient: float32 [16384, 3584], P(('pb', 'pa'))
- grad_passages: float32 [65536, 3584], P(('pb', 'pa'))
- grad_lora_down: float32 [3584, 16], P(('pb', 'pa'))
- grad_lora_up: float32 [16, 3584], P(None, ('pb', 'pa'))
The draws below stay inside these ranges and needn't reach their ends.
Inputs may be any that keep to these rules, and one draw needn't show every extreme that they name: `hard_block_offsets`: each row lists 4 different offsets. Query block k is paired with passage block (k // 32 + 1 + offset) modulo the number of devices. In each aligned block of 32 rows no offset appears more than 2 times, and some offset appears exactly 2 times.
All inputs are finite; a program needn't handle non-finite values.
Results may differ from the reference program's by a relative error of at most 0.0045.
Values may be sent and summed in bfloat16 or wider, within the bound.
A program may use at most 192 MiB of HBM per device.

```python
import math
import jax
import jax.numpy as jnp
import numpy as np
from jax import lax

MODEL_WIDTH = 3584
QBLOCKS = 32
BLOCK_ROWS = 4
HARD = 4
PASS_DEV = 512
ADAPTER_RANK = 16
RERUN_QUERIES = 16
TQ = 32
CAP = 2
NQ = 16384
NQB = 4096
NP = 65536
TOKENS = 65536
N_PB = 8
N_PA = 16


def embedding_pair(key):
    seeded = jax.random.fold_in(key, 5501)
    key_query, key_passage = jax.random.split(seeded, 2)
    queries = jax.random.normal(key_query, (NQ, MODEL_WIDTH), jnp.float32)
    passages = jax.random.normal(key_passage, (NP, MODEL_WIDTH), jnp.float32)
    return (jnp.clip(queries, -16.0, 16.0), jnp.clip(passages, -16.0, 16.0))


def draw_queries(key, part):
    return embedding_pair(key)[0].astype(jnp.bfloat16)


def draw_passages(key, part):
    return embedding_pair(key)[1].astype(jnp.bfloat16)


def plant(values, stream_key, smallest, largest):
    extent = values.shape
    spot = [jax.random.randint(jax.random.fold_in(stream_key, axis), (), 0, extent[axis]) for axis in range(len(extent))]
    values = values.at[tuple(spot)].set(smallest)
    longest = extent.index(max(extent))
    spot[longest] = (spot[longest] + 1) % extent[longest]
    return values.at[tuple(spot)].set(largest)


def strengthened(values, rng, source, target, parts, factor):
    def block_of(axis_at):
        return (jnp.arange(values.shape[axis_at]) // (values.shape[axis_at] // parts)).reshape((-1,) + (1,) * (values.ndim - 1 - axis_at))

    near = jax.random.permutation(rng, parts)[block_of(target)]
    far = (block_of(target) + parts // 2) % parts
    return jnp.where((block_of(source) == near) | (block_of(source) == far), factor * values, values)


def level_of(rng, shape, cuts, smallest, high):
    factor_of, own = 1.0, jax.random.fold_in(rng, 6)
    for dim, parts in cuts:
        steps = jnp.exp(jax.random.uniform(jax.random.fold_in(own, dim), (parts,), jnp.float32, smallest / len(cuts), high / len(cuts)))
        factor_of = factor_of * jnp.repeat(steps, shape[dim] // parts).reshape([-1 if axis == dim else 1 for axis in range(len(shape))])
    return factor_of


def deal_out(own_key, own, number, rows, count, top, limit, lean):
    sequence = jax.random.permutation(own_key, count)
    crowded, usual = shares(count, rows * top, limit, lean, True), shares(count, rows * top, limit, lean, False)
    places = jnp.arange(count)

    def named(tallies, turn):
        used = int((tallies > 0).sum())
        fixed = max(1, used // 4)
        moved = fixed + (places - fixed + turn * (used - fixed)) % max(1, count - fixed)
        return jnp.zeros((count,), jnp.int32).at[sequence[jnp.where(places < fixed, places, moved)]].set(jnp.asarray(tallies, jnp.int32))

    tallies = jnp.where(number % 4 == 0, named(crowded, number // 4), named(usual, number - number // 4 - 1))
    mixed = jax.random.permutation(jax.random.fold_in(own, 3), count)
    donor, sink = mixed[0:count // 2 * 2:2], mixed[1:count // 2 * 2:2]
    room = jnp.minimum(tallies[donor] - 1, limit - tallies[sink]) // 2
    room = jnp.where((donor == sequence[0]) | (sink == sequence[0]) | (tallies[sink] == 0), 0, jnp.maximum(room, 0))
    moved = jax.random.randint(jax.random.fold_in(own, 4), (count // 2,), 0, 1 << 20) % (room + 1)
    tallies = tallies.at[donor].add(-moved).at[sink].add(moved)
    members = jnp.searchsorted(jnp.cumsum(tallies), jnp.arange(rows * top), side="right").astype(jnp.int32)
    listing = members.reshape(top, rows).T
    listing = listing[jax.random.permutation(jax.random.fold_in(own, 1), rows)]
    turn = jax.random.randint(jax.random.fold_in(own, 2), (rows, 1), 0, top)
    return jnp.take_along_axis(listing, (jnp.arange(top)[None, :] + turn) % top, axis=1)


def shares(amount, total, reach, slope, full):
    portions = [(1 << 20) // math.isqrt(rank ** slope) + 1 for rank in range(1, amount + 1)]
    largest = reach if full else min(reach, max(-(-total // amount), total * portions[0] // sum(portions)))
    least = 1 if total - largest >= amount - 1 else 0
    holding, surplus = [largest] + [least] * (amount - 1), total - largest - least * (amount - 1)
    while surplus > 0:
        free = [i for i in range(1, amount) if holding[i] < largest] or [i for i in range(1, amount) if holding[i] < reach]
        pool, budget = sum([portions[i] for i in free]), surplus
        for i in free:
            addition = min(reach - holding[i], max(1, budget * portions[i] // pool), surplus)
            holding[i] = holding[i] + addition
            surplus = surplus - addition
    return np.array(holding)


def normal_values(own_key, shape, scale, limit, cuts=(), held_as=jnp.bfloat16):
    values = scale * jax.random.normal(own_key, shape, jnp.float32)
    if cuts:
        values = values * level_of(own_key, shape, cuts, -0.22, 0.18)
    return jnp.clip(values, -limit, limit).astype(held_as)


def noise_with(stream_key, extent, width, reach, cuts, heavy, kind=jnp.bfloat16):
    values = width * jax.random.normal(stream_key, extent, jnp.float32)
    if cuts:
        values = values * level_of(stream_key, extent, cuts, -0.22, 0.18)
    return jnp.clip(strengthened(values, jax.random.fold_in(stream_key, 3), *heavy), -reach, reach).astype(kind)


def setup_inputs(seed: int = 0) -> dict:
    keys = jax.random.split(jax.random.key(seed), 11)
    queries = draw_queries(jax.random.fold_in(keys[10], 71), 0)
    passages = draw_passages(jax.random.fold_in(keys[10], 71), 0)
    hard_block_offsets_keys = jax.random.split(jax.random.fold_in(keys[2], 1), NQB // QBLOCKS)
    hard_block_offsets_turns = jax.random.permutation(jax.random.fold_in(keys[2], 3), NQB // QBLOCKS)
    hard_block_offsets = jax.vmap(lambda own, number: deal_out(jax.random.fold_in(keys[2], 2), own, number, QBLOCKS, N_PB * N_PA - 1, HARD, CAP, 2))(hard_block_offsets_keys, hard_block_offsets_turns).reshape((NQB, HARD))
    positive = plant(jax.random.randint(keys[3], (NQ,), 0, PASS_DEV), jax.random.fold_in(keys[3], 1), 0, PASS_DEV - 1).astype(jnp.int32)
    context = noise_with(keys[4], (TOKENS, MODEL_WIDTH), 1.0, 24.0, ((0, 128),), (0, 1, 128, 5.5))
    residual = normal_values(keys[5], (TOKENS, MODEL_WIDTH), 1.0, 6.0, ((0, 128),))
    output_weight = normal_values(keys[6], (MODEL_WIDTH, MODEL_WIDTH), MODEL_WIDTH ** -0.5, 0.09375, ((0, 128),))
    adapter_down_weight = normal_values(keys[7], (MODEL_WIDTH, ADAPTER_RANK), MODEL_WIDTH ** -0.5, 0.09375)
    adapter_up_weight = normal_values(keys[8], (ADAPTER_RANK, MODEL_WIDTH), ADAPTER_RANK ** -0.5, 1.5)
    final_norm_weight = jnp.clip(1.0 + 0.18 * jax.random.normal(keys[9], (MODEL_WIDTH,), jnp.float32), 0.099609375, 1.8984375).astype(jnp.bfloat16)
    return {"queries": queries, "passages": passages, "hard_block_offsets": hard_block_offsets, "positive": positive, "context": context, "residual": residual, "output_weight": output_weight, "adapter_down_weight": adapter_down_weight, "adapter_up_weight": adapter_up_weight, "final_norm_weight": final_norm_weight}


inverse_temp = 2.0
loss_scale = 32.0
adapter_scale = 2.0
epsilon = 1e-06
absent_mass = 1e+30

def slot_layout(offsets, source, device_count, capacity):
    flat_offsets = offsets.reshape(-1)
    target = (source + 1 + flat_offsets) % device_count
    pair_order = jnp.arange(flat_offsets.shape[0], dtype=jnp.int32)
    earlier = (target[:, None] == target[None, :]) & (pair_order[:, None] > pair_order[None, :])
    slot_rank = lax.optimization_barrier(jnp.sum(earlier.astype(jnp.int32), axis=1)).astype(jnp.int32)
    slot_index = (target * capacity + slot_rank).astype(jnp.int32)
    slot_block = jnp.full((device_count * capacity,), -1, jnp.int32).at[slot_index].set(pair_order // offsets.shape[1])
    return (slot_index, slot_block)

def partial_softmax(query_rows, passage_rows, score_scale):
    scores = jnp.dot(query_rows, passage_rows.T, preferred_element_type=jnp.float32) * score_scale
    row_peak = lax.optimization_barrier(jnp.max(scores, axis=1))
    weights = jnp.exp(scores - row_peak[:, None])
    row_mass = lax.optimization_barrier(jnp.sum(weights, axis=1))
    row_mean = jnp.dot(weights.astype(jnp.bfloat16), passage_rows, preferred_element_type=jnp.float32) / row_mass[:, None]
    return (scores, row_peak + jnp.log(row_mass), row_mean)

def merge_partials(near_mass, near_mean, far_mass, far_mean):
    block_count, hard_count, block_rows = far_mass.shape
    far_rows = jnp.transpose(far_mass, (0, 2, 1)).reshape(block_count * block_rows, hard_count)
    every_mass = jnp.concatenate([near_mass[:, None], far_rows], axis=1)
    mass_peak = lax.optimization_barrier(jnp.max(every_mass, axis=1))
    log_total = mass_peak + jnp.log(lax.optimization_barrier(jnp.sum(jnp.exp(every_mass - mass_peak[:, None]), axis=1)))
    near_share = jnp.exp(near_mass - log_total)
    far_share = jnp.exp(far_mass - log_total.reshape(block_count, 1, block_rows))
    far_part = lax.optimization_barrier(jnp.sum(far_mean * far_share[..., None], axis=1)).reshape(block_count * block_rows, -1)
    return (log_total, near_share[:, None] * near_mean + far_part)

def layer_parts(context, residual, frozen_output, adapter_down_weight, adapter_up_weight, final_norm_weight, output_gradient):
    token_count = context.shape[0]
    narrow_projection = jnp.dot(context, adapter_down_weight, preferred_element_type=jnp.float32).astype(jnp.bfloat16)
    hidden_state = residual.astype(jnp.float32) + frozen_output + adapter_scale * jnp.dot(narrow_projection, adapter_up_weight, preferred_element_type=jnp.float32)
    inverse_rms = lax.rsqrt(lax.optimization_barrier(jnp.mean(hidden_state * hidden_state, axis=1, keepdims=True)) + epsilon)
    spread_cot = jnp.broadcast_to(output_gradient[:, None, :] / TQ, (output_gradient.shape[0], TQ, output_gradient.shape[1])).reshape(token_count, -1)
    scaled = final_norm_weight.astype(jnp.float32)[None, :] * spread_cot
    grad_hidden = inverse_rms * scaled - hidden_state * inverse_rms ** 3 * lax.optimization_barrier(jnp.mean(hidden_state * scaled, axis=1, keepdims=True))
    gradient_lowered = grad_hidden.astype(jnp.bfloat16)
    product_dims = (((0,), (0,)), ((), ()))
    up_product = adapter_scale * lax.dot_general(narrow_projection, gradient_lowered, product_dims, preferred_element_type=jnp.float32) / RERUN_QUERIES
    gradient_narrow = (adapter_scale * jnp.dot(gradient_lowered, adapter_up_weight.T, preferred_element_type=jnp.float32)).astype(jnp.bfloat16)
    down_term = lax.dot_general(context, gradient_narrow, product_dims, preferred_element_type=jnp.float32) / RERUN_QUERIES
    return (down_term, up_product)

def reference(queries, passages, hard_block_offsets, positive, context, residual, output_weight, adapter_down_weight, adapter_up_weight, final_norm_weight):
    device_count = N_PB * N_PA
    capacity = CAP
    query_count = QBLOCKS * BLOCK_ROWS
    score_scale = inverse_temp / math.sqrt(MODEL_WIDTH)
    query_grid = queries.reshape(device_count, query_count, MODEL_WIDTH)
    passage_grid = passages.reshape(device_count, PASS_DEV, MODEL_WIDTH)
    offset_grid = hard_block_offsets.reshape(device_count, QBLOCKS, HARD)
    sources = jnp.arange(device_count, dtype=jnp.int32)
    slot_grid, holder_grid = jax.vmap(lambda offsets, source: slot_layout(offsets, source, device_count, capacity))(offset_grid, sources)
    query_blocks = query_grid.reshape(device_count, QBLOCKS, BLOCK_ROWS, MODEL_WIDTH)

    def gather_slots(owner_index):
        slot_blocks = lax.dynamic_slice_in_dim(holder_grid, owner_index * capacity, capacity, 1)
        picked = query_blocks[sources[:, None], jnp.maximum(slot_blocks, 0)]
        picked = jnp.where((slot_blocks >= 0)[:, :, None, None], picked, jnp.zeros_like(picked))
        return (picked.reshape(-1, MODEL_WIDTH), slot_blocks)

    def owner_forward(owner_index):
        picked, slot_blocks = gather_slots(owner_index)
        scores, row_mass, row_mean = partial_softmax(picked, passage_grid[owner_index], score_scale)
        return (row_mass, row_mean.astype(jnp.bfloat16))
    far_masses, far_means = lax.map(owner_forward, sources)
    owner_grid = slot_grid // capacity
    place_grid = (sources[:, None] * capacity + slot_grid % capacity) * BLOCK_ROWS
    row_offsets = jnp.arange(BLOCK_ROWS, dtype=jnp.int32)
    far_mass_all = far_masses[owner_grid[:, :, None], place_grid[:, :, None] + row_offsets[None, None, :]]
    far_mean_all = far_means[owner_grid[:, :, None], place_grid[:, :, None] + row_offsets[None, None, :]]

    def query_side(pieces):
        own_queries, own_passages, own_positive, far_mass, far_mean = pieces
        near_scores, near_mass, near_mean = partial_softmax(own_queries, own_passages, score_scale)
        far_mass = far_mass.reshape(QBLOCKS, HARD, BLOCK_ROWS)
        far_mean = far_mean.reshape(QBLOCKS, HARD, BLOCK_ROWS, MODEL_WIDTH)
        log_total, mixed = merge_partials(near_mass, near_mean, far_mass, far_mean)
        positive_hot = own_positive[:, None] == jnp.arange(PASS_DEV, dtype=jnp.int32)[None, :]
        positive_rows = jnp.dot(positive_hot.astype(jnp.bfloat16), own_passages, preferred_element_type=jnp.float32)
        return (loss_scale * score_scale * (mixed - positive_rows), log_total)
    grads_q, log_totals = lax.map(query_side, (query_grid, passage_grid, positive.reshape(device_count, query_count), far_mass_all, far_mean_all))
    log_blocks = log_totals.reshape(device_count, QBLOCKS, BLOCK_ROWS)

    def owner_backward(pieces):
        owner_index, own_queries, own_passages, own_positive, own_log = pieces
        picked, slot_blocks = gather_slots(owner_index)
        far_log = log_blocks[sources[:, None], jnp.maximum(slot_blocks, 0)]
        far_log = jnp.where((slot_blocks >= 0)[:, :, None], far_log, absent_mass).reshape(-1)
        far_scores = jnp.dot(picked, own_passages.T, preferred_element_type=jnp.float32) * score_scale
        far_weight = jnp.exp(far_scores - far_log[:, None]).astype(jnp.bfloat16)
        near_scores = jnp.dot(own_queries, own_passages.T, preferred_element_type=jnp.float32) * score_scale
        positive_hot = own_positive[:, None] == jnp.arange(PASS_DEV, dtype=jnp.int32)[None, :]
        near_weight = (jnp.exp(near_scores - own_log[:, None]) - positive_hot.astype(jnp.float32)).astype(jnp.bfloat16)
        product_dims = (((0,), (0,)), ((), ()))
        far_grad = lax.dot_general(far_weight, picked, product_dims, preferred_element_type=jnp.float32)
        near_grad = lax.dot_general(near_weight, own_queries, product_dims, preferred_element_type=jnp.float32)
        return loss_scale * score_scale * (far_grad + near_grad)
    grads_p = lax.map(owner_backward, (sources, query_grid, passage_grid, positive.reshape(device_count, query_count), log_totals))
    cotangents = grads_q[:, :RERUN_QUERIES]
    context_grid = context.reshape(device_count, RERUN_QUERIES * TQ, MODEL_WIDTH)
    residual_grid = residual.reshape(device_count, RERUN_QUERIES * TQ, MODEL_WIDTH)

    def device_layer(pieces):
        local_context, local_residual, output_gradient = pieces
        frozen_output = jnp.dot(local_context, output_weight, preferred_element_type=jnp.float32)
        return layer_parts(local_context, local_residual, frozen_output, adapter_down_weight, adapter_up_weight, final_norm_weight, output_gradient)
    down_terms, up_terms = lax.map(device_layer, (context_grid, residual_grid, cotangents))
    return (grads_q.reshape(-1, MODEL_WIDTH), grads_p.reshape(-1, MODEL_WIDTH), lax.optimization_barrier(jnp.sum(down_terms, axis=0)), lax.optimization_barrier(jnp.sum(up_terms, axis=0)))
```

```python
import math

import jax
import jax.numpy as jnp
from jax import lax
from jax.sharding import Mesh
from jax.sharding import PartitionSpec as P

MODEL_WIDTH = 3584
RERUN_QUERIES = 16
TQ = 32
PB_PA = ("pb_0", "pb_1", "pa_0", "pa_1")
CHIPS = ("pb_0", "pa_0", "pa_1")

inverse_temp = 2.0
loss_scale = 32.0
adapter_scale = 2.0
epsilon = 1e-06
absent_mass = 1e30
f32 = jnp.float32
bf16 = jnp.bfloat16


def dot(a, b, **kw):
    return jnp.dot(a, b, preferred_element_type=f32, **kw)


def two_parts(x):
    high = x.astype(bf16)
    return high, (x - high.astype(f32)).astype(bf16)


def device_of(chip, core, per_plane):
    return (chip // per_plane) * 2 * per_plane + core * per_plane + chip % per_plane


def gathered_weight_input(rows):
    count = lax.axis_size(PB_PA)
    per_plane = lax.axis_size("pa_0") * lax.axis_size("pa_1")
    half = rows.shape[1] // 2
    left, right = rows[:, :half], rows[:, half:]
    odd = lax.axis_index("pa_1") % 2 == 1
    core = lax.axis_index("pb_1")
    same = [(f, device_of(f // 2, f % 2, per_plane)) for f in range(count)]
    other = [(f, device_of(f // 2, 1 - f % 2, per_plane)) for f in range(count)]
    first = lax.ppermute(jnp.where(odd, right, left), PB_PA, same)
    second = lax.ppermute(jnp.where(odd, left, right), PB_PA, other)
    low = jnp.where(core == 0, first, second)
    high = jnp.where(core == 0, second, first)
    return jnp.concatenate([low, high], axis=0)


def exchange(array):
    return lax.all_to_all(array, PB_PA, split_axis=0, concat_axis=0, tiled=True)


def local(
    queries,
    passages,
    hard_block_offsets,
    positive,
    context,
    residual,
    output_weight,
    adapter_down_weight,
    adapter_up_weight,
    final_norm_weight,
):
    device_count = lax.axis_size(PB_PA)
    block_count, hard_count = hard_block_offsets.shape
    query_count = queries.shape[0]
    block_rows = query_count // block_count
    capacity = 2 * block_count * hard_count // device_count
    slot_rows = capacity * block_rows
    all_rows = device_count * slot_rows
    passage_count = passages.shape[0]
    score_scale = inverse_temp / math.sqrt(MODEL_WIDTH)

    weight_rows = gathered_weight_input(output_weight)

    source = lax.axis_index(PB_PA)
    target = ((source + 1 + hard_block_offsets) % device_count).reshape(-1)
    order = jnp.arange(target.shape[0], dtype=jnp.int32)
    earlier = (target[:, None] == target[None, :]) & (order[:, None] > order[None, :])
    slot = target * capacity + jnp.sum(earlier.astype(jnp.int32), axis=1)
    slot_of = slot.reshape(block_count, hard_count).T
    key = jnp.repeat(slot_of, block_rows, axis=1) * block_rows + (
        jnp.arange(query_count, dtype=jnp.int32) % block_rows
    )
    row_ids = jnp.arange(all_rows, dtype=jnp.int32)
    picks = row_ids[:, None] == key[0][None, :]
    for t in range(1, hard_count):
        picks = picks | (row_ids[:, None] == key[t][None, :])
    outgoing = jnp.dot(picks.astype(bf16), queries, preferred_element_type=bf16)
    arrived = exchange(outgoing.reshape(device_count, slot_rows, MODEL_WIDTH))
    arrived = arrived.reshape(-1, MODEL_WIDTH)

    half_weight = lax.all_gather(weight_rows, CHIPS, axis=0, tiled=True)
    near_scores = dot(queries, passages.T) * score_scale
    near_peak = jnp.max(near_scores, axis=1)
    near_exp = jnp.exp(near_scores - near_peak[:, None])
    near_sum = jnp.sum(near_exp, axis=1)
    near_mass = near_peak + jnp.log(near_sum)
    positive_hot = positive[:, None] == jnp.arange(passage_count, dtype=jnp.int32)[None, :]
    stacked = dot(
        jnp.concatenate([near_exp.astype(bf16), positive_hot.astype(bf16)], axis=0), passages
    )

    far_scores = dot(arrived, passages.T) * score_scale
    far_peak = jnp.max(far_scores, axis=1)
    far_exp = jnp.exp(far_scores - far_peak[:, None])
    far_sum = jnp.sum(far_exp, axis=1)
    far_mass = far_peak + jnp.log(far_sum)
    far_mean = (dot(far_exp.astype(bf16), passages) / far_sum[:, None]).astype(bf16)
    returned = exchange(far_mean.reshape(device_count, slot_rows, MODEL_WIDTH))
    returned = returned.reshape(-1, MODEL_WIDTH)
    far_mass, _ = lax.optimization_barrier((far_mass, far_mean))
    returned_mass = exchange(far_mass.reshape(device_count, slot_rows)).reshape(-1)
    half_weight, returned_mass = lax.optimization_barrier((half_weight, returned_mass))
    both_halves = lax.all_gather(half_weight, "pb_1", axis=0, tiled=False)

    hits = [key[t][:, None] == row_ids[None, :] for t in range(hard_count)]
    masses = [near_mass] + [
        jnp.sum(jnp.where(hit, returned_mass[None, :], 0.0), axis=1) for hit in hits
    ]
    peak = masses[0]
    for mass in masses[1:]:
        peak = jnp.maximum(peak, mass)
    total = jnp.exp(masses[0] - peak)
    for mass in masses[1:]:
        total = total + jnp.exp(mass - peak)
    log_total = peak + jnp.log(total)

    filled = jnp.any(picks, axis=1)
    log_outgoing = jnp.where(
        filled, jnp.sum(jnp.where(picks, log_total[None, :], 0.0), axis=1), absent_mass
    )
    log_arrived = exchange(log_outgoing.reshape(device_count, slot_rows)).reshape(-1)

    mix = jnp.zeros((query_count, all_rows), f32)
    for t in range(hard_count):
        mix = jnp.where(hits[t], jnp.exp(masses[1 + t] - log_total)[:, None], mix)
    mix_parts = jnp.concatenate(two_parts(mix), axis=0)
    near_share = jnp.exp(near_mass - log_total)
    near_part = (near_share / near_sum)[:, None] * stacked[:query_count] - stacked[query_count:]

    product_dims = (((0,), (0,)), ((), ()))
    far_weight = jnp.exp(far_scores - log_arrived[:, None]).astype(bf16)
    near_weight = (
        jnp.exp(near_scores - log_total[:, None]) - positive_hot.astype(f32)
    ).astype(bf16)
    far_grad = lax.dot_general(far_weight, arrived, product_dims, preferred_element_type=f32)
    near_grad = lax.dot_general(near_weight, queries, product_dims, preferred_element_type=f32)
    grad_passages = loss_scale * score_scale * (far_grad + near_grad)

    narrow = dot(context, adapter_down_weight).astype(bf16)
    frozen = jnp.concatenate([dot(context, both_halves[0]), dot(context, both_halves[1])], axis=1)
    hidden = residual.astype(f32) + frozen + adapter_scale * dot(narrow, adapter_up_weight)
    inverse_rms = lax.rsqrt(jnp.mean(hidden * hidden, axis=1, keepdims=True) + epsilon)
    hidden_low = hidden.astype(bf16)
    hidden_up = dot(hidden_low, adapter_up_weight.T)
    token_query = jnp.arange(context.shape[0], dtype=jnp.int32) // TQ
    of_query = token_query[:, None] == jnp.arange(RERUN_QUERIES, dtype=jnp.int32)[None, :]
    narrow_sums = jnp.sum(
        (inverse_rms * narrow.astype(f32)).reshape(RERUN_QUERIES, TQ, -1), axis=1
    )

    returned, hidden_low, hidden_up, inverse_rms, narrow_sums = lax.optimization_barrier(
        (returned, hidden_low, hidden_up, inverse_rms, narrow_sums)
    )
    far_part = dot(mix_parts, returned)
    query_gradient = (loss_scale * score_scale) * (
        far_part[:query_count] + far_part[query_count:] + near_part
    )

    scaled = final_norm_weight.astype(f32)[None, :] * (query_gradient[:RERUN_QUERIES] / TQ)
    products = dot(hidden_low, scaled.astype(bf16).T)
    mean = jnp.sum(jnp.where(of_query, products, 0.0), axis=1, keepdims=True) / MODEL_WIDTH
    slope = inverse_rms**3 * mean
    scaled_up = dot(scaled, adapter_up_weight.astype(f32).T, precision=lax.Precision.HIGHEST)
    spread_up = jnp.broadcast_to(
        scaled_up[:, None, :], (RERUN_QUERIES, TQ, scaled_up.shape[1])
    ).reshape(context.shape[0], -1)
    grad_narrow = (adapter_scale * (inverse_rms * spread_up - slope * hidden_up)).astype(bf16)
    down_term = lax.dot_general(grad_narrow, context, product_dims, preferred_element_type=f32)
    weighted = (slope * narrow.astype(f32)).astype(bf16)
    up_term = adapter_scale * (
        lax.dot_general(
            narrow_sums,
            scaled,
            product_dims,
            precision=lax.Precision.HIGHEST,
            preferred_element_type=f32,
        )
        - lax.dot_general(weighted, hidden_low, product_dims, preferred_element_type=f32)
    )
    terms = jnp.concatenate([down_term, up_term], axis=0) / RERUN_QUERIES
    rank = narrow.shape[1]
    columns = MODEL_WIDTH // device_count
    pieces = jnp.transpose(terms.reshape(2 * rank, device_count, columns), (1, 0, 2))
    sums = jnp.sum(exchange(pieces.reshape(device_count, -1)), axis=0).reshape(2 * rank, columns)
    return (query_gradient, grad_passages, sums[:rank].T, sums[rank:])


def solution(mesh):
    torus = Mesh(mesh.devices.reshape(4, 2, 4, 4), PB_PA)
    in_specs = (
        P(PB_PA, None),
        P(PB_PA, None),
        P(PB_PA, None),
        P(PB_PA),
        P(PB_PA, None),
        P(PB_PA, None),
        P(PB_PA, None),
        P(),
        P(),
        P(),
    )
    out_specs = (P(PB_PA, None), P(PB_PA, None), P(PB_PA, None), P(None, PB_PA))
    return jax.shard_map(local, mesh=torus, in_specs=in_specs, out_specs=out_specs, check_vma=False)
```

```python
import math

import jax
import jax.numpy as jnp
from jax import lax
from jax.experimental import pallas as pl
from jax.experimental.pallas import tpu as pltpu
from jax.sharding import Mesh
from jax.sharding import PartitionSpec as P

MODEL_WIDTH = 3584
RERUN_QUERIES = 16
TQ = 32
PB_PA = ("pb_0", "pb_1", "pa_0", "pa_1")
CHIPS = ("pb_0", "pa_0", "pa_1")

inverse_temp = 2.0
loss_scale = 32.0
adapter_scale = 2.0
epsilon = 1e-06
absent_mass = 1e30
f32 = jnp.float32
bf16 = jnp.bfloat16
MESH = pl.DeviceIdType.MESH


def dot(a, b, **kw):
    return jnp.dot(a, b, preferred_element_type=f32, **kw)


def two_parts(x):
    high = x.astype(bf16)
    return high, (x - high.astype(f32)).astype(bf16)


def device_of(chip, core, per_plane):
    return (chip // per_plane) * 2 * per_plane + core * per_plane + chip % per_plane


def gathered_weight_input(rows):
    count = lax.axis_size(PB_PA)
    per_plane = lax.axis_size("pa_0") * lax.axis_size("pa_1")
    half = rows.shape[1] // 2
    left, right = rows[:, :half], rows[:, half:]
    odd = lax.axis_index("pa_1") % 2 == 1
    core = lax.axis_index("pb_1")
    same = [(f, device_of(f // 2, f % 2, per_plane)) for f in range(count)]
    other = [(f, device_of(f // 2, 1 - f % 2, per_plane)) for f in range(count)]
    first = lax.ppermute(jnp.where(odd, right, left), PB_PA, same)
    second = lax.ppermute(jnp.where(odd, left, right), PB_PA, other)
    low = jnp.where(core == 0, first, second)
    high = jnp.where(core == 0, second, first)
    return jnp.concatenate([low, high], axis=0)


def exchange(array):
    return lax.all_to_all(array, PB_PA, split_axis=0, concat_axis=0, tiled=True)


def layer_forward_kernel(
    context, half_weight, residual, down, up, hidden, narrow, hidden_up, inverse,
    own, other, own_sem, send_sem, recv_sem, squares,
):
    core = lax.axis_index("pb_1")
    twin = (lax.axis_index("pb_0"), 1 - core, lax.axis_index("pa_0"), lax.axis_index("pa_1"))
    tile = own.shape[2]
    half = half_weight.shape[1]
    tiles = half // tile
    barrier = pltpu.get_barrier_semaphore()
    pl.semaphore_signal(barrier, inc=1, device_id=twin, device_id_type=MESH)
    pl.semaphore_wait(barrier, 1)

    def columns(j):
        return pl.ds(pl.multiple_of(j * tile, tile), tile)

    def sent(j):
        return pltpu.make_async_remote_copy(
            half_weight.at[:, columns(j)], other.at[j], send_sem.at[j], recv_sem.at[j],
            device_id=twin, device_id_type=MESH,
        )

    def fetched(j):
        return pltpu.make_async_copy(
            half_weight.at[:, columns(j)], own.at[lax.rem(j, 2)], own_sem.at[lax.rem(j, 2)]
        )

    fetched(0).start()

    def send(j, carry):
        sent(j).start()
        return carry

    lax.fori_loop(0, tiles, send, 0)
    low = lax.dot_general(
        context[...], down[...], (((1,), (1,)), ((), ())), preferred_element_type=f32
    ).astype(bf16)
    narrow[...] = low.astype(f32)
    squares[...] = jnp.zeros_like(squares)
    hidden_up[...] = jnp.zeros_like(hidden_up)

    def step(weight, start):
        at = pl.ds(pl.multiple_of(start, tile), tile)
        up_tile = up[:, at]
        value = (
            residual[:, at].astype(f32)
            + jnp.dot(context[...], weight, preferred_element_type=f32)
            + adapter_scale * jnp.dot(low, up_tile, preferred_element_type=f32)
        )
        squares[...] += jnp.sum(value * value, axis=1, keepdims=True)
        value = value.astype(bf16)
        hidden[:, at] = value
        hidden_up[...] += lax.dot_general(
            value, up_tile, (((1,), (1,)), ((), ())), preferred_element_type=f32
        )

    def own_step(j, carry):
        fetched(j).wait()

        @pl.when(j + 1 < tiles)
        def _():
            fetched(j + 1).start()

        step(own[lax.rem(j, 2)], core * half + j * tile)
        return carry

    lax.fori_loop(0, tiles, own_step, 0)

    def other_step(j, carry):
        sent(j).wait_recv()
        step(other[j], (1 - core) * half + j * tile)
        return carry

    lax.fori_loop(0, tiles, other_step, 0)
    inverse[...] = lax.rsqrt(squares[...] / MODEL_WIDTH + epsilon)

    def done(j, carry):
        sent(j).wait_send()
        return carry

    lax.fori_loop(0, tiles, done, 0)


def layer_forward(context, half_weight, residual, down, up):
    tokens, width = context.shape
    half = half_weight.shape[1]
    tile = 256
    tiles = half // tile
    rank = up.shape[0]
    vmem = pl.BlockSpec(memory_space=pltpu.VMEM)
    return pl.pallas_call(
        layer_forward_kernel,
        out_shape=(
            jax.ShapeDtypeStruct((tokens, width), bf16),
            jax.ShapeDtypeStruct((tokens, rank), f32),
            jax.ShapeDtypeStruct((tokens, rank), f32),
            jax.ShapeDtypeStruct((tokens, 1), f32),
        ),
        in_specs=[vmem, pl.BlockSpec(memory_space=pl.ANY), vmem, vmem, vmem],
        out_specs=(vmem, vmem, vmem, vmem),
        scratch_shapes=[
            pltpu.VMEM((2, width, tile), bf16),
            pltpu.VMEM((tiles, width, tile), bf16),
            pltpu.SemaphoreType.DMA((2,)),
            pltpu.SemaphoreType.DMA((tiles,)),
            pltpu.SemaphoreType.DMA((tiles,)),
            pltpu.VMEM((tokens, 1), f32),
        ],
        compiler_params=pltpu.CompilerParams(
            collective_id=1, has_side_effects=True, vmem_limit_bytes=44 * 1024 * 1024
        ),
        cost_estimate=pl.CostEstimate(flops=1000, bytes_accessed=1000, transcendentals=0),
        name="layer_forward",
    )(context, half_weight, residual, down, up)


def local(
    queries,
    passages,
    hard_block_offsets,
    positive,
    context,
    residual,
    output_weight,
    adapter_down_weight,
    adapter_up_weight,
    final_norm_weight,
):
    device_count = lax.axis_size(PB_PA)
    block_count, hard_count = hard_block_offsets.shape
    query_count = queries.shape[0]
    block_rows = query_count // block_count
    capacity = 2 * block_count * hard_count // device_count
    slot_rows = capacity * block_rows
    all_rows = device_count * slot_rows
    passage_count = passages.shape[0]
    score_scale = inverse_temp / math.sqrt(MODEL_WIDTH)

    weight_rows = gathered_weight_input(output_weight)

    source = lax.axis_index(PB_PA)
    target = ((source + 1 + hard_block_offsets) % device_count).reshape(-1)
    order = jnp.arange(target.shape[0], dtype=jnp.int32)
    earlier = (target[:, None] == target[None, :]) & (order[:, None] > order[None, :])
    slot = target * capacity + jnp.sum(earlier.astype(jnp.int32), axis=1)
    slot_of = slot.reshape(block_count, hard_count).T
    key = jnp.repeat(slot_of, block_rows, axis=1) * block_rows + (
        jnp.arange(query_count, dtype=jnp.int32) % block_rows
    )
    row_ids = jnp.arange(all_rows, dtype=jnp.int32)
    picks = row_ids[:, None] == key[0][None, :]
    for t in range(1, hard_count):
        picks = picks | (row_ids[:, None] == key[t][None, :])
    outgoing = jnp.dot(picks.astype(bf16), queries, preferred_element_type=bf16)
    arrived = exchange(outgoing.reshape(device_count, slot_rows, MODEL_WIDTH))
    arrived = arrived.reshape(-1, MODEL_WIDTH)

    half_weight = lax.all_gather(weight_rows, CHIPS, axis=0, tiled=True)
    near_scores = dot(queries, passages.T) * score_scale
    near_peak = jnp.max(near_scores, axis=1)
    near_exp = jnp.exp(near_scores - near_peak[:, None])
    near_sum = jnp.sum(near_exp, axis=1)
    near_mass = near_peak + jnp.log(near_sum)
    positive_hot = positive[:, None] == jnp.arange(passage_count, dtype=jnp.int32)[None, :]
    stacked = dot(
        jnp.concatenate([near_exp.astype(bf16), positive_hot.astype(bf16)], axis=0), passages
    )

    far_scores = dot(arrived, passages.T) * score_scale
    far_peak = jnp.max(far_scores, axis=1)
    far_exp = jnp.exp(far_scores - far_peak[:, None])
    far_sum = jnp.sum(far_exp, axis=1)
    far_mass = far_peak + jnp.log(far_sum)
    far_mean = (dot(far_exp.astype(bf16), passages) / far_sum[:, None]).astype(bf16)
    returned = exchange(far_mean.reshape(device_count, slot_rows, MODEL_WIDTH))
    returned = returned.reshape(-1, MODEL_WIDTH)
    returned_mass = exchange(far_mass.reshape(device_count, slot_rows)).reshape(-1)

    hits = [key[t][:, None] == row_ids[None, :] for t in range(hard_count)]
    masses = [near_mass] + [
        jnp.sum(jnp.where(hit, returned_mass[None, :], 0.0), axis=1) for hit in hits
    ]
    peak = masses[0]
    for mass in masses[1:]:
        peak = jnp.maximum(peak, mass)
    total = jnp.exp(masses[0] - peak)
    for mass in masses[1:]:
        total = total + jnp.exp(mass - peak)
    log_total = peak + jnp.log(total)

    filled = jnp.any(picks, axis=1)
    log_outgoing = jnp.where(
        filled, jnp.sum(jnp.where(picks, log_total[None, :], 0.0), axis=1), absent_mass
    )
    log_arrived = exchange(log_outgoing.reshape(device_count, slot_rows)).reshape(-1)

    mix = jnp.zeros((query_count, all_rows), f32)
    for t in range(hard_count):
        mix = jnp.where(hits[t], jnp.exp(masses[1 + t] - log_total)[:, None], mix)
    mix_parts = jnp.concatenate(two_parts(mix), axis=0)
    near_share = jnp.exp(near_mass - log_total)
    near_part = (near_share / near_sum)[:, None] * stacked[:query_count] - stacked[query_count:]

    product_dims = (((0,), (0,)), ((), ()))
    far_weight = jnp.exp(far_scores - log_arrived[:, None]).astype(bf16)
    near_weight = (
        jnp.exp(near_scores - log_total[:, None]) - positive_hot.astype(f32)
    ).astype(bf16)
    far_grad = lax.dot_general(far_weight, arrived, product_dims, preferred_element_type=f32)
    near_grad = lax.dot_general(near_weight, queries, product_dims, preferred_element_type=f32)

    hidden_low, narrow, hidden_up, inverse_rms = layer_forward(
        context, half_weight, residual, adapter_down_weight.T, adapter_up_weight
    )
    token_query = jnp.arange(context.shape[0], dtype=jnp.int32) // TQ
    of_query = token_query[:, None] == jnp.arange(RERUN_QUERIES, dtype=jnp.int32)[None, :]
    narrow_sums = jnp.sum(
        (inverse_rms * narrow).reshape(RERUN_QUERIES, TQ, -1), axis=1
    )

    returned, hidden_low, hidden_up, inverse_rms, narrow_sums, far_grad = (
        lax.optimization_barrier(
            (returned, hidden_low, hidden_up, inverse_rms, narrow_sums, far_grad)
        )
    )
    far_part = dot(mix_parts, returned)
    query_gradient = (loss_scale * score_scale) * (
        far_part[:query_count] + far_part[query_count:] + near_part
    )

    grad_passages = loss_scale * score_scale * (far_grad + near_grad)

    scaled = final_norm_weight.astype(f32)[None, :] * (query_gradient[:RERUN_QUERIES] / TQ)
    products = dot(hidden_low, scaled.astype(bf16).T)
    mean = jnp.sum(jnp.where(of_query, products, 0.0), axis=1, keepdims=True) / MODEL_WIDTH
    slope = inverse_rms**3 * mean
    scaled_up = dot(scaled, adapter_up_weight.astype(f32).T, precision=lax.Precision.HIGHEST)
    spread_up = jnp.broadcast_to(
        scaled_up[:, None, :], (RERUN_QUERIES, TQ, scaled_up.shape[1])
    ).reshape(context.shape[0], -1)
    grad_narrow = (adapter_scale * (inverse_rms * spread_up - slope * hidden_up)).astype(bf16)
    down_term = lax.dot_general(grad_narrow, context, product_dims, preferred_element_type=f32)
    weighted = (slope * narrow).astype(bf16)
    up_term = adapter_scale * (
        lax.dot_general(
            narrow_sums,
            scaled,
            product_dims,
            precision=lax.Precision.HIGHEST,
            preferred_element_type=f32,
        )
        - lax.dot_general(weighted, hidden_low, product_dims, preferred_element_type=f32)
    )
    terms = jnp.concatenate([down_term, up_term], axis=0) / RERUN_QUERIES
    rank = narrow.shape[1]
    columns = MODEL_WIDTH // device_count
    pieces = jnp.transpose(terms.reshape(2 * rank, device_count, columns), (1, 0, 2))
    sums = jnp.sum(exchange(pieces.reshape(device_count, -1)), axis=0).reshape(2 * rank, columns)
    return (query_gradient, grad_passages, sums[:rank].T, sums[rank:])


def solution(mesh):
    torus = Mesh(mesh.devices.reshape(4, 2, 4, 4), PB_PA)
    in_specs = (
        P(PB_PA, None),
        P(PB_PA, None),
        P(PB_PA, None),
        P(PB_PA),
        P(PB_PA, None),
        P(PB_PA, None),
        P(PB_PA, None),
        P(),
        P(),
        P(),
    )
    out_specs = (P(PB_PA, None), P(PB_PA, None), P(PB_PA, None), P(None, PB_PA))
    return jax.shard_map(local, mesh=torus, in_specs=in_specs, out_specs=out_specs, check_vma=False)
```

```python
import functools
import math

import jax
import jax.numpy as jnp
from jax import lax
from jax.experimental import pallas as pl
from jax.experimental.pallas import tpu as pltpu
from jax.sharding import Mesh
from jax.sharding import PartitionSpec as P

MODEL_WIDTH = 3584
RERUN_QUERIES = 16
TQ = 32
PB_PA = ("pb_0", "pb_1", "pa_0", "pa_1")
CHIPS = ("pb_0", "pa_0", "pa_1")

inverse_temp = 2.0
loss_scale = 32.0
adapter_scale = 2.0
epsilon = 1e-06
absent_mass = 1e30
f32 = jnp.float32
bf16 = jnp.bfloat16
MESH = pl.DeviceIdType.MESH


def dot(a, b, **kw):
    return jnp.dot(a, b, preferred_element_type=f32, **kw)


def two_parts(x):
    high = x.astype(bf16)
    return high, (x - high.astype(f32)).astype(bf16)


def device_of(chip, core, per_plane):
    return (chip // per_plane) * 2 * per_plane + core * per_plane + chip % per_plane


def gathered_weight_input(rows):
    count = lax.axis_size(PB_PA)
    per_plane = lax.axis_size("pa_0") * lax.axis_size("pa_1")
    half = rows.shape[1] // 2
    left, right = rows[:, :half], rows[:, half:]
    odd = lax.axis_index("pa_1") % 2 == 1
    core = lax.axis_index("pb_1")
    same = [(f, device_of(f // 2, f % 2, per_plane)) for f in range(count)]
    other = [(f, device_of(f // 2, 1 - f % 2, per_plane)) for f in range(count)]
    first = lax.ppermute(jnp.where(odd, right, left), PB_PA, same)
    second = lax.ppermute(jnp.where(odd, left, right), PB_PA, other)
    low = jnp.where(core == 0, first, second)
    high = jnp.where(core == 0, second, first)
    return jnp.concatenate([low, high], axis=0)


def exchange(array):
    return lax.all_to_all(array, PB_PA, split_axis=0, concat_axis=0, tiled=True)


def layer_forward_kernel(
    context, half_weight, residual, down, up, hidden, narrow, hidden_up, inverse,
    own, other, own_sem, send_sem, recv_sem, squares,
):
    core = lax.axis_index("pb_1")
    twin = (lax.axis_index("pb_0"), 1 - core, lax.axis_index("pa_0"), lax.axis_index("pa_1"))
    tile = own.shape[2]
    half = half_weight.shape[1]
    tiles = half // tile
    barrier = pltpu.get_barrier_semaphore()
    pl.semaphore_signal(barrier, inc=1, device_id=twin, device_id_type=MESH)
    pl.semaphore_wait(barrier, 1)

    def columns(j):
        return pl.ds(pl.multiple_of(j * tile, tile), tile)

    def sent(j):
        return pltpu.make_async_remote_copy(
            half_weight.at[:, columns(j)], other.at[j], send_sem.at[j], recv_sem.at[j],
            device_id=twin, device_id_type=MESH,
        )

    def fetched(j):
        return pltpu.make_async_copy(
            half_weight.at[:, columns(j)], own.at[lax.rem(j, 2)], own_sem.at[lax.rem(j, 2)]
        )

    fetched(0).start()

    def send(j, carry):
        sent(j).start()
        return carry

    lax.fori_loop(0, tiles, send, 0)
    low = lax.dot_general(
        context[...], down[...], (((1,), (1,)), ((), ())), preferred_element_type=f32
    ).astype(bf16)
    narrow[...] = low.astype(f32)
    squares[...] = jnp.zeros_like(squares)
    hidden_up[...] = jnp.zeros_like(hidden_up)

    def step(weight, start):
        at = pl.ds(pl.multiple_of(start, tile), tile)
        up_tile = up[:, at]
        value = (
            residual[:, at].astype(f32)
            + jnp.dot(context[...], weight, preferred_element_type=f32)
            + adapter_scale * jnp.dot(low, up_tile, preferred_element_type=f32)
        )
        squares[...] += jnp.sum(value * value, axis=1, keepdims=True)
        value = value.astype(bf16)
        hidden[:, at] = value
        hidden_up[...] += lax.dot_general(
            value, up_tile, (((1,), (1,)), ((), ())), preferred_element_type=f32
        )

    def own_step(j, carry):
        fetched(j).wait()

        @pl.when(j + 1 < tiles)
        def _():
            fetched(j + 1).start()

        step(own[lax.rem(j, 2)], core * half + j * tile)
        return carry

    lax.fori_loop(0, tiles, own_step, 0)

    def other_step(j, carry):
        sent(j).wait_recv()
        step(other[j], (1 - core) * half + j * tile)
        return carry

    lax.fori_loop(0, tiles, other_step, 0)
    inverse[...] = lax.rsqrt(squares[...] / MODEL_WIDTH + epsilon)

    def done(j, carry):
        sent(j).wait_send()
        return carry

    lax.fori_loop(0, tiles, done, 0)


def layer_forward(context, half_weight, residual, down, up):
    tokens, width = context.shape
    half = half_weight.shape[1]
    tile = 256
    tiles = half // tile
    rank = up.shape[0]
    vmem = pl.BlockSpec(memory_space=pltpu.VMEM)
    return pl.pallas_call(
        layer_forward_kernel,
        out_shape=(
            jax.ShapeDtypeStruct((tokens, width), bf16),
            jax.ShapeDtypeStruct((tokens, rank), f32),
            jax.ShapeDtypeStruct((tokens, rank), f32),
            jax.ShapeDtypeStruct((tokens, 1), f32),
        ),
        in_specs=[vmem, pl.BlockSpec(memory_space=pl.ANY), vmem, vmem, vmem],
        out_specs=(vmem, vmem, vmem, vmem),
        scratch_shapes=[
            pltpu.VMEM((2, width, tile), bf16),
            pltpu.VMEM((tiles, width, tile), bf16),
            pltpu.SemaphoreType.DMA((2,)),
            pltpu.SemaphoreType.DMA((tiles,)),
            pltpu.SemaphoreType.DMA((tiles,)),
            pltpu.VMEM((tokens, 1), f32),
        ],
        compiler_params=pltpu.CompilerParams(
            collective_id=1, has_side_effects=True, vmem_limit_bytes=44 * 1024 * 1024
        ),
        cost_estimate=pl.CostEstimate(flops=1000, bytes_accessed=1000, transcendentals=0),
        name="layer_forward",
    )(context, half_weight, residual, down, up)


def far_kernel(score_scale, rows, passages, scores, mean, mass):
    value = score_scale * lax.dot_general(
        rows[...], passages[...], (((1,), (1,)), ((), ())), preferred_element_type=f32
    )
    scores[...] = value
    peak = jnp.max(value, axis=1, keepdims=True)
    weights = jnp.exp(value - peak)
    total = jnp.sum(weights, axis=1, keepdims=True)
    mass[...] = jnp.broadcast_to(peak + jnp.log(total), mass.shape)
    inverse = 1.0 / total
    weights = weights.astype(bf16)
    tile = 512
    for start in range(0, mean.shape[1], tile):
        part = jnp.dot(
            weights, passages[:, start : start + tile], preferred_element_type=f32
        )
        mean[:, start : start + tile] = (part * inverse).astype(bf16)


def far_forward(rows, passages, score_scale):
    count, width = rows.shape
    passage_count = passages.shape[0]
    block = 256
    return pl.pallas_call(
        functools.partial(far_kernel, score_scale),
        out_shape=(
            jax.ShapeDtypeStruct((count, passage_count), f32),
            jax.ShapeDtypeStruct((count, width), bf16),
            jax.ShapeDtypeStruct((count, 128), f32),
        ),
        grid=(count // block,),
        in_specs=[
            pl.BlockSpec((block, width), lambda i: (i, 0)),
            pl.BlockSpec((passage_count, width), lambda i: (0, 0), pipeline_mode=pl.Buffered(1)),
        ],
        out_specs=(
            pl.BlockSpec((block, passage_count), lambda i: (i, 0)),
            pl.BlockSpec((block, width), lambda i: (i, 0)),
            pl.BlockSpec((block, 128), lambda i: (i, 0)),
        ),
        compiler_params=pltpu.CompilerParams(vmem_limit_bytes=32 * 1024 * 1024),
        name="far_forward",
    )(rows, passages)


def torus_place():
    return tuple(lax.axis_index(axis) for axis in PB_PA)


def flat_of(place):
    return ((place[0] * 2 + place[1]) * 4 + place[2]) * 4 + place[3]


def torus_peer(place, j):
    return (
        lax.rem(place[0] + lax.rem(j, 4), 4),
        lax.rem(place[1] + j // 64, 2),
        lax.rem(place[2] + lax.rem(j // 4, 4), 4),
        lax.rem(place[3] + lax.rem(j // 16, 4), 4),
    )


def small_exchange_kernel(
    mass, near_mass, key_column, key_row, mix, log_total, log_arrived,
    mass_in, log_out, mass_send, mass_recv, log_send, log_recv,
):
    place = torus_place()
    own = flat_of(place)
    peers = mass.shape[0]
    slot_rows = mass.shape[1]
    all_rows = peers * slot_rows
    hard_count = key_row.shape[0]
    query_count = near_mass.shape[0]
    barrier = pltpu.get_barrier_semaphore()

    def greet(j, carry):
        pl.semaphore_signal(
            barrier, inc=1, device_id=torus_peer(place, j), device_id_type=MESH
        )
        return carry

    lax.fori_loop(1, peers, greet, 0)
    pl.semaphore_wait(barrier, peers - 1)

    def sends(source, target, send_sem, recv_sem):
        def body(j, carry):
            peer = torus_peer(place, j)
            pltpu.make_async_remote_copy(
                source.at[flat_of(peer)], target.at[own], send_sem, recv_sem,
                device_id=peer, device_id_type=MESH,
            ).start()
            return carry

        lax.fori_loop(1, peers, body, 0)

    def every(source, target, send_sem, recv_sem):
        rest = pl.ds(0, peers - 1)
        return pltpu.make_async_remote_copy(
            source.at[rest], target.at[rest], send_sem, recv_sem,
            device_id=torus_peer(place, 1), device_id_type=MESH,
        )

    sends(mass, mass_in, mass_send, mass_recv)
    mass_in[own] = mass[own]
    row_ids = lax.broadcasted_iota(jnp.int32, (query_count, all_rows), 1)
    hits = [
        key_column[t * query_count : (t + 1) * query_count, :] == row_ids
        for t in range(hard_count)
    ]
    column_ids = lax.broadcasted_iota(jnp.int32, (all_rows, query_count), 0)
    picks = jnp.zeros((all_rows, query_count), f32)
    for t in range(hard_count):
        picks = jnp.where(column_ids == key_row[t : t + 1, :], 1.0, picks)
    filled = jnp.sum(picks, axis=1, keepdims=True) > 0.0
    every(mass, mass_in, mass_send, mass_recv).wait_recv()
    came = mass_in[...].reshape(all_rows, mass.shape[2])
    masses = [jnp.broadcast_to(near_mass[...], (query_count, came.shape[1]))]
    for hit in hits:
        masses.append(
            jnp.dot(
                jnp.where(hit, 1.0, 0.0), came,
                precision=lax.Precision.HIGHEST, preferred_element_type=f32,
            )
        )
    peak = masses[0]
    for value in masses[1:]:
        peak = jnp.maximum(peak, value)
    total = jnp.exp(masses[0] - peak)
    for value in masses[1:]:
        total = total + jnp.exp(value - peak)
    log_value = peak + jnp.log(total)
    log_total[...] = log_value
    outgoing = jnp.dot(
        picks, log_value, precision=lax.Precision.HIGHEST, preferred_element_type=f32
    )
    outgoing = jnp.where(filled, outgoing, absent_mass)
    log_out[...] = outgoing.reshape(log_out.shape)
    sends(log_out, log_arrived, log_send, log_recv)
    log_arrived[own] = log_out[own]
    shares = jnp.zeros((query_count, all_rows), f32)
    for t in range(hard_count):
        shares = jnp.where(hits[t], jnp.exp(masses[1 + t] - log_value)[:, :1], shares)
    high = shares.astype(bf16)
    mix[:query_count, :] = high
    mix[query_count:, :] = (shares - high.astype(f32)).astype(bf16)
    every(mass, mass_in, mass_send, mass_recv).wait_send()
    last = every(log_out, log_arrived, log_send, log_recv)
    last.wait_send()
    last.wait_recv()


def small_exchange(mass, near_mass, key):
    peers, slot_rows, lanes = mass.shape
    hard_count, query_count = key.shape
    vmem = pl.BlockSpec(memory_space=pltpu.VMEM)
    return pl.pallas_call(
        small_exchange_kernel,
        out_shape=(
            jax.ShapeDtypeStruct((2 * query_count, peers * slot_rows), bf16),
            jax.ShapeDtypeStruct((query_count, lanes), f32),
            jax.ShapeDtypeStruct(mass.shape, f32),
        ),
        in_specs=[vmem] * 4,
        out_specs=(vmem, vmem, vmem),
        scratch_shapes=[
            pltpu.VMEM(mass.shape, f32),
            pltpu.VMEM(mass.shape, f32),
            pltpu.SemaphoreType.DMA(()),
            pltpu.SemaphoreType.DMA(()),
            pltpu.SemaphoreType.DMA(()),
            pltpu.SemaphoreType.DMA(()),
        ],
        compiler_params=pltpu.CompilerParams(
            collective_id=2, has_side_effects=True, vmem_limit_bytes=24 * 1024 * 1024
        ),
        cost_estimate=pl.CostEstimate(flops=1000, bytes_accessed=1000, transcendentals=0),
        name="small_exchange",
    )(mass, near_mass[:, None], key.reshape(-1)[:, None], key)


def local(
    queries,
    passages,
    hard_block_offsets,
    positive,
    context,
    residual,
    output_weight,
    adapter_down_weight,
    adapter_up_weight,
    final_norm_weight,
):
    device_count = lax.axis_size(PB_PA)
    block_count, hard_count = hard_block_offsets.shape
    query_count = queries.shape[0]
    block_rows = query_count // block_count
    capacity = 2 * block_count * hard_count // device_count
    slot_rows = capacity * block_rows
    all_rows = device_count * slot_rows
    passage_count = passages.shape[0]
    score_scale = inverse_temp / math.sqrt(MODEL_WIDTH)

    weight_rows = gathered_weight_input(output_weight)

    source = lax.axis_index(PB_PA)
    target = ((source + 1 + hard_block_offsets) % device_count).reshape(-1)
    order = jnp.arange(target.shape[0], dtype=jnp.int32)
    earlier = (target[:, None] == target[None, :]) & (order[:, None] > order[None, :])
    slot = target * capacity + jnp.sum(earlier.astype(jnp.int32), axis=1)
    slot_of = slot.reshape(block_count, hard_count).T
    key = jnp.repeat(slot_of, block_rows, axis=1) * block_rows + (
        jnp.arange(query_count, dtype=jnp.int32) % block_rows
    )
    row_ids = jnp.arange(all_rows, dtype=jnp.int32)
    picks = row_ids[:, None] == key[0][None, :]
    for t in range(1, hard_count):
        picks = picks | (row_ids[:, None] == key[t][None, :])
    outgoing = jnp.dot(picks.astype(bf16), queries, preferred_element_type=bf16)
    arrived = exchange(outgoing.reshape(device_count, slot_rows, MODEL_WIDTH))
    arrived = arrived.reshape(-1, MODEL_WIDTH)

    half_weight = lax.all_gather(weight_rows, CHIPS, axis=0, tiled=True)
    near_scores = dot(queries, passages.T) * score_scale
    near_peak = jnp.max(near_scores, axis=1)
    near_exp = jnp.exp(near_scores - near_peak[:, None])
    near_sum = jnp.sum(near_exp, axis=1)
    near_mass = near_peak + jnp.log(near_sum)
    positive_hot = positive[:, None] == jnp.arange(passage_count, dtype=jnp.int32)[None, :]
    stacked = dot(
        jnp.concatenate([near_exp.astype(bf16), positive_hot.astype(bf16)], axis=0), passages
    )

    far_scores, far_mean, far_mass = far_forward(arrived, passages, score_scale)
    returned = exchange(far_mean.reshape(device_count, slot_rows, MODEL_WIDTH))
    returned = returned.reshape(-1, MODEL_WIDTH)
    mix_parts, log_total, log_arrived = small_exchange(
        far_mass.reshape(device_count, slot_rows, -1), near_mass, key
    )
    log_total = log_total[:, 0]
    log_arrived = log_arrived.reshape(all_rows, -1)[:, :1]
    near_share = jnp.exp(near_mass - log_total)
    near_part = (near_share / near_sum)[:, None] * stacked[:query_count] - stacked[query_count:]

    product_dims = (((0,), (0,)), ((), ()))
    far_weight = jnp.exp(far_scores - log_arrived).astype(bf16)
    near_weight = (
        jnp.exp(near_scores - log_total[:, None]) - positive_hot.astype(f32)
    ).astype(bf16)
    far_grad = lax.dot_general(far_weight, arrived, product_dims, preferred_element_type=f32)
    near_grad = lax.dot_general(near_weight, queries, product_dims, preferred_element_type=f32)

    hidden_low, narrow, hidden_up, inverse_rms = layer_forward(
        context, half_weight, residual, adapter_down_weight.T, adapter_up_weight
    )
    token_query = jnp.arange(context.shape[0], dtype=jnp.int32) // TQ
    of_query = token_query[:, None] == jnp.arange(RERUN_QUERIES, dtype=jnp.int32)[None, :]
    narrow_sums = jnp.sum(
        (inverse_rms * narrow).reshape(RERUN_QUERIES, TQ, -1), axis=1
    )

    returned, hidden_low, hidden_up, inverse_rms, narrow_sums, far_grad = (
        lax.optimization_barrier(
            (returned, hidden_low, hidden_up, inverse_rms, narrow_sums, far_grad)
        )
    )
    far_part = dot(mix_parts, returned)
    query_gradient = (loss_scale * score_scale) * (
        far_part[:query_count] + far_part[query_count:] + near_part
    )

    grad_passages = loss_scale * score_scale * (far_grad + near_grad)

    scaled = final_norm_weight.astype(f32)[None, :] * (query_gradient[:RERUN_QUERIES] / TQ)
    products = dot(hidden_low, scaled.astype(bf16).T)
    mean = jnp.sum(jnp.where(of_query, products, 0.0), axis=1, keepdims=True) / MODEL_WIDTH
    slope = inverse_rms**3 * mean
    scaled_up = dot(scaled, adapter_up_weight.astype(f32).T, precision=lax.Precision.HIGHEST)
    spread_up = jnp.broadcast_to(
        scaled_up[:, None, :], (RERUN_QUERIES, TQ, scaled_up.shape[1])
    ).reshape(context.shape[0], -1)
    grad_narrow = (adapter_scale * (inverse_rms * spread_up - slope * hidden_up)).astype(bf16)
    down_term = lax.dot_general(grad_narrow, context, product_dims, preferred_element_type=f32)
    weighted = (slope * narrow).astype(bf16)
    up_term = adapter_scale * (
        lax.dot_general(
            narrow_sums,
            scaled,
            product_dims,
            precision=lax.Precision.HIGHEST,
            preferred_element_type=f32,
        )
        - lax.dot_general(weighted, hidden_low, product_dims, preferred_element_type=f32)
    )
    terms = jnp.concatenate([down_term, up_term], axis=0) / RERUN_QUERIES
    rank = narrow.shape[1]
    columns = MODEL_WIDTH // device_count
    pieces = jnp.transpose(terms.reshape(2 * rank, device_count, columns), (1, 0, 2))
    sums = jnp.sum(exchange(pieces.reshape(device_count, -1)), axis=0).reshape(2 * rank, columns)
    return (query_gradient, grad_passages, sums[:rank].T, sums[rank:])


def solution(mesh):
    torus = Mesh(mesh.devices.reshape(4, 2, 4, 4), PB_PA)
    in_specs = (
        P(PB_PA, None),
        P(PB_PA, None),
        P(PB_PA, None),
        P(PB_PA),
        P(PB_PA, None),
        P(PB_PA, None),
        P(PB_PA, None),
        P(),
        P(),
        P(),
    )
    out_specs = (P(PB_PA, None), P(PB_PA, None), P(PB_PA, None), P(None, PB_PA))
    return jax.shard_map(local, mesh=torus, in_specs=in_specs, out_specs=out_specs, check_vma=False)
```

```python
import functools
import math

import jax
import jax.numpy as jnp
from jax import lax
from jax.experimental import pallas as pl
from jax.experimental.pallas import tpu as pltpu
from jax.sharding import Mesh
from jax.sharding import PartitionSpec as P

MODEL_WIDTH = 3584
RERUN_QUERIES = 16
TQ = 32
PB_PA = ("pb_0", "pb_1", "pa_0", "pa_1")
CHIPS = ("pb_0", "pa_0", "pa_1")

inverse_temp = 2.0
loss_scale = 32.0
adapter_scale = 2.0
epsilon = 1e-06
absent_mass = 1e30
f32 = jnp.float32
bf16 = jnp.bfloat16
MESH = pl.DeviceIdType.MESH


def dot(a, b, **kw):
    return jnp.dot(a, b, preferred_element_type=f32, **kw)


def two_parts(x):
    high = x.astype(bf16)
    return high, (x - high.astype(f32)).astype(bf16)


def device_of(chip, core, per_plane):
    return (chip // per_plane) * 2 * per_plane + core * per_plane + chip % per_plane


def gathered_weight_input(rows):
    count = lax.axis_size(PB_PA)
    per_plane = lax.axis_size("pa_0") * lax.axis_size("pa_1")
    half = rows.shape[1] // 2
    left, right = rows[:, :half], rows[:, half:]
    odd = lax.axis_index("pa_1") % 2 == 1
    core = lax.axis_index("pb_1")
    same = [(f, device_of(f // 2, f % 2, per_plane)) for f in range(count)]
    other = [(f, device_of(f // 2, 1 - f % 2, per_plane)) for f in range(count)]
    first = lax.ppermute(jnp.where(odd, right, left), PB_PA, same)
    second = lax.ppermute(jnp.where(odd, left, right), PB_PA, other)
    low = jnp.where(core == 0, first, second)
    high = jnp.where(core == 0, second, first)
    return jnp.concatenate([low, high], axis=0)


def exchange(array):
    return lax.all_to_all(array, PB_PA, split_axis=0, concat_axis=0, tiled=True)


def layer_forward_kernel(
    context, half_weight, residual, down, up, hidden, narrow, hidden_up, inverse,
    own, other, own_sem, send_sem, recv_sem, squares,
):
    core = lax.axis_index("pb_1")
    twin = (lax.axis_index("pb_0"), 1 - core, lax.axis_index("pa_0"), lax.axis_index("pa_1"))
    tile = own.shape[2]
    half = half_weight.shape[1]
    tiles = half // tile
    barrier = pltpu.get_barrier_semaphore()
    pl.semaphore_signal(barrier, inc=1, device_id=twin, device_id_type=MESH)
    pl.semaphore_wait(barrier, 1)

    def columns(j):
        return pl.ds(pl.multiple_of(j * tile, tile), tile)

    def sent(j):
        return pltpu.make_async_remote_copy(
            half_weight.at[:, columns(j)], other.at[j], send_sem.at[j], recv_sem.at[j],
            device_id=twin, device_id_type=MESH,
        )

    def fetched(j):
        return pltpu.make_async_copy(
            half_weight.at[:, columns(j)], own.at[lax.rem(j, 2)], own_sem.at[lax.rem(j, 2)]
        )

    fetched(0).start()

    def send(j, carry):
        sent(j).start()
        return carry

    lax.fori_loop(0, tiles, send, 0)
    low = lax.dot_general(
        context[...], down[...], (((1,), (1,)), ((), ())), preferred_element_type=f32
    ).astype(bf16)
    narrow[...] = low.astype(f32)
    squares[...] = jnp.zeros_like(squares)
    hidden_up[...] = jnp.zeros_like(hidden_up)

    def step(weight, start):
        at = pl.ds(pl.multiple_of(start, tile), tile)
        up_tile = up[:, at]
        value = (
            residual[:, at].astype(f32)
            + jnp.dot(context[...], weight, preferred_element_type=f32)
            + adapter_scale * jnp.dot(low, up_tile, preferred_element_type=f32)
        )
        squares[...] += jnp.sum(value * value, axis=1, keepdims=True)
        value = value.astype(bf16)
        hidden[:, at] = value
        hidden_up[...] += lax.dot_general(
            value, up_tile, (((1,), (1,)), ((), ())), preferred_element_type=f32
        )

    def own_step(j, carry):
        fetched(j).wait()

        @pl.when(j + 1 < tiles)
        def _():
            fetched(j + 1).start()

        step(own[lax.rem(j, 2)], core * half + j * tile)
        return carry

    lax.fori_loop(0, tiles, own_step, 0)

    def other_step(j, carry):
        sent(j).wait_recv()
        step(other[j], (1 - core) * half + j * tile)
        return carry

    lax.fori_loop(0, tiles, other_step, 0)
    inverse[...] = lax.rsqrt(squares[...] / MODEL_WIDTH + epsilon)

    def done(j, carry):
        sent(j).wait_send()
        return carry

    lax.fori_loop(0, tiles, done, 0)


def layer_forward(context, half_weight, residual, down, up):
    tokens, width = context.shape
    half = half_weight.shape[1]
    tile = 256
    tiles = half // tile
    rank = up.shape[0]
    vmem = pl.BlockSpec(memory_space=pltpu.VMEM)
    return pl.pallas_call(
        layer_forward_kernel,
        out_shape=(
            jax.ShapeDtypeStruct((tokens, width), bf16),
            jax.ShapeDtypeStruct((tokens, rank), f32),
            jax.ShapeDtypeStruct((tokens, rank), f32),
            jax.ShapeDtypeStruct((tokens, 1), f32),
        ),
        in_specs=[vmem, pl.BlockSpec(memory_space=pl.ANY), vmem, vmem, vmem],
        out_specs=(vmem, vmem, vmem, vmem),
        scratch_shapes=[
            pltpu.VMEM((2, width, tile), bf16),
            pltpu.VMEM((tiles, width, tile), bf16),
            pltpu.SemaphoreType.DMA((2,)),
            pltpu.SemaphoreType.DMA((tiles,)),
            pltpu.SemaphoreType.DMA((tiles,)),
            pltpu.VMEM((tokens, 1), f32),
        ],
        compiler_params=pltpu.CompilerParams(
            collective_id=1, has_side_effects=True, vmem_limit_bytes=44 * 1024 * 1024
        ),
        cost_estimate=pl.CostEstimate(flops=1000, bytes_accessed=1000, transcendentals=0),
        name="layer_forward",
    )(context, half_weight, residual, down, up)


def torus_place():
    return tuple(lax.axis_index(axis) for axis in PB_PA)


def flat_of(place):
    return ((place[0] * 2 + place[1]) * 4 + place[2]) * 4 + place[3]


def torus_peer(place, j):
    return (
        lax.rem(place[0] + lax.rem(j, 4), 4),
        lax.rem(place[1] + j // 64, 2),
        lax.rem(place[2] + lax.rem(j // 4, 4), 4),
        lax.rem(place[3] + lax.rem(j // 16, 4), 4),
    )


def far_kernel(
    score_scale, arrived, passages, near_mass, key_column, key_row, mean, scores, mix, log_total,
    log_arrived, rows, weights, inverse, means, mass, mass_in, log_out, row_sem, mean_sem,
    mass_send, mass_recv, log_send, log_recv,
):
    place = torus_place()
    own = flat_of(place)
    peers, slot_rows, lanes = mass.shape
    all_rows = peers * slot_rows
    hard_count = key_row.shape[0]
    query_count = near_mass.shape[0]
    width = passages.shape[1]
    chunks = row_sem.shape[0]
    block = all_rows // chunks
    block_peers = peers // chunks
    barrier = pltpu.get_barrier_semaphore()

    def greet(j, carry):
        pl.semaphore_signal(
            barrier, inc=1, device_id=torus_peer(place, j), device_id_type=MESH
        )
        return carry

    def part(c):
        return pl.ds(pl.multiple_of(c * block, block), block)

    def came_in(c):
        return pltpu.make_async_copy(arrived.at[part(c)], rows.at[part(c)], row_sem.at[c])

    def went_out(c):
        return pltpu.make_async_copy(means.at[part(c)], mean.at[part(c)], mean_sem.at[c])

    for c in range(chunks):
        came_in(c).start()
    lax.fori_loop(1, peers, greet, 0)

    def score(c, carry):
        came_in(c).wait()
        value = score_scale * lax.dot_general(
            rows[part(c), :], passages[...], (((1,), (1,)), ((), ())),
            preferred_element_type=f32,
        )
        scores[part(c), :] = value
        peak = jnp.max(value, axis=1, keepdims=True)
        weight = jnp.exp(value - peak)
        total = jnp.sum(weight, axis=1, keepdims=True)
        weights[part(c), :] = weight.astype(bf16)
        inverse[part(c), :] = 1.0 / total
        spread = jnp.broadcast_to(peak + jnp.log(total), (block, lanes))
        mass[pl.ds(c * block_peers, block_peers)] = spread.reshape(block_peers, slot_rows, lanes)
        return carry

    lax.fori_loop(0, chunks, score, 0)
    pl.semaphore_wait(barrier, peers - 1)

    def sends(source, target, send_sem, recv_sem):
        def body(j, carry):
            peer = torus_peer(place, j)
            pltpu.make_async_remote_copy(
                source.at[flat_of(peer)], target.at[own], send_sem, recv_sem,
                device_id=peer, device_id_type=MESH,
            ).start()
            return carry

        lax.fori_loop(1, peers, body, 0)

    def every(source, target, send_sem, recv_sem):
        rest = pl.ds(0, peers - 1)
        return pltpu.make_async_remote_copy(
            source.at[rest], target.at[rest], send_sem, recv_sem,
            device_id=torus_peer(place, 1), device_id_type=MESH,
        )

    sends(mass, mass_in, mass_send, mass_recv)
    mass_in[own] = mass[own]

    def average(c, carry):
        weight = weights[part(c), :]
        scale = inverse[part(c), :]
        tile = 512
        for start in range(0, width, tile):
            value = jnp.dot(
                weight, passages[:, start : start + tile], preferred_element_type=f32
            )
            means[part(c), start : start + tile] = (value * scale).astype(bf16)
        went_out(c).start()
        return carry

    lax.fori_loop(0, chunks, average, 0)
    row_ids = lax.broadcasted_iota(jnp.int32, (query_count, all_rows), 1)
    hits = [
        key_column[t * query_count : (t + 1) * query_count, :] == row_ids
        for t in range(hard_count)
    ]
    column_ids = lax.broadcasted_iota(jnp.int32, (all_rows, query_count), 0)
    picks = jnp.zeros((all_rows, query_count), f32)
    for t in range(hard_count):
        picks = jnp.where(column_ids == key_row[t : t + 1, :], 1.0, picks)
    filled = jnp.sum(picks, axis=1, keepdims=True) > 0.0
    every(mass, mass_in, mass_send, mass_recv).wait_recv()
    came = mass_in[...].reshape(all_rows, lanes)
    masses = [jnp.broadcast_to(near_mass[...], (query_count, lanes))]
    for hit in hits:
        masses.append(
            jnp.dot(
                jnp.where(hit, 1.0, 0.0), came,
                precision=lax.Precision.HIGHEST, preferred_element_type=f32,
            )
        )
    peak = masses[0]
    for value in masses[1:]:
        peak = jnp.maximum(peak, value)
    total = jnp.exp(masses[0] - peak)
    for value in masses[1:]:
        total = total + jnp.exp(value - peak)
    log_value = peak + jnp.log(total)
    log_total[...] = log_value
    outgoing = jnp.dot(
        picks, log_value, precision=lax.Precision.HIGHEST, preferred_element_type=f32
    )
    outgoing = jnp.where(filled, outgoing, absent_mass)
    log_out[...] = outgoing.reshape(log_out.shape)
    sends(log_out, log_arrived, log_send, log_recv)
    log_arrived[own] = log_out[own]
    shares = jnp.zeros((query_count, all_rows), f32)
    for t in range(hard_count):
        shares = jnp.where(hits[t], jnp.exp(masses[1 + t] - log_value)[:, :1], shares)
    high = shares.astype(bf16)
    mix[:query_count, :] = high
    mix[query_count:, :] = (shares - high.astype(f32)).astype(bf16)
    every(mass, mass_in, mass_send, mass_recv).wait_send()
    for c in range(chunks):
        went_out(c).wait()
    last = every(log_out, log_arrived, log_send, log_recv)
    last.wait_send()
    last.wait_recv()


def far_forward(arrived, passages, near_mass, key, peers, score_scale):
    all_rows, width = arrived.shape
    passage_count = passages.shape[0]
    hard_count, query_count = key.shape
    lanes, chunks = 128, 4
    small = (peers, all_rows // peers, lanes)
    vmem = pl.BlockSpec(memory_space=pltpu.VMEM)
    hbm = pl.BlockSpec(memory_space=pl.ANY)
    dma = pltpu.SemaphoreType.DMA
    return pl.pallas_call(
        functools.partial(far_kernel, score_scale),
        out_shape=(
            jax.ShapeDtypeStruct((all_rows, width), bf16),
            jax.ShapeDtypeStruct((all_rows, passage_count), f32),
            jax.ShapeDtypeStruct((2 * query_count, all_rows), bf16),
            jax.ShapeDtypeStruct((query_count, lanes), f32),
            jax.ShapeDtypeStruct(small, f32),
        ),
        in_specs=[hbm, vmem, vmem, vmem, vmem],
        out_specs=(hbm, vmem, vmem, vmem, vmem),
        scratch_shapes=[
            pltpu.VMEM((all_rows, width), bf16),
            pltpu.VMEM((all_rows, passage_count), bf16),
            pltpu.VMEM((all_rows, 1), f32),
            pltpu.VMEM((all_rows, width), bf16),
            pltpu.VMEM(small, f32),
            pltpu.VMEM(small, f32),
            pltpu.VMEM(small, f32),
            dma((chunks,)),
            dma((chunks,)),
            dma(()),
            dma(()),
            dma(()),
            dma(()),
        ],
        compiler_params=pltpu.CompilerParams(
            collective_id=2, has_side_effects=True, vmem_limit_bytes=44 * 1024 * 1024
        ),
        name="far_forward",
    )(arrived, passages, near_mass[:, None], key.reshape(-1)[:, None], key)


def local(
    queries,
    passages,
    hard_block_offsets,
    positive,
    context,
    residual,
    output_weight,
    adapter_down_weight,
    adapter_up_weight,
    final_norm_weight,
):
    device_count = lax.axis_size(PB_PA)
    block_count, hard_count = hard_block_offsets.shape
    query_count = queries.shape[0]
    block_rows = query_count // block_count
    capacity = 2 * block_count * hard_count // device_count
    slot_rows = capacity * block_rows
    all_rows = device_count * slot_rows
    passage_count = passages.shape[0]
    score_scale = inverse_temp / math.sqrt(MODEL_WIDTH)

    weight_rows = gathered_weight_input(output_weight)

    source = lax.axis_index(PB_PA)
    target = ((source + 1 + hard_block_offsets) % device_count).reshape(-1)
    order = jnp.arange(target.shape[0], dtype=jnp.int32)
    earlier = (target[:, None] == target[None, :]) & (order[:, None] > order[None, :])
    slot = target * capacity + jnp.sum(earlier.astype(jnp.int32), axis=1)
    slot_of = slot.reshape(block_count, hard_count).T
    key = jnp.repeat(slot_of, block_rows, axis=1) * block_rows + (
        jnp.arange(query_count, dtype=jnp.int32) % block_rows
    )
    row_ids = jnp.arange(all_rows, dtype=jnp.int32)
    picks = row_ids[:, None] == key[0][None, :]
    for t in range(1, hard_count):
        picks = picks | (row_ids[:, None] == key[t][None, :])
    outgoing = jnp.dot(picks.astype(bf16), queries, preferred_element_type=bf16)
    arrived = exchange(outgoing.reshape(device_count, slot_rows, MODEL_WIDTH))
    arrived = arrived.reshape(-1, MODEL_WIDTH)

    half_weight = lax.all_gather(weight_rows, CHIPS, axis=0, tiled=True)
    near_scores = dot(queries, passages.T) * score_scale
    near_peak = jnp.max(near_scores, axis=1)
    near_exp = jnp.exp(near_scores - near_peak[:, None])
    near_sum = jnp.sum(near_exp, axis=1)
    near_mass = near_peak + jnp.log(near_sum)
    positive_hot = positive[:, None] == jnp.arange(passage_count, dtype=jnp.int32)[None, :]
    stacked = dot(
        jnp.concatenate([near_exp.astype(bf16), positive_hot.astype(bf16)], axis=0), passages
    )

    far_mean, far_scores, mix_parts, log_total, log_arrived = far_forward(
        arrived, passages, near_mass, key, device_count, score_scale
    )
    returned = exchange(far_mean.reshape(device_count, slot_rows, MODEL_WIDTH))
    returned = returned.reshape(-1, MODEL_WIDTH)
    log_total = log_total[:, 0]
    log_arrived = log_arrived.reshape(all_rows, -1)[:, :1]
    near_share = jnp.exp(near_mass - log_total)
    near_part = (near_share / near_sum)[:, None] * stacked[:query_count] - stacked[query_count:]

    product_dims = (((0,), (0,)), ((), ()))
    far_weight = jnp.exp(far_scores - log_arrived).astype(bf16)
    near_weight = (
        jnp.exp(near_scores - log_total[:, None]) - positive_hot.astype(f32)
    ).astype(bf16)
    far_grad = lax.dot_general(far_weight, arrived, product_dims, preferred_element_type=f32)
    near_grad = lax.dot_general(near_weight, queries, product_dims, preferred_element_type=f32)

    hidden_low, narrow, hidden_up, inverse_rms = layer_forward(
        context, half_weight, residual, adapter_down_weight.T, adapter_up_weight
    )
    token_query = jnp.arange(context.shape[0], dtype=jnp.int32) // TQ
    of_query = token_query[:, None] == jnp.arange(RERUN_QUERIES, dtype=jnp.int32)[None, :]
    narrow_sums = jnp.sum(
        (inverse_rms * narrow).reshape(RERUN_QUERIES, TQ, -1), axis=1
    )

    returned, hidden_low, hidden_up, inverse_rms, narrow_sums, far_grad = (
        lax.optimization_barrier(
            (returned, hidden_low, hidden_up, inverse_rms, narrow_sums, far_grad)
        )
    )
    far_part = dot(mix_parts, returned)
    query_gradient = (loss_scale * score_scale) * (
        far_part[:query_count] + far_part[query_count:] + near_part
    )

    grad_passages = loss_scale * score_scale * (far_grad + near_grad)

    scaled = final_norm_weight.astype(f32)[None, :] * (query_gradient[:RERUN_QUERIES] / TQ)
    products = dot(hidden_low, scaled.astype(bf16).T)
    mean = jnp.sum(jnp.where(of_query, products, 0.0), axis=1, keepdims=True) / MODEL_WIDTH
    slope = inverse_rms**3 * mean
    scaled_up = dot(scaled, adapter_up_weight.astype(f32).T, precision=lax.Precision.HIGHEST)
    spread_up = jnp.broadcast_to(
        scaled_up[:, None, :], (RERUN_QUERIES, TQ, scaled_up.shape[1])
    ).reshape(context.shape[0], -1)
    grad_narrow = (adapter_scale * (inverse_rms * spread_up - slope * hidden_up)).astype(bf16)
    down_term = lax.dot_general(grad_narrow, context, product_dims, preferred_element_type=f32)
    weighted = (slope * narrow).astype(bf16)
    up_term = adapter_scale * (
        lax.dot_general(
            narrow_sums,
            scaled,
            product_dims,
            precision=lax.Precision.HIGHEST,
            preferred_element_type=f32,
        )
        - lax.dot_general(weighted, hidden_low, product_dims, preferred_element_type=f32)
    )
    terms = jnp.concatenate([down_term, up_term], axis=0) / RERUN_QUERIES
    rank = narrow.shape[1]
    columns = MODEL_WIDTH // device_count
    pieces = jnp.transpose(terms.reshape(2 * rank, device_count, columns), (1, 0, 2))
    sums = jnp.sum(exchange(pieces.reshape(device_count, -1)), axis=0).reshape(2 * rank, columns)
    return (query_gradient, grad_passages, sums[:rank].T, sums[rank:])


def solution(mesh):
    torus = Mesh(mesh.devices.reshape(4, 2, 4, 4), PB_PA)
    in_specs = (
        P(PB_PA, None),
        P(PB_PA, None),
        P(PB_PA, None),
        P(PB_PA),
        P(PB_PA, None),
        P(PB_PA, None),
        P(PB_PA, None),
        P(),
        P(),
        P(),
    )
    out_specs = (P(PB_PA, None), P(PB_PA, None), P(PB_PA, None), P(None, PB_PA))
    return jax.shard_map(local, mesh=torus, in_specs=in_specs, out_specs=out_specs, check_vma=False)
```

```python
import functools
import math

import jax
import jax.numpy as jnp
from jax import lax
from jax.experimental import pallas as pl
from jax.experimental.pallas import tpu as pltpu
from jax.sharding import Mesh
from jax.sharding import PartitionSpec as P

MODEL_WIDTH = 3584
RERUN_QUERIES = 16
TQ = 32
PB_PA = ("pb_0", "pb_1", "pa_0", "pa_1")
CHIPS = ("pb_0", "pa_0", "pa_1")

inverse_temp = 2.0
loss_scale = 32.0
adapter_scale = 2.0
epsilon = 1e-06
absent_mass = 1e30
f32 = jnp.float32
bf16 = jnp.bfloat16
MESH = pl.DeviceIdType.MESH


def dot(a, b, **kw):
    return jnp.dot(a, b, preferred_element_type=f32, **kw)


def two_parts(x):
    high = x.astype(bf16)
    return high, (x - high.astype(f32)).astype(bf16)


def device_of(chip, core, per_plane):
    return (chip // per_plane) * 2 * per_plane + core * per_plane + chip % per_plane


def gathered_weight_input(rows):
    count = lax.axis_size(PB_PA)
    per_plane = lax.axis_size("pa_0") * lax.axis_size("pa_1")
    half = rows.shape[1] // 2
    left, right = rows[:, :half], rows[:, half:]
    odd = lax.axis_index("pa_1") % 2 == 1
    core = lax.axis_index("pb_1")
    same = [(f, device_of(f // 2, f % 2, per_plane)) for f in range(count)]
    other = [(f, device_of(f // 2, 1 - f % 2, per_plane)) for f in range(count)]
    first = lax.ppermute(jnp.where(odd, right, left), PB_PA, same)
    second = lax.ppermute(jnp.where(odd, left, right), PB_PA, other)
    low = jnp.where(core == 0, first, second)
    high = jnp.where(core == 0, second, first)
    return jnp.concatenate([low, high], axis=0)


def exchange(array):
    return lax.all_to_all(array, PB_PA, split_axis=0, concat_axis=0, tiled=True)


def layer_forward_kernel(
    context, half_weight, residual, down, up, hidden, narrow, hidden_up, inverse,
    own, other, own_sem, send_sem, recv_sem, squares,
):
    core = lax.axis_index("pb_1")
    twin = (lax.axis_index("pb_0"), 1 - core, lax.axis_index("pa_0"), lax.axis_index("pa_1"))
    tile = own.shape[2]
    half = half_weight.shape[1]
    tiles = half // tile
    barrier = pltpu.get_barrier_semaphore()
    pl.semaphore_signal(barrier, inc=1, device_id=twin, device_id_type=MESH)
    pl.semaphore_wait(barrier, 1)

    def columns(j):
        return pl.ds(pl.multiple_of(j * tile, tile), tile)

    def sent(j):
        return pltpu.make_async_remote_copy(
            half_weight.at[:, columns(j)], other.at[j], send_sem.at[j], recv_sem.at[j],
            device_id=twin, device_id_type=MESH,
        )

    def fetched(j):
        return pltpu.make_async_copy(
            half_weight.at[:, columns(j)], own.at[lax.rem(j, 2)], own_sem.at[lax.rem(j, 2)]
        )

    fetched(0).start()

    def send(j, carry):
        sent(j).start()
        return carry

    lax.fori_loop(0, tiles, send, 0)
    low = lax.dot_general(
        context[...], down[...], (((1,), (1,)), ((), ())), preferred_element_type=f32
    ).astype(bf16)
    narrow[...] = low.astype(f32)
    squares[...] = jnp.zeros_like(squares)
    hidden_up[...] = jnp.zeros_like(hidden_up)

    def step(weight, start):
        at = pl.ds(pl.multiple_of(start, tile), tile)
        up_tile = up[:, at]
        value = (
            residual[:, at].astype(f32)
            + jnp.dot(context[...], weight, preferred_element_type=f32)
            + adapter_scale * jnp.dot(low, up_tile, preferred_element_type=f32)
        )
        squares[...] += jnp.sum(value * value, axis=1, keepdims=True)
        value = value.astype(bf16)
        hidden[:, at] = value
        hidden_up[...] += lax.dot_general(
            value, up_tile, (((1,), (1,)), ((), ())), preferred_element_type=f32
        )

    def own_step(j, carry):
        fetched(j).wait()

        @pl.when(j + 1 < tiles)
        def _():
            fetched(j + 1).start()

        step(own[lax.rem(j, 2)], core * half + j * tile)
        return carry

    lax.fori_loop(0, tiles, own_step, 0)

    def other_step(j, carry):
        sent(j).wait_recv()
        step(other[j], (1 - core) * half + j * tile)
        return carry

    lax.fori_loop(0, tiles, other_step, 0)
    inverse[...] = lax.rsqrt(squares[...] / MODEL_WIDTH + epsilon)

    def done(j, carry):
        sent(j).wait_send()
        return carry

    lax.fori_loop(0, tiles, done, 0)


def layer_forward(context, half_weight, residual, down, up):
    tokens, width = context.shape
    half = half_weight.shape[1]
    tile = 256
    tiles = half // tile
    rank = up.shape[0]
    vmem = pl.BlockSpec(memory_space=pltpu.VMEM)
    return pl.pallas_call(
        layer_forward_kernel,
        out_shape=(
            jax.ShapeDtypeStruct((tokens, width), bf16),
            jax.ShapeDtypeStruct((tokens, rank), f32),
            jax.ShapeDtypeStruct((tokens, rank), f32),
            jax.ShapeDtypeStruct((tokens, 1), f32),
        ),
        in_specs=[vmem, pl.BlockSpec(memory_space=pl.ANY), vmem, vmem, vmem],
        out_specs=(vmem, vmem, vmem, vmem),
        scratch_shapes=[
            pltpu.VMEM((2, width, tile), bf16),
            pltpu.VMEM((tiles, width, tile), bf16),
            pltpu.SemaphoreType.DMA((2,)),
            pltpu.SemaphoreType.DMA((tiles,)),
            pltpu.SemaphoreType.DMA((tiles,)),
            pltpu.VMEM((tokens, 1), f32),
        ],
        compiler_params=pltpu.CompilerParams(
            collective_id=1, has_side_effects=True, vmem_limit_bytes=44 * 1024 * 1024
        ),
        cost_estimate=pl.CostEstimate(flops=1000, bytes_accessed=1000, transcendentals=0),
        name="layer_forward",
    )(context, half_weight, residual, down, up)


def torus_place():
    return tuple(lax.axis_index(axis) for axis in PB_PA)


def flat_of(place):
    return ((place[0] * 2 + place[1]) * 4 + place[2]) * 4 + place[3]


def torus_peer(place, j):
    return (
        lax.rem(place[0] + lax.rem(j, 4), 4),
        lax.rem(place[1] + j // 64, 2),
        lax.rem(place[2] + lax.rem(j // 4, 4), 4),
        lax.rem(place[3] + lax.rem(j // 16, 4), 4),
    )


def far_kernel(
    score_scale, arrived, passages, near_mass, key_column, key_row, mean, scores, mix, log_total,
    log_arrived, rows, weights, inverse, means, mass, mass_in, log_out, row_sem, mean_sem,
    mass_send, mass_recv, log_send, log_recv,
):
    place = torus_place()
    own = flat_of(place)
    peers, slot_rows, lanes = mass.shape
    all_rows = peers * slot_rows
    hard_count = key_row.shape[0]
    query_count = near_mass.shape[0]
    width = passages.shape[1]
    chunks = row_sem.shape[0]
    block = all_rows // chunks
    block_peers = peers // chunks
    barrier = pltpu.get_barrier_semaphore()

    def greet(j, carry):
        pl.semaphore_signal(
            barrier, inc=1, device_id=torus_peer(place, j), device_id_type=MESH
        )
        return carry

    def part(c):
        return pl.ds(pl.multiple_of(c * block, block), block)

    def came_in(c):
        return pltpu.make_async_copy(arrived.at[part(c)], rows.at[part(c)], row_sem.at[c])

    def went_out(c):
        return pltpu.make_async_copy(means.at[part(c)], mean.at[part(c)], mean_sem.at[c])

    for c in range(chunks):
        came_in(c).start()
    lax.fori_loop(1, peers, greet, 0)

    def score(c, carry):
        came_in(c).wait()
        value = score_scale * lax.dot_general(
            rows[part(c), :], passages[...], (((1,), (1,)), ((), ())),
            preferred_element_type=f32,
        )
        scores[part(c), :] = value
        peak = jnp.max(value, axis=1, keepdims=True)
        weight = jnp.exp(value - peak)
        total = jnp.sum(weight, axis=1, keepdims=True)
        weights[part(c), :] = weight.astype(bf16)
        inverse[part(c), :] = 1.0 / total
        spread = jnp.broadcast_to(peak + jnp.log(total), (block, lanes))
        mass[pl.ds(c * block_peers, block_peers)] = spread.reshape(block_peers, slot_rows, lanes)
        return carry

    lax.fori_loop(0, chunks, score, 0)
    pl.semaphore_wait(barrier, peers - 1)

    def sends(source, target, send_sem, recv_sem):
        def body(j, carry):
            peer = torus_peer(place, j)
            pltpu.make_async_remote_copy(
                source.at[flat_of(peer)], target.at[own], send_sem, recv_sem,
                device_id=peer, device_id_type=MESH,
            ).start()
            return carry

        lax.fori_loop(1, peers, body, 0)

    def every(source, target, send_sem, recv_sem):
        rest = pl.ds(0, peers - 1)
        return pltpu.make_async_remote_copy(
            source.at[rest], target.at[rest], send_sem, recv_sem,
            device_id=torus_peer(place, 1), device_id_type=MESH,
        )

    sends(mass, mass_in, mass_send, mass_recv)
    mass_in[own] = mass[own]

    def average(c, carry):
        weight = weights[part(c), :]
        scale = inverse[part(c), :]
        tile = 512
        for start in range(0, width, tile):
            value = jnp.dot(
                weight, passages[:, start : start + tile], preferred_element_type=f32
            )
            means[part(c), start : start + tile] = (value * scale).astype(bf16)
        went_out(c).start()
        return carry

    lax.fori_loop(0, chunks, average, 0)
    row_ids = lax.broadcasted_iota(jnp.int32, (query_count, all_rows), 1)
    hits = [
        key_column[t * query_count : (t + 1) * query_count, :] == row_ids
        for t in range(hard_count)
    ]
    column_ids = lax.broadcasted_iota(jnp.int32, (all_rows, query_count), 0)
    picks = jnp.zeros((all_rows, query_count), f32)
    for t in range(hard_count):
        picks = jnp.where(column_ids == key_row[t : t + 1, :], 1.0, picks)
    filled = jnp.sum(picks, axis=1, keepdims=True) > 0.0
    every(mass, mass_in, mass_send, mass_recv).wait_recv()
    came = mass_in[...].reshape(all_rows, lanes)
    masses = [jnp.broadcast_to(near_mass[...], (query_count, lanes))]
    for hit in hits:
        masses.append(
            jnp.dot(
                jnp.where(hit, 1.0, 0.0), came,
                precision=lax.Precision.HIGHEST, preferred_element_type=f32,
            )
        )
    peak = masses[0]
    for value in masses[1:]:
        peak = jnp.maximum(peak, value)
    total = jnp.exp(masses[0] - peak)
    for value in masses[1:]:
        total = total + jnp.exp(value - peak)
    log_value = peak + jnp.log(total)
    log_total[...] = log_value
    outgoing = jnp.dot(
        picks, log_value, precision=lax.Precision.HIGHEST, preferred_element_type=f32
    )
    outgoing = jnp.where(filled, outgoing, absent_mass)
    log_out[...] = outgoing.reshape(log_out.shape)
    sends(log_out, log_arrived, log_send, log_recv)
    log_arrived[own] = log_out[own]
    shares = jnp.zeros((query_count, all_rows), f32)
    for t in range(hard_count):
        shares = jnp.where(hits[t], jnp.exp(masses[1 + t] - log_value)[:, :1], shares)
    high = shares.astype(bf16)
    mix[:query_count, :] = high
    mix[query_count:, :] = (shares - high.astype(f32)).astype(bf16)
    every(mass, mass_in, mass_send, mass_recv).wait_send()
    for c in range(chunks):
        went_out(c).wait()
    last = every(log_out, log_arrived, log_send, log_recv)
    last.wait_send()
    last.wait_recv()


def far_forward(arrived, passages, near_mass, key, peers, score_scale):
    all_rows, width = arrived.shape
    passage_count = passages.shape[0]
    hard_count, query_count = key.shape
    lanes, chunks = 128, 4
    small = (peers, all_rows // peers, lanes)
    vmem = pl.BlockSpec(memory_space=pltpu.VMEM)
    hbm = pl.BlockSpec(memory_space=pl.ANY)
    dma = pltpu.SemaphoreType.DMA
    return pl.pallas_call(
        functools.partial(far_kernel, score_scale),
        out_shape=(
            jax.ShapeDtypeStruct((all_rows, width), bf16),
            jax.ShapeDtypeStruct((all_rows, passage_count), f32),
            jax.ShapeDtypeStruct((2 * query_count, all_rows), bf16),
            jax.ShapeDtypeStruct((query_count, lanes), f32),
            jax.ShapeDtypeStruct(small, f32),
        ),
        in_specs=[hbm, vmem, vmem, vmem, vmem],
        out_specs=(hbm, vmem, vmem, vmem, vmem),
        scratch_shapes=[
            pltpu.VMEM((all_rows, width), bf16),
            pltpu.VMEM((all_rows, passage_count), bf16),
            pltpu.VMEM((all_rows, 1), f32),
            pltpu.VMEM((all_rows, width), bf16),
            pltpu.VMEM(small, f32),
            pltpu.VMEM(small, f32),
            pltpu.VMEM(small, f32),
            dma((chunks,)),
            dma((chunks,)),
            dma(()),
            dma(()),
            dma(()),
            dma(()),
        ],
        compiler_params=pltpu.CompilerParams(
            collective_id=2, has_side_effects=True, vmem_limit_bytes=44 * 1024 * 1024
        ),
        name="far_forward",
    )(arrived, passages, near_mass[:, None], key.reshape(-1)[:, None], key)


def tail_kernel(
    gradient_scale, returned, mix, near_part, norm, hidden, context, up, narrow, hidden_up, inverse,
    gradient, piece, rows, hid, ctx, grad, scaled, products, scaled_up, terms, first, part, second,
    row_sem, hid_sem, ctx_sem, grad_sem, send1, recv1, send2, recv2,
):
    place = torus_place()
    own = flat_of(place)
    lane_group = place[3]
    column = own // 4
    peers = 128
    tiles = row_sem.shape[0]
    width = terms.shape[2] * terms.shape[0]
    tile = width // tiles
    lanes = terms.shape[2]
    count = terms.shape[0]
    columns = first.shape[0]
    per_tile = tile // lanes
    query_count = gradient.shape[0]
    rerun = scaled.shape[0]
    rank = up.shape[0]
    tokens = narrow.shape[0]
    exact = dict(precision=lax.Precision.HIGHEST, preferred_element_type=f32)
    over_rows = (((0,), (0,)), ((), ()))
    over_lanes = (((1,), (1,)), ((), ()))

    def at(j):
        return pl.ds(pl.multiple_of(j * tile, tile), tile)

    def came_in(j):
        return pltpu.make_async_copy(returned.at[:, at(j)], rows.at[:, at(j)], row_sem.at[j])

    hid_in = pltpu.make_async_copy(hidden, hid, hid_sem)
    ctx_in = pltpu.make_async_copy(context, ctx, ctx_sem)
    came_in(0).start()
    hid_in.start()
    for j in range(1, tiles):
        came_in(j).start()
    ctx_in.start()
    barrier = pltpu.get_barrier_semaphore()

    def greet(j, carry):
        pl.semaphore_signal(
            barrier, inc=1, device_id=torus_peer(place, j), device_id_type=MESH
        )
        return carry

    lax.fori_loop(1, peers, greet, 0)
    products[...] = jnp.zeros_like(products)
    scaled_up[...] = jnp.zeros_like(scaled_up)
    hid_in.wait()

    def mixing(j, carry):
        came_in(j).wait()
        both = jnp.dot(mix[...], rows[:, at(j)], preferred_element_type=f32)
        value = gradient_scale * (both[:query_count] + both[query_count:] + near_part[:, at(j)])
        grad[:, at(j)] = value
        spread = norm[:, at(j)] * (value[:rerun] / TQ)
        scaled[:, at(j)] = spread
        products[...] += lax.dot_general(
            hid[:, at(j)], spread.astype(bf16), over_lanes, preferred_element_type=f32
        )
        scaled_up[...] += lax.dot_general(spread, up[:, at(j)].astype(f32), over_lanes, **exact)
        return carry

    lax.fori_loop(0, tiles, mixing, 0)
    gradient_out = pltpu.make_async_copy(grad, gradient, grad_sem)
    gradient_out.start()

    token_query = lax.broadcasted_iota(jnp.int32, (tokens, rerun), 0) // TQ
    of_query = token_query == lax.broadcasted_iota(jnp.int32, (tokens, rerun), 1)
    hot = jnp.where(of_query, 1.0, 0.0)
    mean = jnp.sum(jnp.where(of_query, products[...], 0.0), axis=1, keepdims=True) / width
    rms = inverse[...]
    slope = rms * rms * rms * mean
    spread_up = jnp.dot(hot, scaled_up[...], **exact)
    grad_narrow = (adapter_scale * (rms * spread_up - slope * hidden_up[...])).astype(bf16)
    weighted = (slope * narrow[...]).astype(bf16)
    sums = lax.dot_general(hot, rms * narrow[...], over_rows, **exact)
    ctx_in.wait()

    def products_of(j, carry):
        down = lax.dot_general(
            grad_narrow, ctx[:, at(j)], over_rows, preferred_element_type=f32
        ) / RERUN_QUERIES
        up_part = (adapter_scale / RERUN_QUERIES) * (
            lax.dot_general(sums, scaled[:, at(j)], over_rows, **exact)
            - lax.dot_general(weighted, hid[:, at(j)], over_rows, preferred_element_type=f32)
        )
        for k in range(per_tile):
            terms[j * per_tile + k, :rank, :] = down[:, k * lanes : (k + 1) * lanes]
            terms[j * per_tile + k, rank:, :] = up_part[:, k * lanes : (k + 1) * lanes]
        return carry

    lax.fori_loop(0, tiles, products_of, 0)
    pl.semaphore_wait(barrier, peers - 1)

    def stage1(j):
        to = (j // 8, lax.rem(j // 4, 2), lax.rem(j, 4), lane_group)
        return pltpu.make_async_remote_copy(
            terms.at[j], first.at[column], send1, recv1, device_id=to, device_id_type=MESH
        )

    def start1(j, carry):
        @pl.when(j != column)
        def _():
            stage1(j).start()

        return carry

    lax.fori_loop(0, count, start1, 0)
    gathers = column < count
    base = (lanes * column) // 28
    last = (lanes * column + lanes - 1) // 28
    tile0 = (28 * own) // lanes
    tile1 = (28 * own + 27) // lanes

    def sized(buffer, n, send_sem, recv_sem):
        piece_of = buffer.at[pl.ds(0, n)]
        return pltpu.make_async_remote_copy(
            piece_of, piece_of, send_sem, recv_sem,
            device_id=torus_peer(place, 1), device_id_type=MESH,
        )

    @pl.when(tile0 == tile1)
    def _():
        second[1] = jnp.zeros(second.shape[1:], f32)

    def stage2(i):
        e = base + i
        slot = column - (28 * e) // lanes
        to = (e // 32, lax.rem(e // 16, 2), lax.rem(e // 4, 4), lax.rem(e, 4))
        return pltpu.make_async_remote_copy(
            part, second.at[slot, lane_group], send2.at[i], recv2.at[slot, lane_group],
            device_id=to, device_id_type=MESH,
        )

    @pl.when(gathers)
    def _():
        first[column] = terms[column]
        sized(first, columns - 1, send1, recv1).wait_recv()
        part[...] = jnp.sum(first[...], axis=0)
        for i in range(6):
            e = base + i

            @pl.when((e <= last) & (e != own))
            def _():
                stage2(i).start()

            @pl.when((e <= last) & (e == own))
            def _():
                second[column - tile0, lane_group] = part[...]

        sized(terms, count - 1, send1, recv1).wait_send()

    @pl.when(column >= count)
    def _():
        sized(terms, count, send1, recv1).wait_send()

    for slot in range(2):
        from_tile = tile0 + slot
        for b in range(4):
            @pl.when((from_tile <= tile1) & ((from_tile != column) | (lane_group != b)))
            def _():
                pltpu.make_async_remote_copy(
                    part, second.at[slot, b], send2.at[0], recv2.at[slot, b],
                    device_id=torus_peer(place, 1), device_id_type=MESH,
                ).wait_recv()

    left = jnp.sum(second[0], axis=0)
    right = jnp.sum(second[1], axis=0)
    offset = 28 * own - lanes * tile0
    source = lax.broadcasted_iota(jnp.int32, (lanes, lanes), 0)
    target = lax.broadcasted_iota(jnp.int32, (lanes, lanes), 1) + offset
    piece[...] = jnp.dot(left, jnp.where(source == target, 1.0, 0.0), **exact) + jnp.dot(
        right, jnp.where(source + lanes == target, 1.0, 0.0), **exact
    )

    @pl.when(gathers)
    def _():
        for i in range(6):
            e = base + i

            @pl.when((e <= last) & (e != own))
            def _():
                stage2(i).wait_send()

    gradient_out.wait()


def tail(returned, mix, near_part, norm, hidden, context, up, narrow, hidden_up, inverse, scale):
    all_rows, width = returned.shape
    query_count = near_part.shape[0]
    tokens, rank = narrow.shape
    tiles, lanes, rerun = 7, 128, RERUN_QUERIES
    vmem = pl.BlockSpec(memory_space=pltpu.VMEM)
    hbm = pl.BlockSpec(memory_space=pl.ANY)
    dma = pltpu.SemaphoreType.DMA
    return pl.pallas_call(
        functools.partial(tail_kernel, scale),
        out_shape=(
            jax.ShapeDtypeStruct((query_count, width), f32),
            jax.ShapeDtypeStruct((2 * rank, lanes), f32),
        ),
        in_specs=[hbm, vmem, vmem, vmem, hbm, hbm, vmem, vmem, vmem, vmem],
        out_specs=(hbm, vmem),
        scratch_shapes=[
            pltpu.VMEM((all_rows, width), bf16),
            pltpu.VMEM((tokens, width), bf16),
            pltpu.VMEM((tokens, width), bf16),
            pltpu.VMEM((query_count, width), f32),
            pltpu.VMEM((rerun, width), f32),
            pltpu.VMEM((tokens, rerun), f32),
            pltpu.VMEM((rerun, rank), f32),
            pltpu.VMEM((width // lanes, 2 * rank, lanes), f32),
            pltpu.VMEM((32, 2 * rank, lanes), f32),
            pltpu.VMEM((2 * rank, lanes), f32),
            pltpu.VMEM((2, 4, 2 * rank, lanes), f32),
            dma((tiles,)),
            dma(()),
            dma(()),
            dma(()),
            dma(()),
            dma(()),
            dma((6,)),
            dma((2, 4)),
        ],
        compiler_params=pltpu.CompilerParams(
            collective_id=3, has_side_effects=True, vmem_limit_bytes=44 * 1024 * 1024
        ),
        name="tail",
    )(returned, mix, near_part, norm, hidden, context, up, narrow, hidden_up, inverse)


def local(
    queries,
    passages,
    hard_block_offsets,
    positive,
    context,
    residual,
    output_weight,
    adapter_down_weight,
    adapter_up_weight,
    final_norm_weight,
):
    device_count = lax.axis_size(PB_PA)
    block_count, hard_count = hard_block_offsets.shape
    query_count = queries.shape[0]
    block_rows = query_count // block_count
    capacity = 2 * block_count * hard_count // device_count
    slot_rows = capacity * block_rows
    all_rows = device_count * slot_rows
    passage_count = passages.shape[0]
    score_scale = inverse_temp / math.sqrt(MODEL_WIDTH)

    weight_rows = gathered_weight_input(output_weight)

    source = lax.axis_index(PB_PA)
    target = ((source + 1 + hard_block_offsets) % device_count).reshape(-1)
    order = jnp.arange(target.shape[0], dtype=jnp.int32)
    earlier = (target[:, None] == target[None, :]) & (order[:, None] > order[None, :])
    slot = target * capacity + jnp.sum(earlier.astype(jnp.int32), axis=1)
    slot_of = slot.reshape(block_count, hard_count).T
    key = jnp.repeat(slot_of, block_rows, axis=1) * block_rows + (
        jnp.arange(query_count, dtype=jnp.int32) % block_rows
    )
    row_ids = jnp.arange(all_rows, dtype=jnp.int32)
    picks = row_ids[:, None] == key[0][None, :]
    for t in range(1, hard_count):
        picks = picks | (row_ids[:, None] == key[t][None, :])
    outgoing = jnp.dot(picks.astype(bf16), queries, preferred_element_type=bf16)
    arrived = exchange(outgoing.reshape(device_count, slot_rows, MODEL_WIDTH))
    arrived = arrived.reshape(-1, MODEL_WIDTH)

    half_weight = lax.all_gather(weight_rows, CHIPS, axis=0, tiled=True)
    near_scores = dot(queries, passages.T) * score_scale
    near_peak = jnp.max(near_scores, axis=1)
    near_exp = jnp.exp(near_scores - near_peak[:, None])
    near_sum = jnp.sum(near_exp, axis=1)
    near_mass = near_peak + jnp.log(near_sum)
    positive_hot = positive[:, None] == jnp.arange(passage_count, dtype=jnp.int32)[None, :]
    stacked = dot(
        jnp.concatenate([near_exp.astype(bf16), positive_hot.astype(bf16)], axis=0), passages
    )

    far_mean, far_scores, mix_parts, log_total, log_arrived = far_forward(
        arrived, passages, near_mass, key, device_count, score_scale
    )
    returned = exchange(far_mean.reshape(device_count, slot_rows, MODEL_WIDTH))
    returned = returned.reshape(-1, MODEL_WIDTH)
    log_total = log_total[:, 0]
    log_arrived = log_arrived.reshape(all_rows, -1)[:, :1]
    near_share = jnp.exp(near_mass - log_total)
    near_part = (near_share / near_sum)[:, None] * stacked[:query_count] - stacked[query_count:]

    product_dims = (((0,), (0,)), ((), ()))
    far_weight = jnp.exp(far_scores - log_arrived).astype(bf16)
    near_weight = (
        jnp.exp(near_scores - log_total[:, None]) - positive_hot.astype(f32)
    ).astype(bf16)
    far_grad = lax.dot_general(far_weight, arrived, product_dims, preferred_element_type=f32)
    near_grad = lax.dot_general(near_weight, queries, product_dims, preferred_element_type=f32)

    hidden_low, narrow, hidden_up, inverse_rms = layer_forward(
        context, half_weight, residual, adapter_down_weight.T, adapter_up_weight
    )
    grad_passages = loss_scale * score_scale * (far_grad + near_grad)

    returned, near_part, hidden_low, grad_passages = lax.optimization_barrier(
        (returned, near_part, hidden_low, grad_passages)
    )
    query_gradient, sums = tail(
        returned,
        mix_parts,
        near_part,
        final_norm_weight.astype(f32)[None, :],
        hidden_low,
        context,
        adapter_up_weight,
        narrow,
        hidden_up,
        inverse_rms,
        loss_scale * score_scale,
    )
    rank = narrow.shape[1]
    columns = MODEL_WIDTH // device_count
    return (
        query_gradient,
        grad_passages,
        sums[:rank, :columns].T,
        sums[rank:, :columns],
    )


def solution(mesh):
    torus = Mesh(mesh.devices.reshape(4, 2, 4, 4), PB_PA)
    in_specs = (
        P(PB_PA, None),
        P(PB_PA, None),
        P(PB_PA, None),
        P(PB_PA),
        P(PB_PA, None),
        P(PB_PA, None),
        P(PB_PA, None),
        P(),
        P(),
        P(),
    )
    out_specs = (P(PB_PA, None), P(PB_PA, None), P(PB_PA, None), P(None, PB_PA))
    return jax.shard_map(local, mesh=torus, in_specs=in_specs, out_specs=out_specs, check_vma=False)
```

```python
import functools
import math

import jax
import jax.numpy as jnp
from jax import lax
from jax.experimental import pallas as pl
from jax.experimental.pallas import tpu as pltpu
from jax.sharding import Mesh
from jax.sharding import PartitionSpec as P

MODEL_WIDTH = 3584
RERUN_QUERIES = 16
TQ = 32
PB_PA = ("pb_0", "pb_1", "pa_0", "pa_1")
CHIPS = ("pb_0", "pa_0", "pa_1")

inverse_temp = 2.0
loss_scale = 32.0
adapter_scale = 2.0
epsilon = 1e-06
absent_mass = 1e30
f32 = jnp.float32
bf16 = jnp.bfloat16
MESH = pl.DeviceIdType.MESH


def dot(a, b, **kw):
    return jnp.dot(a, b, preferred_element_type=f32, **kw)


def two_parts(x):
    high = x.astype(bf16)
    return high, (x - high.astype(f32)).astype(bf16)


def device_of(chip, core, per_plane):
    return (chip // per_plane) * 2 * per_plane + core * per_plane + chip % per_plane


def weight_halves_sent(rows):
    count = lax.axis_size(PB_PA)
    per_plane = lax.axis_size("pa_0") * lax.axis_size("pa_1")
    half = rows.shape[1] // 2
    left, right = rows[:, :half], rows[:, half:]
    odd = lax.axis_index("pa_1") % 2 == 1
    same = [(f, device_of(f // 2, f % 2, per_plane)) for f in range(count)]
    other = [(f, device_of(f // 2, 1 - f % 2, per_plane)) for f in range(count)]
    first = lax.ppermute(jnp.where(odd, right, left), PB_PA, same)
    second = lax.ppermute(jnp.where(odd, left, right), PB_PA, other)
    return first, second


def gather_input(first, second):
    core = lax.axis_index("pb_1")
    low = jnp.where(core == 0, first, second)
    high = jnp.where(core == 0, second, first)
    return jnp.concatenate([low, high], axis=0)


def exchange(array):
    return lax.all_to_all(array, PB_PA, split_axis=0, concat_axis=0, tiled=True)


def layer_forward_kernel(
    context, half_weight, residual, down, up, hidden, narrow, hidden_up, inverse,
    own, other, own_sem, send_sem, recv_sem, squares,
):
    core = lax.axis_index("pb_1")
    twin = (lax.axis_index("pb_0"), 1 - core, lax.axis_index("pa_0"), lax.axis_index("pa_1"))
    tile = own.shape[2]
    half = half_weight.shape[1]
    tiles = half // tile
    barrier = pltpu.get_barrier_semaphore()
    pl.semaphore_signal(barrier, inc=1, device_id=twin, device_id_type=MESH)
    pl.semaphore_wait(barrier, 1)

    def columns(j):
        return pl.ds(pl.multiple_of(j * tile, tile), tile)

    def sent(j):
        return pltpu.make_async_remote_copy(
            half_weight.at[:, columns(j)], other.at[j], send_sem.at[j], recv_sem.at[j],
            device_id=twin, device_id_type=MESH,
        )

    def fetched(j):
        return pltpu.make_async_copy(
            half_weight.at[:, columns(j)], own.at[lax.rem(j, 2)], own_sem.at[lax.rem(j, 2)]
        )

    fetched(0).start()

    def send(j, carry):
        sent(j).start()
        return carry

    lax.fori_loop(0, tiles, send, 0)
    low = lax.dot_general(
        context[...], down[...], (((1,), (1,)), ((), ())), preferred_element_type=f32
    ).astype(bf16)
    narrow[...] = low.astype(f32)
    squares[...] = jnp.zeros_like(squares)
    hidden_up[...] = jnp.zeros_like(hidden_up)

    def step(weight, start):
        at = pl.ds(pl.multiple_of(start, tile), tile)
        up_tile = up[:, at]
        value = (
            residual[:, at].astype(f32)
            + jnp.dot(context[...], weight, preferred_element_type=f32)
            + adapter_scale * jnp.dot(low, up_tile, preferred_element_type=f32)
        )
        squares[...] += jnp.sum(value * value, axis=1, keepdims=True)
        value = value.astype(bf16)
        hidden[:, at] = value
        hidden_up[...] += lax.dot_general(
            value, up_tile, (((1,), (1,)), ((), ())), preferred_element_type=f32
        )

    def own_step(j, carry):
        fetched(j).wait()

        @pl.when(j + 1 < tiles)
        def _():
            fetched(j + 1).start()

        step(own[lax.rem(j, 2)], core * half + j * tile)
        return carry

    lax.fori_loop(0, tiles, own_step, 0)

    def other_step(j, carry):
        sent(j).wait_recv()
        step(other[j], (1 - core) * half + j * tile)
        return carry

    lax.fori_loop(0, tiles, other_step, 0)
    inverse[...] = lax.rsqrt(squares[...] / MODEL_WIDTH + epsilon)

    def done(j, carry):
        sent(j).wait_send()
        return carry

    lax.fori_loop(0, tiles, done, 0)


def layer_forward(context, half_weight, residual, down, up):
    tokens, width = context.shape
    half = half_weight.shape[1]
    tile = 256
    tiles = half // tile
    rank = up.shape[0]
    vmem = pl.BlockSpec(memory_space=pltpu.VMEM)
    return pl.pallas_call(
        layer_forward_kernel,
        out_shape=(
            jax.ShapeDtypeStruct((tokens, width), bf16),
            jax.ShapeDtypeStruct((tokens, rank), f32),
            jax.ShapeDtypeStruct((tokens, rank), f32),
            jax.ShapeDtypeStruct((tokens, 1), f32),
        ),
        in_specs=[vmem, pl.BlockSpec(memory_space=pl.ANY), vmem, vmem, vmem],
        out_specs=(vmem, vmem, vmem, vmem),
        scratch_shapes=[
            pltpu.VMEM((2, width, tile), bf16),
            pltpu.VMEM((tiles, width, tile), bf16),
            pltpu.SemaphoreType.DMA((2,)),
            pltpu.SemaphoreType.DMA((tiles,)),
            pltpu.SemaphoreType.DMA((tiles,)),
            pltpu.VMEM((tokens, 1), f32),
        ],
        compiler_params=pltpu.CompilerParams(
            collective_id=1, has_side_effects=True, vmem_limit_bytes=44 * 1024 * 1024
        ),
        cost_estimate=pl.CostEstimate(flops=1000, bytes_accessed=1000, transcendentals=0),
        name="layer_forward",
    )(context, half_weight, residual, down, up)


def torus_place():
    return tuple(lax.axis_index(axis) for axis in PB_PA)


def flat_of(place):
    return ((place[0] * 2 + place[1]) * 4 + place[2]) * 4 + place[3]


def torus_peer(place, j):
    return (
        lax.rem(place[0] + lax.rem(j, 4), 4),
        lax.rem(place[1] + j // 64, 2),
        lax.rem(place[2] + lax.rem(j // 4, 4), 4),
        lax.rem(place[3] + lax.rem(j // 16, 4), 4),
    )


def far_kernel(
    score_scale, arrived, passages_in, near_mass, key_column, mean, scores, mix, log_total,
    log_column, rows, passages, weights, inverse, means, mass, log_out, mass1, mass2, mass3, log1,
    log2, log3, row_sem, passage_sem, mean_sem, send_sem, recv_sem,
):
    place = torus_place()
    outer = place[0] * 2 + place[1]
    inner = place[2] * 4 + place[3]
    outers, inners, lanes = mass.shape
    peers = outers * inners
    query_count = near_mass.shape[0]
    hard_count = key_column.shape[0] // query_count
    all_rows, passage_count = scores.shape
    slot_rows = all_rows // peers
    width = passages.shape[1]
    chunks = row_sem.shape[0]
    block = all_rows // chunks
    exact = dict(precision=lax.Precision.HIGHEST, preferred_element_type=f32)

    def along_outer(d):
        to = lax.rem(outer + d, outers)
        return to, (to // 2, lax.rem(to, 2), place[2], place[3])

    def along_inner(d):
        to = lax.rem(inner + d, inners)
        return to, (place[0], place[1], to // 4, lax.rem(to, 4))

    def part(c):
        return pl.ds(pl.multiple_of(c * block, block), block)

    def came_in(c):
        return pltpu.make_async_copy(arrived.at[part(c)], rows.at[part(c)], row_sem.at[c])

    def went_out(c):
        return pltpu.make_async_copy(means.at[part(c)], mean.at[part(c)], mean_sem.at[c])

    passages_here = pltpu.make_async_copy(passages_in, passages, passage_sem)
    passages_here.start()
    for c in range(chunks):
        came_in(c).start()
    barrier = pltpu.get_barrier_semaphore()
    for d in range(1, outers):
        pl.semaphore_signal(barrier, inc=1, device_id=along_outer(d)[1], device_id_type=MESH)
    for d in range(1, inners):
        pl.semaphore_signal(barrier, inc=1, device_id=along_inner(d)[1], device_id_type=MESH)
    passages_here.wait()
    lane_ids = lax.broadcasted_iota(jnp.int32, (block, lanes), 1)
    slot_ids = lax.rem(lax.broadcasted_iota(jnp.int32, (block, lanes), 0), slot_rows)
    block_peers = block // slot_rows
    peer_ids = lax.broadcasted_iota(jnp.int32, (block_peers, block), 0)
    peer_rows = lax.broadcasted_iota(jnp.int32, (block_peers, block), 1) // slot_rows
    gather_rows = jnp.where(peer_ids == peer_rows, 1.0, 0.0)

    def score(c, carry):
        came_in(c).wait()
        value = score_scale * lax.dot_general(
            rows[part(c), :], passages[...], (((1,), (1,)), ((), ())),
            preferred_element_type=f32,
        )
        scores[part(c), :] = value
        peak = jnp.max(value, axis=1, keepdims=True)
        weight = jnp.exp(value - peak)
        total = jnp.sum(weight, axis=1, keepdims=True)
        weights[part(c), :] = weight.astype(bf16)
        inverse[part(c), :] = 1.0 / total
        spread = jnp.where(lane_ids == slot_ids, peak + jnp.log(total), 0.0)
        compact = jnp.dot(gather_rows, spread, **exact)
        step = block_peers // inners
        mass[pl.ds(c * step, step)] = compact.reshape(step, inners, lanes)
        return carry

    lax.fori_loop(0, chunks, score, 0)
    pl.semaphore_wait(barrier, outers - 1 + inners - 1)

    def hop1(source, target, which):
        for d in range(1, outers):
            to, device = along_outer(d)
            pltpu.make_async_remote_copy(
                source.at[to], target.at[outer], send_sem.at[which], recv_sem.at[which],
                device_id=device, device_id_type=MESH,
            ).start()
        target[outer] = source[outer]

    def hop2(source, target, which):
        for d in range(1, inners):
            to, device = along_inner(d)
            pltpu.make_async_remote_copy(
                source.at[to], target.at[inner], send_sem.at[which], recv_sem.at[which],
                device_id=device, device_id_type=MESH,
            ).start()
        target[inner] = source[inner]

    def others(source, target, which):
        rest = pl.ds(0, source.shape[0] - 1)
        return pltpu.make_async_remote_copy(
            source.at[rest], target.at[rest], send_sem.at[which], recv_sem.at[which],
            device_id=along_outer(1)[1], device_id_type=MESH,
        )

    def repack(source, target):
        for r in range(inners):
            target[r] = source[:, r, :]

    def average(c, carry):
        weight = weights[part(c), :]
        scale = inverse[part(c), :]
        tile = 512
        for start in range(0, width, tile):
            value = jnp.dot(
                weight, passages[:, start : start + tile], preferred_element_type=f32
            )
            means[part(c), start : start + tile] = (value * scale).astype(bf16)
        went_out(c).start()
        return carry

    hop1(mass, mass1, 0)
    lax.fori_loop(0, chunks // 2, average, 0)
    others(mass, mass1, 0).wait_recv()
    repack(mass1, mass2)
    hop2(mass2, mass3, 1)
    lax.fori_loop(chunks // 2, chunks, average, 0)

    key = key_column[...]
    peer = key // slot_rows
    slot = lax.rem(key, slot_rows)
    pairs = key.shape[0]
    ids = lax.broadcasted_iota(jnp.int32, (pairs, peers), 1)
    at_slot = lax.broadcasted_iota(jnp.int32, (pairs, lanes), 1) == slot
    to_peer = jnp.where(ids == peer, 1.0, 0.0)
    from_peer = jnp.where(ids == lax.rem(peer, inners) * outers + peer // inners, 1.0, 0.0)
    others(mass2, mass3, 1).wait_recv()
    came = jnp.dot(from_peer, mass3[...].reshape(peers, lanes), **exact)
    came = jnp.sum(jnp.where(at_slot, came, 0.0), axis=1, keepdims=True)
    masses = [near_mass[...]] + [
        came[t * query_count : (t + 1) * query_count] for t in range(hard_count)
    ]
    peak = masses[0]
    for value in masses[1:]:
        peak = jnp.maximum(peak, value)
    total = jnp.exp(masses[0] - peak)
    for value in masses[1:]:
        total = total + jnp.exp(value - peak)
    log_value = peak + jnp.log(total)
    log_total[...] = log_value
    log_pairs = jnp.concatenate([log_value] * hard_count, axis=0)
    over_pairs = (((0,), (0,)), ((), ()))
    outgoing = lax.dot_general(to_peer, jnp.where(at_slot, log_pairs, 0.0), over_pairs, **exact)
    filled = lax.dot_general(to_peer, jnp.where(at_slot, 1.0, 0.0), over_pairs, **exact)
    outgoing = jnp.where(filled > 0.5, outgoing, absent_mass)
    log_out[...] = outgoing.reshape(log_out.shape)
    hop1(log_out, log1, 2)
    row_ids = lax.broadcasted_iota(jnp.int32, (query_count, all_rows), 1)
    shares = jnp.zeros((query_count, all_rows), f32)
    for t in range(hard_count):
        hit = key[t * query_count : (t + 1) * query_count] == row_ids
        shares = jnp.where(hit, jnp.exp(masses[1 + t] - log_value), shares)
    high = shares.astype(bf16)
    mix[:query_count, :] = high
    mix[query_count:, :] = (shares - high.astype(f32)).astype(bf16)
    others(log_out, log1, 2).wait_recv()
    repack(log1, log2)
    hop2(log2, log3, 3)
    row = lax.broadcasted_iota(jnp.int32, (all_rows, peers), 0)
    row_peer = row // slot_rows
    back = lax.rem(row_peer, inners) * outers + row_peer // inners
    spread = jnp.where(
        lax.broadcasted_iota(jnp.int32, (all_rows, peers), 1) == back, 1.0, 0.0
    )
    mine = lax.broadcasted_iota(jnp.int32, (all_rows, lanes), 1) == lax.rem(
        lax.broadcasted_iota(jnp.int32, (all_rows, lanes), 0), slot_rows
    )
    for c in range(chunks):
        went_out(c).wait()
    others(mass, mass1, 0).wait_send()
    others(mass2, mass3, 1).wait_send()
    others(log_out, log1, 2).wait_send()
    others(log2, log3, 3).wait_recv()
    logs = jnp.dot(spread, log3[...].reshape(peers, lanes), **exact)
    log_column[...] = jnp.sum(jnp.where(mine, logs, 0.0), axis=1, keepdims=True)
    others(log2, log3, 3).wait_send()


def far_forward(arrived, passages, near_mass, key, peers, score_scale):
    all_rows, width = arrived.shape
    passage_count = passages.shape[0]
    hard_count, query_count = key.shape
    lanes, chunks, outers = 128, 4, 8
    inners = peers // outers
    by_outer = pltpu.VMEM((outers, inners, lanes), f32)
    by_inner = pltpu.VMEM((inners, outers, lanes), f32)
    vmem = pl.BlockSpec(memory_space=pltpu.VMEM)
    hbm = pl.BlockSpec(memory_space=pltpu.HBM)
    dma = pltpu.SemaphoreType.DMA
    return pl.pallas_call(
        functools.partial(far_kernel, score_scale),
        out_shape=(
            jax.ShapeDtypeStruct((all_rows, width), bf16),
            jax.ShapeDtypeStruct((all_rows, passage_count), f32),
            jax.ShapeDtypeStruct((2 * query_count, all_rows), bf16),
            jax.ShapeDtypeStruct((query_count, 1), f32),
            jax.ShapeDtypeStruct((all_rows, 1), f32),
        ),
        in_specs=[hbm, hbm, vmem, vmem],
        out_specs=(hbm, vmem, vmem, vmem, vmem),
        scratch_shapes=[
            pltpu.VMEM((all_rows, width), bf16),
            pltpu.VMEM((passage_count, width), bf16),
            pltpu.VMEM((all_rows, passage_count), bf16),
            pltpu.VMEM((all_rows, 1), f32),
            pltpu.VMEM((all_rows, width), bf16),
            by_outer,
            by_outer,
            by_outer,
            by_inner,
            by_inner,
            by_outer,
            by_inner,
            by_inner,
            dma((chunks,)),
            dma(()),
            dma((chunks,)),
            dma((4,)),
            dma((4,)),
        ],
        compiler_params=pltpu.CompilerParams(
            collective_id=2, has_side_effects=True, vmem_limit_bytes=44 * 1024 * 1024
        ),
        name="far_forward",
    )(arrived, passages, near_mass[:, None], key.reshape(-1)[:, None])


def tail_kernel(
    gradient_scale, returned, mix, near_part, norm, hidden, context, up, narrow, hidden_up, inverse,
    gradient, piece, rows, hid, ctx, grad, scaled, products, scaled_up, terms, first, part, second,
    row_sem, hid_sem, ctx_sem, grad_sem, send1, recv1, send2, recv2,
):
    place = torus_place()
    own = flat_of(place)
    lane_group = place[3]
    column = own // 4
    tiles = row_sem.shape[0]
    width = terms.shape[2] * terms.shape[0]
    tile = width // tiles
    lanes = terms.shape[2]
    count = terms.shape[0]
    columns = first.shape[0]
    per_tile = tile // lanes
    query_count = gradient.shape[0]
    rerun = scaled.shape[0]
    rank = up.shape[0]
    tokens = narrow.shape[0]
    exact = dict(precision=lax.Precision.HIGHEST, preferred_element_type=f32)
    over_rows = (((0,), (0,)), ((), ()))
    over_lanes = (((1,), (1,)), ((), ()))

    def at(j):
        return pl.ds(pl.multiple_of(j * tile, tile), tile)

    def came_in(j):
        return pltpu.make_async_copy(returned.at[:, at(j)], rows.at[:, at(j)], row_sem.at[j])

    hid_in = pltpu.make_async_copy(hidden, hid, hid_sem)
    ctx_in = pltpu.make_async_copy(context, ctx, ctx_sem)
    came_in(0).start()
    hid_in.start()
    for j in range(1, tiles):
        came_in(j).start()
    ctx_in.start()
    barrier = pltpu.get_barrier_semaphore()

    gathers = column < count
    base = (lanes * column) // 28
    last = (lanes * column + lanes - 1) // 28
    tile0 = (28 * own) // lanes
    tile1 = (28 * own + 27) // lanes

    def of_column(j, b):
        return (j // 8, lax.rem(j // 4, 2), lax.rem(j, 4), b)

    def greet(d, carry):
        to = of_column(lax.rem(column + d, columns), lane_group)
        pl.semaphore_signal(barrier, inc=1, device_id=to, device_id_type=MESH)
        return carry

    lax.fori_loop(1, columns, greet, 0)
    for slot in range(2):
        for b in range(4):
            @pl.when((tile0 + slot <= tile1) & ((tile0 + slot != column) | (lane_group != b)))
            def _():
                to = of_column(tile0 + slot, b)
                pl.semaphore_signal(barrier, inc=1, device_id=to, device_id_type=MESH)

    products[...] = jnp.zeros_like(products)
    scaled_up[...] = jnp.zeros_like(scaled_up)
    hid_in.wait()

    def mixing(j, carry):
        came_in(j).wait()
        both = jnp.dot(mix[...], rows[:, at(j)], preferred_element_type=f32)
        value = gradient_scale * (both[:query_count] + both[query_count:] + near_part[:, at(j)])
        grad[:, at(j)] = value
        spread = norm[:, at(j)] * (value[:rerun] / TQ)
        scaled[:, at(j)] = spread
        products[...] += lax.dot_general(
            hid[:, at(j)], spread.astype(bf16), over_lanes, preferred_element_type=f32
        )
        scaled_up[...] += lax.dot_general(spread, up[:, at(j)].astype(f32), over_lanes, **exact)
        return carry

    lax.fori_loop(0, tiles, mixing, 0)
    gradient_out = pltpu.make_async_copy(grad, gradient, grad_sem)
    gradient_out.start()

    token_query = lax.broadcasted_iota(jnp.int32, (tokens, rerun), 0) // TQ
    of_query = token_query == lax.broadcasted_iota(jnp.int32, (tokens, rerun), 1)
    hot = jnp.where(of_query, 1.0, 0.0)
    mean = jnp.sum(jnp.where(of_query, products[...], 0.0), axis=1, keepdims=True) / width
    rms = inverse[...]
    slope = rms * rms * rms * mean
    spread_up = jnp.dot(hot, scaled_up[...], **exact)
    grad_narrow = (adapter_scale * (rms * spread_up - slope * hidden_up[...])).astype(bf16)
    weighted = (slope * narrow[...]).astype(bf16)
    sums = lax.dot_general(hot, rms * narrow[...], over_rows, **exact)
    ctx_in.wait()

    def products_of(j, carry):
        down = lax.dot_general(
            grad_narrow, ctx[:, at(j)], over_rows, preferred_element_type=f32
        ) / RERUN_QUERIES
        up_part = (adapter_scale / RERUN_QUERIES) * (
            lax.dot_general(sums, scaled[:, at(j)], over_rows, **exact)
            - lax.dot_general(weighted, hid[:, at(j)], over_rows, preferred_element_type=f32)
        )
        for k in range(per_tile):
            terms[j * per_tile + k, :rank, :] = down[:, k * lanes : (k + 1) * lanes]
            terms[j * per_tile + k, rank:, :] = up_part[:, k * lanes : (k + 1) * lanes]
        return carry

    lax.fori_loop(0, tiles, products_of, 0)
    inside = jnp.where((base <= own) & (own <= last), 1, 0)
    pl.semaphore_wait(barrier, columns - 1 + jnp.where(gathers, last - base + 1 - inside, 0))

    def stage1(j):
        to = (j // 8, lax.rem(j // 4, 2), lax.rem(j, 4), lane_group)
        return pltpu.make_async_remote_copy(
            terms.at[j], first.at[column], send1, recv1, device_id=to, device_id_type=MESH
        )

    def start1(j, carry):
        @pl.when(j != column)
        def _():
            stage1(j).start()

        return carry

    lax.fori_loop(0, count, start1, 0)

    def sized(buffer, n, send_sem, recv_sem):
        piece_of = buffer.at[pl.ds(0, n)]
        return pltpu.make_async_remote_copy(
            piece_of, piece_of, send_sem, recv_sem,
            device_id=torus_peer(place, 1), device_id_type=MESH,
        )

    @pl.when(tile0 == tile1)
    def _():
        second[1] = jnp.zeros(second.shape[1:], f32)

    def stage2(i):
        e = base + i
        slot = column - (28 * e) // lanes
        to = (e // 32, lax.rem(e // 16, 2), lax.rem(e // 4, 4), lax.rem(e, 4))
        return pltpu.make_async_remote_copy(
            part, second.at[slot, lane_group], send2.at[i], recv2.at[slot, lane_group],
            device_id=to, device_id_type=MESH,
        )

    @pl.when(gathers)
    def _():
        first[column] = terms[column]
        sized(first, columns - 1, send1, recv1).wait_recv()
        part[...] = jnp.sum(first[...], axis=0)
        for i in range(6):
            e = base + i

            @pl.when((e <= last) & (e != own))
            def _():
                stage2(i).start()

            @pl.when((e <= last) & (e == own))
            def _():
                second[column - tile0, lane_group] = part[...]

        sized(terms, count - 1, send1, recv1).wait_send()

    @pl.when(column >= count)
    def _():
        sized(terms, count, send1, recv1).wait_send()

    for slot in range(2):
        from_tile = tile0 + slot
        for b in range(4):
            @pl.when((from_tile <= tile1) & ((from_tile != column) | (lane_group != b)))
            def _():
                pltpu.make_async_remote_copy(
                    part, second.at[slot, b], send2.at[0], recv2.at[slot, b],
                    device_id=torus_peer(place, 1), device_id_type=MESH,
                ).wait_recv()

    left = jnp.sum(second[0], axis=0)
    right = jnp.sum(second[1], axis=0)
    offset = 28 * own - lanes * tile0
    source = lax.broadcasted_iota(jnp.int32, (lanes, lanes), 0)
    target = lax.broadcasted_iota(jnp.int32, (lanes, lanes), 1) + offset
    piece[...] = jnp.dot(left, jnp.where(source == target, 1.0, 0.0), **exact) + jnp.dot(
        right, jnp.where(source + lanes == target, 1.0, 0.0), **exact
    )

    @pl.when(gathers)
    def _():
        for i in range(6):
            e = base + i

            @pl.when((e <= last) & (e != own))
            def _():
                stage2(i).wait_send()

    gradient_out.wait()


def tail(returned, mix, near_part, norm, hidden, context, up, narrow, hidden_up, inverse, scale):
    all_rows, width = returned.shape
    query_count = near_part.shape[0]
    tokens, rank = narrow.shape
    tiles, lanes, rerun = 7, 128, RERUN_QUERIES
    vmem = pl.BlockSpec(memory_space=pltpu.VMEM)
    hbm = pl.BlockSpec(memory_space=pltpu.HBM)
    dma = pltpu.SemaphoreType.DMA
    return pl.pallas_call(
        functools.partial(tail_kernel, scale),
        out_shape=(
            jax.ShapeDtypeStruct((query_count, width), f32),
            jax.ShapeDtypeStruct((2 * rank, lanes), f32),
        ),
        in_specs=[hbm, vmem, vmem, vmem, hbm, hbm, vmem, vmem, vmem, vmem],
        out_specs=(hbm, vmem),
        scratch_shapes=[
            pltpu.VMEM((all_rows, width), bf16),
            pltpu.VMEM((tokens, width), bf16),
            pltpu.VMEM((tokens, width), bf16),
            pltpu.VMEM((query_count, width), f32),
            pltpu.VMEM((rerun, width), f32),
            pltpu.VMEM((tokens, rerun), f32),
            pltpu.VMEM((rerun, rank), f32),
            pltpu.VMEM((width // lanes, 2 * rank, lanes), f32),
            pltpu.VMEM((32, 2 * rank, lanes), f32),
            pltpu.VMEM((2 * rank, lanes), f32),
            pltpu.VMEM((2, 4, 2 * rank, lanes), f32),
            dma((tiles,)),
            dma(()),
            dma(()),
            dma(()),
            dma(()),
            dma(()),
            dma((6,)),
            dma((2, 4)),
        ],
        compiler_params=pltpu.CompilerParams(
            collective_id=3, has_side_effects=True, vmem_limit_bytes=44 * 1024 * 1024
        ),
        name="tail",
    )(returned, mix, near_part, norm, hidden, context, up, narrow, hidden_up, inverse)


def local(
    queries,
    passages,
    hard_block_offsets,
    positive,
    context,
    residual,
    output_weight,
    adapter_down_weight,
    adapter_up_weight,
    final_norm_weight,
):
    device_count = lax.axis_size(PB_PA)
    block_count, hard_count = hard_block_offsets.shape
    query_count = queries.shape[0]
    block_rows = query_count // block_count
    capacity = 2 * block_count * hard_count // device_count
    slot_rows = capacity * block_rows
    all_rows = device_count * slot_rows
    passage_count = passages.shape[0]
    score_scale = inverse_temp / math.sqrt(MODEL_WIDTH)


    source = lax.axis_index(PB_PA)
    target = ((source + 1 + hard_block_offsets) % device_count).reshape(-1)
    order = jnp.arange(target.shape[0], dtype=jnp.int32)
    earlier = (target[:, None] == target[None, :]) & (order[:, None] > order[None, :])
    slot = target * capacity + jnp.sum(earlier.astype(jnp.int32), axis=1)
    slot_of = slot.reshape(block_count, hard_count).T
    key = jnp.repeat(slot_of, block_rows, axis=1) * block_rows + (
        jnp.arange(query_count, dtype=jnp.int32) % block_rows
    )
    row_ids = jnp.arange(all_rows, dtype=jnp.int32)
    picks = row_ids[:, None] == key[0][None, :]
    for t in range(1, hard_count):
        picks = picks | (row_ids[:, None] == key[t][None, :])
    outgoing = jnp.dot(picks.astype(bf16), queries, preferred_element_type=bf16)
    outgoing, first, second = lax.optimization_barrier(
        (outgoing, *weight_halves_sent(output_weight))
    )
    weight_rows = gather_input(first, second)
    arrived = exchange(outgoing.reshape(device_count, slot_rows, MODEL_WIDTH))
    arrived = arrived.reshape(-1, MODEL_WIDTH)

    half_weight = lax.all_gather(weight_rows, CHIPS, axis=0, tiled=True)
    near_scores = dot(queries, passages.T) * score_scale
    near_peak = jnp.max(near_scores, axis=1)
    near_exp = jnp.exp(near_scores - near_peak[:, None])
    near_sum = jnp.sum(near_exp, axis=1)
    near_mass = near_peak + jnp.log(near_sum)
    positive_hot = positive[:, None] == jnp.arange(passage_count, dtype=jnp.int32)[None, :]
    stacked = dot(
        jnp.concatenate([near_exp.astype(bf16), positive_hot.astype(bf16)], axis=0), passages
    )

    far_mean, far_scores, mix_parts, log_total, log_arrived = far_forward(
        arrived, passages, near_mass, key, device_count, score_scale
    )
    returned = exchange(far_mean.reshape(device_count, slot_rows, MODEL_WIDTH))
    returned = returned.reshape(-1, MODEL_WIDTH)
    log_total = log_total[:, 0]
    near_share = jnp.exp(near_mass - log_total)
    near_part = (near_share / near_sum)[:, None] * stacked[:query_count] - stacked[query_count:]

    product_dims = (((0,), (0,)), ((), ()))
    far_weight = jnp.exp(far_scores - log_arrived).astype(bf16)
    near_weight = (
        jnp.exp(near_scores - log_total[:, None]) - positive_hot.astype(f32)
    ).astype(bf16)
    far_grad = lax.dot_general(far_weight, arrived, product_dims, preferred_element_type=f32)
    near_grad = lax.dot_general(near_weight, queries, product_dims, preferred_element_type=f32)

    hidden_low, narrow, hidden_up, inverse_rms = layer_forward(
        context, half_weight, residual, adapter_down_weight.T, adapter_up_weight
    )
    grad_passages = loss_scale * score_scale * (far_grad + near_grad)

    returned, near_part, hidden_low, grad_passages = lax.optimization_barrier(
        (returned, near_part, hidden_low, grad_passages)
    )
    query_gradient, sums = tail(
        returned,
        mix_parts,
        near_part,
        final_norm_weight.astype(f32)[None, :],
        hidden_low,
        context,
        adapter_up_weight,
        narrow,
        hidden_up,
        inverse_rms,
        loss_scale * score_scale,
    )
    rank = narrow.shape[1]
    columns = MODEL_WIDTH // device_count
    return (
        query_gradient,
        grad_passages,
        sums[:rank, :columns].T,
        sums[rank:, :columns],
    )


def solution(mesh):
    torus = Mesh(mesh.devices.reshape(4, 2, 4, 4), PB_PA)
    in_specs = (
        P(PB_PA, None),
        P(PB_PA, None),
        P(PB_PA, None),
        P(PB_PA),
        P(PB_PA, None),
        P(PB_PA, None),
        P(PB_PA, None),
        P(),
        P(),
        P(),
    )
    out_specs = (P(PB_PA, None), P(PB_PA, None), P(PB_PA, None), P(None, PB_PA))
    return jax.shard_map(local, mesh=torus, in_specs=in_specs, out_specs=out_specs, check_vma=False)
```

```python
import functools
import math

import jax
import jax.numpy as jnp
from jax import lax
from jax.experimental import pallas as pl
from jax.experimental.pallas import tpu as pltpu
from jax.sharding import Mesh
from jax.sharding import PartitionSpec as P

MODEL_WIDTH = 3584
RERUN_QUERIES = 16
TQ = 32
SPLIT = 1024
PB_PA = ("pb_0", "pb_1", "pa_0", "pa_1")
CHIPS = ("pb_0", "pa_0", "pa_1")

inverse_temp = 2.0
loss_scale = 32.0
adapter_scale = 2.0
epsilon = 1e-06
absent_mass = 1e30
f32 = jnp.float32
bf16 = jnp.bfloat16
MESH = pl.DeviceIdType.MESH


def dot(a, b, **kw):
    return jnp.dot(a, b, preferred_element_type=f32, **kw)


def two_parts(x):
    high = x.astype(bf16)
    return high, (x - high.astype(f32)).astype(bf16)


def device_of(chip, core, per_plane):
    return (chip // per_plane) * 2 * per_plane + core * per_plane + chip % per_plane


def weight_halves_sent(rows):
    count = lax.axis_size(PB_PA)
    per_plane = lax.axis_size("pa_0") * lax.axis_size("pa_1")
    half = rows.shape[1] // 2
    left, right = rows[:, :half], rows[:, half:]
    odd = lax.axis_index("pa_1") % 2 == 1
    same = [(f, device_of(f // 2, f % 2, per_plane)) for f in range(count)]
    other = [(f, device_of(f // 2, 1 - f % 2, per_plane)) for f in range(count)]
    first = lax.ppermute(jnp.where(odd, right, left), PB_PA, same)
    second = lax.ppermute(jnp.where(odd, left, right), PB_PA, other)
    return first, second


def gather_input(first, second):
    core = lax.axis_index("pb_1")
    low = jnp.where(core == 0, first, second)
    high = jnp.where(core == 0, second, first)
    return jnp.concatenate([low, high], axis=0)


def exchange(array):
    return lax.all_to_all(array, PB_PA, split_axis=0, concat_axis=0, tiled=True)


def layer_forward_kernel(
    context, weight_a, weight_b, residual, down, up, hidden, narrow, hidden_up, inverse,
    own, other, own_sem, send_sem, recv_sem, squares,
):
    core = lax.axis_index("pb_1")
    twin = (lax.axis_index("pb_0"), 1 - core, lax.axis_index("pa_0"), lax.axis_index("pa_1"))
    tile = own.shape[2]
    tiles_a = weight_a.shape[1] // tile
    tiles_b = weight_b.shape[1] // tile
    half = weight_a.shape[1] + weight_b.shape[1]
    tiles = tiles_a + tiles_b
    barrier = pltpu.get_barrier_semaphore()
    pl.semaphore_signal(barrier, inc=1, device_id=twin, device_id_type=MESH)
    pl.semaphore_wait(barrier, 1)

    def tile_of(j):
        source, k = (weight_a, j) if j < tiles_a else (weight_b, j - tiles_a)
        return source.at[:, k * tile : (k + 1) * tile]

    def sent(j, source):
        return pltpu.make_async_remote_copy(
            source, other.at[j], send_sem.at[j], recv_sem.at[j],
            device_id=twin, device_id_type=MESH,
        )

    for j in range(tiles):
        pltpu.make_async_copy(tile_of(j), own.at[j], own_sem.at[j]).start()
        sent(j, tile_of(j)).start()
    low = lax.dot_general(
        context[...], down[...], (((1,), (1,)), ((), ())), preferred_element_type=f32
    ).astype(bf16)
    narrow[...] = low.astype(f32)
    squares[...] = jnp.zeros_like(squares)
    hidden_up[...] = jnp.zeros_like(hidden_up)

    def step(weight, start):
        at = pl.ds(pl.multiple_of(start, tile), tile)
        up_tile = up[:, at]
        value = (
            residual[:, at].astype(f32)
            + jnp.dot(context[...], weight, preferred_element_type=f32)
            + adapter_scale * jnp.dot(low, up_tile, preferred_element_type=f32)
        )
        squares[...] += jnp.sum(value * value, axis=1, keepdims=True)
        value = value.astype(bf16)
        hidden[:, at] = value
        hidden_up[...] += lax.dot_general(
            value, up_tile, (((1,), (1,)), ((), ())), preferred_element_type=f32
        )

    def own_step(j, carry):
        pltpu.make_async_copy(own.at[j], own.at[j], own_sem.at[j]).wait()
        step(own[j], core * half + j * tile)
        return carry

    lax.fori_loop(0, tiles, own_step, 0)

    def other_step(j, carry):
        sent(j, own.at[j]).wait_recv()
        step(other[j], (1 - core) * half + j * tile)
        return carry

    lax.fori_loop(0, tiles, other_step, 0)
    inverse[...] = lax.rsqrt(squares[...] / MODEL_WIDTH + epsilon)

    def done(j, carry):
        sent(j, own.at[j]).wait_send()
        return carry

    lax.fori_loop(0, tiles, done, 0)


def layer_forward(context, weight_a, weight_b, residual, down, up):
    tokens, width = context.shape
    half = weight_a.shape[1] + weight_b.shape[1]
    tile = 256
    tiles = half // tile
    rank = up.shape[0]
    vmem = pl.BlockSpec(memory_space=pltpu.VMEM)
    hbm = pl.BlockSpec(memory_space=pltpu.HBM)
    return pl.pallas_call(
        layer_forward_kernel,
        out_shape=(
            jax.ShapeDtypeStruct((tokens, width), bf16),
            jax.ShapeDtypeStruct((tokens, rank), f32),
            jax.ShapeDtypeStruct((tokens, rank), f32),
            jax.ShapeDtypeStruct((tokens, 1), f32),
        ),
        in_specs=[vmem, hbm, hbm, vmem, vmem, vmem],
        out_specs=(vmem, vmem, vmem, vmem),
        scratch_shapes=[
            pltpu.VMEM((tiles, width, tile), bf16),
            pltpu.VMEM((tiles, width, tile), bf16),
            pltpu.SemaphoreType.DMA((tiles,)),
            pltpu.SemaphoreType.DMA((tiles,)),
            pltpu.SemaphoreType.DMA((tiles,)),
            pltpu.VMEM((tokens, 1), f32),
        ],
        compiler_params=pltpu.CompilerParams(
            collective_id=1, has_side_effects=True, vmem_limit_bytes=58 * 1024 * 1024
        ),
        cost_estimate=pl.CostEstimate(flops=1000, bytes_accessed=1000, transcendentals=0),
        name="layer_forward",
    )(context, weight_a, weight_b, residual, down, up)


def torus_place():
    return tuple(lax.axis_index(axis) for axis in PB_PA)


def flat_of(place):
    return ((place[0] * 2 + place[1]) * 4 + place[2]) * 4 + place[3]


def torus_peer(place, j):
    return (
        lax.rem(place[0] + lax.rem(j, 4), 4),
        lax.rem(place[1] + j // 64, 2),
        lax.rem(place[2] + lax.rem(j // 4, 4), 4),
        lax.rem(place[3] + lax.rem(j // 16, 4), 4),
    )


def far_kernel(
    score_scale, arrived, passages_in, near_mass, key_column, mean, scores, mix, log_total,
    log_column, rows, passages, weights, inverse, means, mass, log_out, mass1, mass2, mass3, log1,
    log2, log3, row_sem, passage_sem, mean_sem, send_sem, recv_sem,
):
    place = torus_place()
    outer = place[0] * 2 + place[1]
    inner = place[2] * 4 + place[3]
    outers, inners, lanes = mass.shape
    peers = outers * inners
    query_count = near_mass.shape[0]
    hard_count = key_column.shape[0] // query_count
    all_rows, passage_count = scores.shape
    slot_rows = all_rows // peers
    width = passages.shape[1]
    chunks = row_sem.shape[0]
    block = all_rows // chunks
    exact = dict(precision=lax.Precision.HIGHEST, preferred_element_type=f32)

    def along_outer(d):
        to = lax.rem(outer + d, outers)
        return to, (to // 2, lax.rem(to, 2), place[2], place[3])

    def along_inner(d):
        to = lax.rem(inner + d, inners)
        return to, (place[0], place[1], to // 4, lax.rem(to, 4))

    def part(c):
        return pl.ds(pl.multiple_of(c * block, block), block)

    def came_in(c):
        return pltpu.make_async_copy(arrived.at[part(c)], rows.at[part(c)], row_sem.at[c])

    def went_out(c):
        return pltpu.make_async_copy(means.at[part(c)], mean.at[part(c)], mean_sem.at[c])

    passages_here = pltpu.make_async_copy(passages_in, passages, passage_sem)
    passages_here.start()
    for c in range(chunks):
        came_in(c).start()
    barrier = pltpu.get_barrier_semaphore()
    for d in range(1, outers):
        pl.semaphore_signal(barrier, inc=1, device_id=along_outer(d)[1], device_id_type=MESH)
    for d in range(1, inners):
        pl.semaphore_signal(barrier, inc=1, device_id=along_inner(d)[1], device_id_type=MESH)
    passages_here.wait()
    lane_ids = lax.broadcasted_iota(jnp.int32, (block, lanes), 1)
    slot_ids = lax.rem(lax.broadcasted_iota(jnp.int32, (block, lanes), 0), slot_rows)
    block_peers = block // slot_rows
    peer_ids = lax.broadcasted_iota(jnp.int32, (block_peers, block), 0)
    peer_rows = lax.broadcasted_iota(jnp.int32, (block_peers, block), 1) // slot_rows
    gather_rows = jnp.where(peer_ids == peer_rows, 1.0, 0.0)

    def score(c, carry):
        came_in(c).wait()
        value = score_scale * lax.dot_general(
            rows[part(c), :], passages[...], (((1,), (1,)), ((), ())),
            preferred_element_type=f32,
        )
        scores[part(c), :] = value
        peak = jnp.max(value, axis=1, keepdims=True)
        weight = jnp.exp(value - peak)
        total = jnp.sum(weight, axis=1, keepdims=True)
        weights[part(c), :] = weight.astype(bf16)
        inverse[part(c), :] = 1.0 / total
        spread = jnp.where(lane_ids == slot_ids, peak + jnp.log(total), 0.0)
        compact = jnp.dot(gather_rows, spread, **exact)
        step = block_peers // inners
        mass[pl.ds(c * step, step)] = compact.reshape(step, inners, lanes)
        return carry

    lax.fori_loop(0, chunks, score, 0)
    pl.semaphore_wait(barrier, outers - 1 + inners - 1)

    def hop1(source, target, which):
        for d in range(1, outers):
            to, device = along_outer(d)
            pltpu.make_async_remote_copy(
                source.at[to], target.at[outer], send_sem.at[which], recv_sem.at[which],
                device_id=device, device_id_type=MESH,
            ).start()
        target[outer] = source[outer]

    def hop2(source, target, which):
        for d in range(1, inners):
            to, device = along_inner(d)
            pltpu.make_async_remote_copy(
                source.at[to], target.at[inner], send_sem.at[which], recv_sem.at[which],
                device_id=device, device_id_type=MESH,
            ).start()
        target[inner] = source[inner]

    def others(source, target, which):
        rest = pl.ds(0, source.shape[0] - 1)
        return pltpu.make_async_remote_copy(
            source.at[rest], target.at[rest], send_sem.at[which], recv_sem.at[which],
            device_id=along_outer(1)[1], device_id_type=MESH,
        )

    def repack(source, target):
        for r in range(inners):
            target[r] = source[:, r, :]

    def average(c, carry):
        weight = weights[part(c), :]
        scale = inverse[part(c), :]
        tile = 512
        for start in range(0, width, tile):
            value = jnp.dot(
                weight, passages[:, start : start + tile], preferred_element_type=f32
            )
            means[part(c), start : start + tile] = (value * scale).astype(bf16)
        went_out(c).start()
        return carry

    hop1(mass, mass1, 0)
    lax.fori_loop(0, chunks // 2, average, 0)
    others(mass, mass1, 0).wait_recv()
    repack(mass1, mass2)
    hop2(mass2, mass3, 1)
    lax.fori_loop(chunks // 2, chunks, average, 0)

    key = key_column[...]
    peer = key // slot_rows
    slot = lax.rem(key, slot_rows)
    pairs = key.shape[0]
    ids = lax.broadcasted_iota(jnp.int32, (pairs, peers), 1)
    at_slot = lax.broadcasted_iota(jnp.int32, (pairs, lanes), 1) == slot
    to_peer = jnp.where(ids == peer, 1.0, 0.0)
    from_peer = jnp.where(ids == lax.rem(peer, inners) * outers + peer // inners, 1.0, 0.0)
    others(mass2, mass3, 1).wait_recv()
    came = jnp.dot(from_peer, mass3[...].reshape(peers, lanes), **exact)
    came = jnp.sum(jnp.where(at_slot, came, 0.0), axis=1, keepdims=True)
    masses = [near_mass[...]] + [
        came[t * query_count : (t + 1) * query_count] for t in range(hard_count)
    ]
    peak = masses[0]
    for value in masses[1:]:
        peak = jnp.maximum(peak, value)
    total = jnp.exp(masses[0] - peak)
    for value in masses[1:]:
        total = total + jnp.exp(value - peak)
    log_value = peak + jnp.log(total)
    log_total[...] = log_value
    log_pairs = jnp.concatenate([log_value] * hard_count, axis=0)
    over_pairs = (((0,), (0,)), ((), ()))
    outgoing = lax.dot_general(to_peer, jnp.where(at_slot, log_pairs, 0.0), over_pairs, **exact)
    filled = lax.dot_general(to_peer, jnp.where(at_slot, 1.0, 0.0), over_pairs, **exact)
    outgoing = jnp.where(filled > 0.5, outgoing, absent_mass)
    log_out[...] = outgoing.reshape(log_out.shape)
    hop1(log_out, log1, 2)
    row_ids = lax.broadcasted_iota(jnp.int32, (query_count, all_rows), 1)
    shares = jnp.zeros((query_count, all_rows), f32)
    for t in range(hard_count):
        hit = key[t * query_count : (t + 1) * query_count] == row_ids
        shares = jnp.where(hit, jnp.exp(masses[1 + t] - log_value), shares)
    high = shares.astype(bf16)
    mix[:query_count, :] = high
    mix[query_count:, :] = (shares - high.astype(f32)).astype(bf16)
    others(log_out, log1, 2).wait_recv()
    repack(log1, log2)
    hop2(log2, log3, 3)
    row = lax.broadcasted_iota(jnp.int32, (all_rows, peers), 0)
    row_peer = row // slot_rows
    back = lax.rem(row_peer, inners) * outers + row_peer // inners
    spread = jnp.where(
        lax.broadcasted_iota(jnp.int32, (all_rows, peers), 1) == back, 1.0, 0.0
    )
    mine = lax.broadcasted_iota(jnp.int32, (all_rows, lanes), 1) == lax.rem(
        lax.broadcasted_iota(jnp.int32, (all_rows, lanes), 0), slot_rows
    )
    for c in range(chunks):
        went_out(c).wait()
    others(mass, mass1, 0).wait_send()
    others(mass2, mass3, 1).wait_send()
    others(log_out, log1, 2).wait_send()
    others(log2, log3, 3).wait_recv()
    logs = jnp.dot(spread, log3[...].reshape(peers, lanes), **exact)
    log_column[...] = jnp.sum(jnp.where(mine, logs, 0.0), axis=1, keepdims=True)
    others(log2, log3, 3).wait_send()


def far_forward(arrived, passages, near_mass, key, peers, score_scale):
    all_rows, width = arrived.shape
    passage_count = passages.shape[0]
    hard_count, query_count = key.shape
    lanes, chunks, outers = 128, 4, 8
    inners = peers // outers
    by_outer = pltpu.VMEM((outers, inners, lanes), f32)
    by_inner = pltpu.VMEM((inners, outers, lanes), f32)
    vmem = pl.BlockSpec(memory_space=pltpu.VMEM)
    hbm = pl.BlockSpec(memory_space=pltpu.HBM)
    dma = pltpu.SemaphoreType.DMA
    return pl.pallas_call(
        functools.partial(far_kernel, score_scale),
        out_shape=(
            jax.ShapeDtypeStruct((all_rows, width), bf16),
            jax.ShapeDtypeStruct((all_rows, passage_count), f32),
            jax.ShapeDtypeStruct((2 * query_count, all_rows), bf16),
            jax.ShapeDtypeStruct((query_count, 1), f32),
            jax.ShapeDtypeStruct((all_rows, 1), f32),
        ),
        in_specs=[hbm, hbm, vmem, vmem],
        out_specs=(hbm, vmem, vmem, vmem, vmem),
        scratch_shapes=[
            pltpu.VMEM((all_rows, width), bf16),
            pltpu.VMEM((passage_count, width), bf16),
            pltpu.VMEM((all_rows, passage_count), bf16),
            pltpu.VMEM((all_rows, 1), f32),
            pltpu.VMEM((all_rows, width), bf16),
            by_outer,
            by_outer,
            by_outer,
            by_inner,
            by_inner,
            by_outer,
            by_inner,
            by_inner,
            dma((chunks,)),
            dma(()),
            dma((chunks,)),
            dma((4,)),
            dma((4,)),
        ],
        compiler_params=pltpu.CompilerParams(
            collective_id=2, has_side_effects=True, vmem_limit_bytes=58 * 1024 * 1024
        ),
        name="far_forward",
    )(arrived, passages, near_mass[:, None], key.reshape(-1)[:, None])


def tail_kernel(
    gradient_scale, returned, mix, near_part, norm, hidden, context, up, narrow, hidden_up, inverse,
    gradient, piece, rows, hid, ctx, grad, scaled, products, scaled_up, terms, first, part, second,
    row_sem, hid_sem, ctx_sem, grad_sem, send1, recv1, send2, recv2,
):
    place = torus_place()
    own = flat_of(place)
    lane_group = place[3]
    column = own // 4
    tiles = row_sem.shape[0]
    width = terms.shape[2] * terms.shape[0]
    tile = width // tiles
    lanes = terms.shape[2]
    count = terms.shape[0]
    columns = first.shape[0]
    per_tile = tile // lanes
    query_count = gradient.shape[0]
    rerun = scaled.shape[0]
    rank = up.shape[0]
    tokens = narrow.shape[0]
    exact = dict(precision=lax.Precision.HIGHEST, preferred_element_type=f32)
    over_rows = (((0,), (0,)), ((), ()))
    over_lanes = (((1,), (1,)), ((), ()))

    def at(j):
        return pl.ds(pl.multiple_of(j * tile, tile), tile)

    def came_in(j):
        return pltpu.make_async_copy(returned.at[:, at(j)], rows.at[:, at(j)], row_sem.at[j])

    hid_in = pltpu.make_async_copy(hidden, hid, hid_sem)
    ctx_in = pltpu.make_async_copy(context, ctx, ctx_sem)
    came_in(0).start()
    hid_in.start()
    for j in range(1, tiles):
        came_in(j).start()
    ctx_in.start()
    barrier = pltpu.get_barrier_semaphore()

    gathers = column < count
    base = (lanes * column) // 28
    last = (lanes * column + lanes - 1) // 28
    tile0 = (28 * own) // lanes
    tile1 = (28 * own + 27) // lanes

    def of_column(j, b):
        return (j // 8, lax.rem(j // 4, 2), lax.rem(j, 4), b)

    def greet(d, carry):
        to = of_column(lax.rem(column + d, columns), lane_group)
        pl.semaphore_signal(barrier, inc=1, device_id=to, device_id_type=MESH)
        return carry

    lax.fori_loop(1, columns, greet, 0)
    for slot in range(2):
        for b in range(4):
            @pl.when((tile0 + slot <= tile1) & ((tile0 + slot != column) | (lane_group != b)))
            def _():
                to = of_column(tile0 + slot, b)
                pl.semaphore_signal(barrier, inc=1, device_id=to, device_id_type=MESH)

    products[...] = jnp.zeros_like(products)
    scaled_up[...] = jnp.zeros_like(scaled_up)
    hid_in.wait()

    def mixing(j, carry):
        came_in(j).wait()
        both = jnp.dot(mix[...], rows[:, at(j)], preferred_element_type=f32)
        value = gradient_scale * (both[:query_count] + both[query_count:] + near_part[:, at(j)])
        grad[:, at(j)] = value
        spread = norm[:, at(j)] * (value[:rerun] / TQ)
        scaled[:, at(j)] = spread
        products[...] += lax.dot_general(
            hid[:, at(j)], spread.astype(bf16), over_lanes, preferred_element_type=f32
        )
        scaled_up[...] += lax.dot_general(spread, up[:, at(j)].astype(f32), over_lanes, **exact)
        return carry

    lax.fori_loop(0, tiles, mixing, 0)
    gradient_out = pltpu.make_async_copy(grad, gradient, grad_sem)
    gradient_out.start()

    token_query = lax.broadcasted_iota(jnp.int32, (tokens, rerun), 0) // TQ
    of_query = token_query == lax.broadcasted_iota(jnp.int32, (tokens, rerun), 1)
    hot = jnp.where(of_query, 1.0, 0.0)
    mean = jnp.sum(jnp.where(of_query, products[...], 0.0), axis=1, keepdims=True) / width
    rms = inverse[...]
    slope = rms * rms * rms * mean
    spread_up = jnp.dot(hot, scaled_up[...], **exact)
    grad_narrow = (adapter_scale * (rms * spread_up - slope * hidden_up[...])).astype(bf16)
    weighted = (slope * narrow[...]).astype(bf16)
    sums = lax.dot_general(hot, rms * narrow[...], over_rows, **exact)
    ctx_in.wait()

    def products_of(j, carry):
        down = lax.dot_general(
            grad_narrow, ctx[:, at(j)], over_rows, preferred_element_type=f32
        ) / RERUN_QUERIES
        up_part = (adapter_scale / RERUN_QUERIES) * (
            lax.dot_general(sums, scaled[:, at(j)], over_rows, **exact)
            - lax.dot_general(weighted, hid[:, at(j)], over_rows, preferred_element_type=f32)
        )
        for k in range(per_tile):
            terms[j * per_tile + k, :rank, :] = down[:, k * lanes : (k + 1) * lanes]
            terms[j * per_tile + k, rank:, :] = up_part[:, k * lanes : (k + 1) * lanes]
        return carry

    lax.fori_loop(0, tiles, products_of, 0)
    inside = jnp.where((base <= own) & (own <= last), 1, 0)
    pl.semaphore_wait(barrier, columns - 1 + jnp.where(gathers, last - base + 1 - inside, 0))

    def stage1(j):
        to = (j // 8, lax.rem(j // 4, 2), lax.rem(j, 4), lane_group)
        return pltpu.make_async_remote_copy(
            terms.at[j], first.at[column], send1, recv1, device_id=to, device_id_type=MESH
        )

    def start1(j, carry):
        @pl.when(j != column)
        def _():
            stage1(j).start()

        return carry

    lax.fori_loop(0, count, start1, 0)

    def sized(buffer, n, send_sem, recv_sem):
        piece_of = buffer.at[pl.ds(0, n)]
        return pltpu.make_async_remote_copy(
            piece_of, piece_of, send_sem, recv_sem,
            device_id=torus_peer(place, 1), device_id_type=MESH,
        )

    @pl.when(tile0 == tile1)
    def _():
        second[1] = jnp.zeros(second.shape[1:], f32)

    def stage2(i):
        e = base + i
        slot = column - (28 * e) // lanes
        to = (e // 32, lax.rem(e // 16, 2), lax.rem(e // 4, 4), lax.rem(e, 4))
        return pltpu.make_async_remote_copy(
            part, second.at[slot, lane_group], send2.at[i], recv2.at[slot, lane_group],
            device_id=to, device_id_type=MESH,
        )

    @pl.when(gathers)
    def _():
        first[column] = terms[column]
        sized(first, columns - 1, send1, recv1).wait_recv()
        part[...] = jnp.sum(first[...], axis=0)
        for i in range(6):
            e = base + i

            @pl.when((e <= last) & (e != own))
            def _():
                stage2(i).start()

            @pl.when((e <= last) & (e == own))
            def _():
                second[column - tile0, lane_group] = part[...]

        sized(terms, count - 1, send1, recv1).wait_send()

    @pl.when(column >= count)
    def _():
        sized(terms, count, send1, recv1).wait_send()

    for slot in range(2):
        from_tile = tile0 + slot
        for b in range(4):
            @pl.when((from_tile <= tile1) & ((from_tile != column) | (lane_group != b)))
            def _():
                pltpu.make_async_remote_copy(
                    part, second.at[slot, b], send2.at[0], recv2.at[slot, b],
                    device_id=torus_peer(place, 1), device_id_type=MESH,
                ).wait_recv()

    left = jnp.sum(second[0], axis=0)
    right = jnp.sum(second[1], axis=0)
    offset = 28 * own - lanes * tile0
    source = lax.broadcasted_iota(jnp.int32, (lanes, lanes), 0)
    target = lax.broadcasted_iota(jnp.int32, (lanes, lanes), 1) + offset
    piece[...] = jnp.dot(left, jnp.where(source == target, 1.0, 0.0), **exact) + jnp.dot(
        right, jnp.where(source + lanes == target, 1.0, 0.0), **exact
    )

    @pl.when(gathers)
    def _():
        for i in range(6):
            e = base + i

            @pl.when((e <= last) & (e != own))
            def _():
                stage2(i).wait_send()

    gradient_out.wait()


def tail(returned, mix, near_part, norm, hidden, context, up, narrow, hidden_up, inverse, scale):
    all_rows, width = returned.shape
    query_count = near_part.shape[0]
    tokens, rank = narrow.shape
    tiles, lanes, rerun = 7, 128, RERUN_QUERIES
    vmem = pl.BlockSpec(memory_space=pltpu.VMEM)
    hbm = pl.BlockSpec(memory_space=pltpu.HBM)
    dma = pltpu.SemaphoreType.DMA
    return pl.pallas_call(
        functools.partial(tail_kernel, scale),
        out_shape=(
            jax.ShapeDtypeStruct((query_count, width), f32),
            jax.ShapeDtypeStruct((2 * rank, lanes), f32),
        ),
        in_specs=[hbm, vmem, vmem, vmem, hbm, hbm, vmem, vmem, vmem, vmem],
        out_specs=(hbm, vmem),
        scratch_shapes=[
            pltpu.VMEM((all_rows, width), bf16),
            pltpu.VMEM((tokens, width), bf16),
            pltpu.VMEM((tokens, width), bf16),
            pltpu.VMEM((query_count, width), f32),
            pltpu.VMEM((rerun, width), f32),
            pltpu.VMEM((tokens, rerun), f32),
            pltpu.VMEM((rerun, rank), f32),
            pltpu.VMEM((width // lanes, 2 * rank, lanes), f32),
            pltpu.VMEM((32, 2 * rank, lanes), f32),
            pltpu.VMEM((2 * rank, lanes), f32),
            pltpu.VMEM((2, 4, 2 * rank, lanes), f32),
            dma((tiles,)),
            dma(()),
            dma(()),
            dma(()),
            dma(()),
            dma(()),
            dma((6,)),
            dma((2, 4)),
        ],
        compiler_params=pltpu.CompilerParams(
            collective_id=3, has_side_effects=True, vmem_limit_bytes=58 * 1024 * 1024
        ),
        name="tail",
    )(returned, mix, near_part, norm, hidden, context, up, narrow, hidden_up, inverse)


def local(
    queries,
    passages,
    hard_block_offsets,
    positive,
    context,
    residual,
    output_weight,
    adapter_down_weight,
    adapter_up_weight,
    final_norm_weight,
):
    device_count = lax.axis_size(PB_PA)
    block_count, hard_count = hard_block_offsets.shape
    query_count = queries.shape[0]
    block_rows = query_count // block_count
    capacity = 2 * block_count * hard_count // device_count
    slot_rows = capacity * block_rows
    all_rows = device_count * slot_rows
    passage_count = passages.shape[0]
    score_scale = inverse_temp / math.sqrt(MODEL_WIDTH)


    source = lax.axis_index(PB_PA)
    target = ((source + 1 + hard_block_offsets) % device_count).reshape(-1)
    order = jnp.arange(target.shape[0], dtype=jnp.int32)
    earlier = (target[:, None] == target[None, :]) & (order[:, None] > order[None, :])
    slot = target * capacity + jnp.sum(earlier.astype(jnp.int32), axis=1)
    slot_of = slot.reshape(block_count, hard_count).T
    key = jnp.repeat(slot_of, block_rows, axis=1) * block_rows + (
        jnp.arange(query_count, dtype=jnp.int32) % block_rows
    )
    row_ids = jnp.arange(all_rows, dtype=jnp.int32)
    picks = row_ids[:, None] == key[0][None, :]
    for t in range(1, hard_count):
        picks = picks | (row_ids[:, None] == key[t][None, :])
    outgoing = jnp.dot(picks.astype(bf16), queries, preferred_element_type=bf16)
    outgoing, first, second = lax.optimization_barrier(
        (outgoing, *weight_halves_sent(output_weight))
    )
    weight_rows = gather_input(first, second)
    arrived = exchange(outgoing.reshape(device_count, slot_rows, MODEL_WIDTH))
    arrived = arrived.reshape(-1, MODEL_WIDTH)

    weight_a = lax.all_gather(weight_rows[:, :SPLIT], CHIPS, axis=0, tiled=True)
    weight_b = lax.all_gather(weight_rows[:, SPLIT:], CHIPS, axis=0, tiled=True)
    near_scores = dot(queries, passages.T) * score_scale
    near_peak = jnp.max(near_scores, axis=1)
    near_exp = jnp.exp(near_scores - near_peak[:, None])
    near_sum = jnp.sum(near_exp, axis=1)
    near_mass = near_peak + jnp.log(near_sum)
    positive_hot = positive[:, None] == jnp.arange(passage_count, dtype=jnp.int32)[None, :]
    stacked = dot(
        jnp.concatenate([near_exp.astype(bf16), positive_hot.astype(bf16)], axis=0), passages
    )

    far_mean, far_scores, mix_parts, log_total, log_arrived = far_forward(
        arrived, passages, near_mass, key, device_count, score_scale
    )
    returned = exchange(far_mean.reshape(device_count, slot_rows, MODEL_WIDTH))
    returned = returned.reshape(-1, MODEL_WIDTH)
    log_total = log_total[:, 0]
    near_share = jnp.exp(near_mass - log_total)
    near_part = (near_share / near_sum)[:, None] * stacked[:query_count] - stacked[query_count:]

    product_dims = (((0,), (0,)), ((), ()))
    far_weight = jnp.exp(far_scores - log_arrived).astype(bf16)
    near_weight = (
        jnp.exp(near_scores - log_total[:, None]) - positive_hot.astype(f32)
    ).astype(bf16)
    far_grad = lax.dot_general(far_weight, arrived, product_dims, preferred_element_type=f32)
    near_grad = lax.dot_general(near_weight, queries, product_dims, preferred_element_type=f32)

    hidden_low, narrow, hidden_up, inverse_rms = layer_forward(
        context, weight_a, weight_b, residual, adapter_down_weight.T, adapter_up_weight
    )
    grad_passages = loss_scale * score_scale * (far_grad + near_grad)

    returned, near_part, hidden_low, grad_passages = lax.optimization_barrier(
        (returned, near_part, hidden_low, grad_passages)
    )
    query_gradient, sums = tail(
        returned,
        mix_parts,
        near_part,
        final_norm_weight.astype(f32)[None, :],
        hidden_low,
        context,
        adapter_up_weight,
        narrow,
        hidden_up,
        inverse_rms,
        loss_scale * score_scale,
    )
    rank = narrow.shape[1]
    columns = MODEL_WIDTH // device_count
    return (
        query_gradient,
        grad_passages,
        sums[:rank, :columns].T,
        sums[rank:, :columns],
    )


def solution(mesh):
    torus = Mesh(mesh.devices.reshape(4, 2, 4, 4), PB_PA)
    in_specs = (
        P(PB_PA, None),
        P(PB_PA, None),
        P(PB_PA, None),
        P(PB_PA),
        P(PB_PA, None),
        P(PB_PA, None),
        P(PB_PA, None),
        P(),
        P(),
        P(),
    )
    out_specs = (P(PB_PA, None), P(PB_PA, None), P(PB_PA, None), P(None, PB_PA))
    return jax.shard_map(local, mesh=torus, in_specs=in_specs, out_specs=out_specs, check_vma=False)
```

```python
import functools
import math

import jax
import jax.numpy as jnp
from jax import lax
from jax.experimental import pallas as pl
from jax.experimental.pallas import tpu as pltpu
from jax.sharding import Mesh
from jax.sharding import PartitionSpec as P

MODEL_WIDTH = 3584
RERUN_QUERIES = 16
TQ = 32
PB_PA = ("pb_0", "pb_1", "pa_0", "pa_1")
CHIPS = ("pb_0", "pa_0", "pa_1")

inverse_temp = 2.0
loss_scale = 32.0
adapter_scale = 2.0
epsilon = 1e-06
absent_mass = 1e30
f32 = jnp.float32
bf16 = jnp.bfloat16
MESH = pl.DeviceIdType.MESH


def dot(a, b, **kw):
    return jnp.dot(a, b, preferred_element_type=f32, **kw)


def two_parts(x):
    high = x.astype(bf16)
    return high, (x - high.astype(f32)).astype(bf16)


def device_of(chip, core, per_plane):
    return (chip // per_plane) * 2 * per_plane + core * per_plane + chip % per_plane


def weight_halves_sent(rows):
    count = lax.axis_size(PB_PA)
    per_plane = lax.axis_size("pa_0") * lax.axis_size("pa_1")
    half = rows.shape[1] // 2
    left, right = rows[:, :half], rows[:, half:]
    odd = lax.axis_index("pa_1") % 2 == 1
    same = [(f, device_of(f // 2, f % 2, per_plane)) for f in range(count)]
    other = [(f, device_of(f // 2, 1 - f % 2, per_plane)) for f in range(count)]
    first = lax.ppermute(jnp.where(odd, right, left), PB_PA, same)
    second = lax.ppermute(jnp.where(odd, left, right), PB_PA, other)
    return first, second


def gather_input(first, second):
    core = lax.axis_index("pb_1")
    low = jnp.where(core == 0, first, second)
    high = jnp.where(core == 0, second, first)
    return jnp.concatenate([low, high], axis=0)


def exchange(array):
    return lax.all_to_all(array, PB_PA, split_axis=0, concat_axis=0, tiled=True)


def layer_forward_kernel(
    context, half_weight, residual, down, up, hidden, narrow, hidden_up, inverse,
    own, other, block, own_sem, send_sem, recv_sem, out_sem, squares,
):
    core = lax.axis_index("pb_1")
    twin = (lax.axis_index("pb_0"), 1 - core, lax.axis_index("pa_0"), lax.axis_index("pa_1"))
    tile = own.shape[2]
    half = half_weight.shape[1]
    tiles = half // tile
    barrier = pltpu.get_barrier_semaphore()
    pl.semaphore_signal(barrier, inc=1, device_id=twin, device_id_type=MESH)
    pl.semaphore_wait(barrier, 1)

    def columns(j):
        return pl.ds(pl.multiple_of(j * tile, tile), tile)

    def sent(j):
        return pltpu.make_async_remote_copy(
            half_weight.at[:, columns(j)], other.at[j], send_sem.at[j], recv_sem.at[j],
            device_id=twin, device_id_type=MESH,
        )

    def fetched(j):
        return pltpu.make_async_copy(
            half_weight.at[:, columns(j)], own.at[lax.rem(j, 2)], own_sem.at[lax.rem(j, 2)]
        )

    fetched(0).start()

    def send(j, carry):
        sent(j).start()
        return carry

    lax.fori_loop(0, tiles, send, 0)
    low = lax.dot_general(
        context[...], down[...], (((1,), (1,)), ((), ())), preferred_element_type=f32
    ).astype(bf16)
    narrow[...] = low.astype(f32)
    squares[...] = jnp.zeros_like(squares)
    hidden_up[...] = jnp.zeros_like(hidden_up)

    def stored(columns, k):
        return pltpu.make_async_copy(
            block.at[:, columns], hidden.at[:, columns], out_sem.at[k]
        )

    def step(weight, start, k):
        at = pl.ds(pl.multiple_of(start, tile), tile)
        up_tile = up[:, at]
        value = (
            residual[:, at].astype(f32)
            + jnp.dot(context[...], weight, preferred_element_type=f32)
            + adapter_scale * jnp.dot(low, up_tile, preferred_element_type=f32)
        )
        squares[...] += jnp.sum(value * value, axis=1, keepdims=True)
        value = value.astype(bf16)
        block[:, at] = value
        stored(at, k).start()
        hidden_up[...] += lax.dot_general(
            value, up_tile, (((1,), (1,)), ((), ())), preferred_element_type=f32
        )

    def own_step(j, carry):
        fetched(j).wait()

        @pl.when(j + 1 < tiles)
        def _():
            fetched(j + 1).start()

        step(own[lax.rem(j, 2)], core * half + j * tile, j)
        return carry

    lax.fori_loop(0, tiles, own_step, 0)

    def other_step(j, carry):
        sent(j).wait_recv()
        step(other[j], (1 - core) * half + j * tile, tiles + j)
        return carry

    lax.fori_loop(0, tiles, other_step, 0)
    inverse[...] = lax.rsqrt(squares[...] / MODEL_WIDTH + epsilon)

    def done(j, carry):
        sent(j).wait_send()
        stored(columns(j), j).wait()
        stored(columns(j), tiles + j).wait()
        return carry

    lax.fori_loop(0, tiles, done, 0)


def layer_forward(context, half_weight, residual, down, up):
    tokens, width = context.shape
    half = half_weight.shape[1]
    tile = 256
    tiles = half // tile
    rank = up.shape[0]
    vmem = pl.BlockSpec(memory_space=pltpu.VMEM)
    return pl.pallas_call(
        layer_forward_kernel,
        out_shape=(
            jax.ShapeDtypeStruct((tokens, width), bf16),
            jax.ShapeDtypeStruct((tokens, rank), f32),
            jax.ShapeDtypeStruct((tokens, rank), f32),
            jax.ShapeDtypeStruct((tokens, 1), f32),
        ),
        in_specs=[vmem, pl.BlockSpec(memory_space=pl.ANY), vmem, vmem, vmem],
        out_specs=(pl.BlockSpec(memory_space=pltpu.HBM), vmem, vmem, vmem),
        scratch_shapes=[
            pltpu.VMEM((2, width, tile), bf16),
            pltpu.VMEM((tiles, width, tile), bf16),
            pltpu.VMEM((tokens, width), bf16),
            pltpu.SemaphoreType.DMA((2,)),
            pltpu.SemaphoreType.DMA((tiles,)),
            pltpu.SemaphoreType.DMA((tiles,)),
            pltpu.SemaphoreType.DMA((2 * tiles,)),
            pltpu.VMEM((tokens, 1), f32),
        ],
        compiler_params=pltpu.CompilerParams(
            collective_id=1, has_side_effects=True, vmem_limit_bytes=58 * 1024 * 1024
        ),
        cost_estimate=pl.CostEstimate(flops=1000, bytes_accessed=1000, transcendentals=0),
        name="layer_forward",
    )(context, half_weight, residual, down, up)


def torus_place():
    return tuple(lax.axis_index(axis) for axis in PB_PA)


def flat_of(place):
    return ((place[0] * 2 + place[1]) * 4 + place[2]) * 4 + place[3]


def torus_peer(place, j):
    return (
        lax.rem(place[0] + lax.rem(j, 4), 4),
        lax.rem(place[1] + j // 64, 2),
        lax.rem(place[2] + lax.rem(j // 4, 4), 4),
        lax.rem(place[3] + lax.rem(j // 16, 4), 4),
    )


def far_kernel(
    score_scale, arrived, passages_in, near_mass, key_column, mean, scores_out, mix_out, log_total,
    log_column, scores, mix, score_sem, mix_sem, rows, passages, weights, inverse, means, mass, log_out, mass1, mass2, mass3, log1,
    log2, log3, row_sem, passage_sem, mean_sem, send_sem, recv_sem,
):
    place = torus_place()
    outer = place[0] * 2 + place[1]
    inner = place[2] * 4 + place[3]
    outers, inners, lanes = mass.shape
    peers = outers * inners
    query_count = near_mass.shape[0]
    hard_count = key_column.shape[0] // query_count
    all_rows, passage_count = scores.shape
    slot_rows = all_rows // peers
    width = passages.shape[1]
    chunks = row_sem.shape[0]
    block = all_rows // chunks
    exact = dict(precision=lax.Precision.HIGHEST, preferred_element_type=f32)

    def along_outer(d):
        to = lax.rem(outer + d, outers)
        return to, (to // 2, lax.rem(to, 2), place[2], place[3])

    def along_inner(d):
        to = lax.rem(inner + d, inners)
        return to, (place[0], place[1], to // 4, lax.rem(to, 4))

    def part(c):
        return pl.ds(pl.multiple_of(c * block, block), block)

    def came_in(c):
        return pltpu.make_async_copy(arrived.at[part(c)], rows.at[part(c)], row_sem.at[c])

    def went_out(c):
        return pltpu.make_async_copy(means.at[part(c)], mean.at[part(c)], mean_sem.at[c])

    def scores_stored(c):
        return pltpu.make_async_copy(
            scores.at[part(c)], scores_out.at[part(c)], score_sem.at[c]
        )

    mix_stored = pltpu.make_async_copy(mix, mix_out, mix_sem)
    passages_here = pltpu.make_async_copy(passages_in, passages, passage_sem)
    passages_here.start()
    for c in range(chunks):
        came_in(c).start()
    barrier = pltpu.get_barrier_semaphore()
    for d in range(1, outers):
        pl.semaphore_signal(barrier, inc=1, device_id=along_outer(d)[1], device_id_type=MESH)
    for d in range(1, inners):
        pl.semaphore_signal(barrier, inc=1, device_id=along_inner(d)[1], device_id_type=MESH)
    passages_here.wait()
    lane_ids = lax.broadcasted_iota(jnp.int32, (block, lanes), 1)
    slot_ids = lax.rem(lax.broadcasted_iota(jnp.int32, (block, lanes), 0), slot_rows)
    block_peers = block // slot_rows
    peer_ids = lax.broadcasted_iota(jnp.int32, (block_peers, block), 0)
    peer_rows = lax.broadcasted_iota(jnp.int32, (block_peers, block), 1) // slot_rows
    gather_rows = jnp.where(peer_ids == peer_rows, 1.0, 0.0)

    def score(c, carry):
        came_in(c).wait()
        value = score_scale * lax.dot_general(
            rows[part(c), :], passages[...], (((1,), (1,)), ((), ())),
            preferred_element_type=f32,
        )
        scores[part(c), :] = value
        scores_stored(c).start()
        peak = jnp.max(value, axis=1, keepdims=True)
        weight = jnp.exp(value - peak)
        total = jnp.sum(weight, axis=1, keepdims=True)
        weights[part(c), :] = weight.astype(bf16)
        inverse[part(c), :] = 1.0 / total
        spread = jnp.where(lane_ids == slot_ids, peak + jnp.log(total), 0.0)
        compact = jnp.dot(gather_rows, spread, **exact)
        step = block_peers // inners
        mass[pl.ds(c * step, step)] = compact.reshape(step, inners, lanes)
        return carry

    lax.fori_loop(0, chunks, score, 0)
    pl.semaphore_wait(barrier, outers - 1 + inners - 1)

    def hop1(source, target, which):
        for d in range(1, outers):
            to, device = along_outer(d)
            pltpu.make_async_remote_copy(
                source.at[to], target.at[outer], send_sem.at[which], recv_sem.at[which],
                device_id=device, device_id_type=MESH,
            ).start()
        target[outer] = source[outer]

    def hop2(source, target, which):
        for d in range(1, inners):
            to, device = along_inner(d)
            pltpu.make_async_remote_copy(
                source.at[to], target.at[inner], send_sem.at[which], recv_sem.at[which],
                device_id=device, device_id_type=MESH,
            ).start()
        target[inner] = source[inner]

    def others(source, target, which):
        rest = pl.ds(0, source.shape[0] - 1)
        return pltpu.make_async_remote_copy(
            source.at[rest], target.at[rest], send_sem.at[which], recv_sem.at[which],
            device_id=along_outer(1)[1], device_id_type=MESH,
        )

    def repack(source, target):
        for r in range(inners):
            target[r] = source[:, r, :]

    def average(c, carry):
        weight = weights[part(c), :]
        scale = inverse[part(c), :]
        tile = 512
        for start in range(0, width, tile):
            value = jnp.dot(
                weight, passages[:, start : start + tile], preferred_element_type=f32
            )
            means[part(c), start : start + tile] = (value * scale).astype(bf16)
        went_out(c).start()
        return carry

    hop1(mass, mass1, 0)
    lax.fori_loop(0, chunks // 2, average, 0)
    others(mass, mass1, 0).wait_recv()
    repack(mass1, mass2)
    hop2(mass2, mass3, 1)
    lax.fori_loop(chunks // 2, chunks, average, 0)

    key = key_column[...]
    peer = key // slot_rows
    slot = lax.rem(key, slot_rows)
    pairs = key.shape[0]
    ids = lax.broadcasted_iota(jnp.int32, (pairs, peers), 1)
    at_slot = lax.broadcasted_iota(jnp.int32, (pairs, lanes), 1) == slot
    to_peer = jnp.where(ids == peer, 1.0, 0.0)
    from_peer = jnp.where(ids == lax.rem(peer, inners) * outers + peer // inners, 1.0, 0.0)
    others(mass2, mass3, 1).wait_recv()
    came = jnp.dot(from_peer, mass3[...].reshape(peers, lanes), **exact)
    came = jnp.sum(jnp.where(at_slot, came, 0.0), axis=1, keepdims=True)
    masses = [near_mass[...]] + [
        came[t * query_count : (t + 1) * query_count] for t in range(hard_count)
    ]
    peak = masses[0]
    for value in masses[1:]:
        peak = jnp.maximum(peak, value)
    total = jnp.exp(masses[0] - peak)
    for value in masses[1:]:
        total = total + jnp.exp(value - peak)
    log_value = peak + jnp.log(total)
    log_total[...] = log_value
    log_pairs = jnp.concatenate([log_value] * hard_count, axis=0)
    over_pairs = (((0,), (0,)), ((), ()))
    outgoing = lax.dot_general(to_peer, jnp.where(at_slot, log_pairs, 0.0), over_pairs, **exact)
    filled = lax.dot_general(to_peer, jnp.where(at_slot, 1.0, 0.0), over_pairs, **exact)
    outgoing = jnp.where(filled > 0.5, outgoing, absent_mass)
    log_out[...] = outgoing.reshape(log_out.shape)
    hop1(log_out, log1, 2)
    row_ids = lax.broadcasted_iota(jnp.int32, (query_count, all_rows), 1)
    shares = jnp.zeros((query_count, all_rows), f32)
    for t in range(hard_count):
        hit = key[t * query_count : (t + 1) * query_count] == row_ids
        shares = jnp.where(hit, jnp.exp(masses[1 + t] - log_value), shares)
    high = shares.astype(bf16)
    mix[:query_count, :] = high
    mix[query_count:, :] = (shares - high.astype(f32)).astype(bf16)
    mix_stored.start()
    others(log_out, log1, 2).wait_recv()
    repack(log1, log2)
    hop2(log2, log3, 3)
    row = lax.broadcasted_iota(jnp.int32, (all_rows, peers), 0)
    row_peer = row // slot_rows
    back = lax.rem(row_peer, inners) * outers + row_peer // inners
    spread = jnp.where(
        lax.broadcasted_iota(jnp.int32, (all_rows, peers), 1) == back, 1.0, 0.0
    )
    mine = lax.broadcasted_iota(jnp.int32, (all_rows, lanes), 1) == lax.rem(
        lax.broadcasted_iota(jnp.int32, (all_rows, lanes), 0), slot_rows
    )
    for c in range(chunks):
        went_out(c).wait()
        scores_stored(c).wait()
    mix_stored.wait()
    others(mass, mass1, 0).wait_send()
    others(mass2, mass3, 1).wait_send()
    others(log_out, log1, 2).wait_send()
    others(log2, log3, 3).wait_recv()
    logs = jnp.dot(spread, log3[...].reshape(peers, lanes), **exact)
    log_column[...] = jnp.sum(jnp.where(mine, logs, 0.0), axis=1, keepdims=True)
    others(log2, log3, 3).wait_send()


def far_forward(arrived, passages, near_mass, key, peers, score_scale):
    all_rows, width = arrived.shape
    passage_count = passages.shape[0]
    hard_count, query_count = key.shape
    lanes, chunks, outers = 128, 4, 8
    inners = peers // outers
    by_outer = pltpu.VMEM((outers, inners, lanes), f32)
    by_inner = pltpu.VMEM((inners, outers, lanes), f32)
    vmem = pl.BlockSpec(memory_space=pltpu.VMEM)
    hbm = pl.BlockSpec(memory_space=pltpu.HBM)
    dma = pltpu.SemaphoreType.DMA
    return pl.pallas_call(
        functools.partial(far_kernel, score_scale),
        out_shape=(
            jax.ShapeDtypeStruct((all_rows, width), bf16),
            jax.ShapeDtypeStruct((all_rows, passage_count), f32),
            jax.ShapeDtypeStruct((2 * query_count, all_rows), bf16),
            jax.ShapeDtypeStruct((query_count, 1), f32),
            jax.ShapeDtypeStruct((all_rows, 1), f32),
        ),
        in_specs=[hbm, hbm, vmem, vmem],
        out_specs=(hbm, hbm, hbm, vmem, vmem),
        scratch_shapes=[
            pltpu.VMEM((all_rows, passage_count), f32),
            pltpu.VMEM((2 * query_count, all_rows), bf16),
            dma((chunks,)),
            dma(()),
            pltpu.VMEM((all_rows, width), bf16),
            pltpu.VMEM((passage_count, width), bf16),
            pltpu.VMEM((all_rows, passage_count), bf16),
            pltpu.VMEM((all_rows, 1), f32),
            pltpu.VMEM((all_rows, width), bf16),
            by_outer,
            by_outer,
            by_outer,
            by_inner,
            by_inner,
            by_outer,
            by_inner,
            by_inner,
            dma((chunks,)),
            dma(()),
            dma((chunks,)),
            dma((4,)),
            dma((4,)),
        ],
        compiler_params=pltpu.CompilerParams(
            collective_id=2, has_side_effects=True, vmem_limit_bytes=58 * 1024 * 1024
        ),
        name="far_forward",
    )(arrived, passages, near_mass[:, None], key.reshape(-1)[:, None])


def tail_kernel(
    gradient_scale, returned, mix_in, near_in, norm, hidden, context, up, narrow_in, hidden_up_in,
    inverse_in, gradient, piece, mix, near_part, narrow, hidden_up, inverse, small_sem, near_sem, rows, hid, ctx, grad, scaled, products, scaled_up, terms, first, part, second,
    row_sem, hid_sem, ctx_sem, grad_sem, send1, recv1, send2, recv2,
):
    place = torus_place()
    own = flat_of(place)
    lane_group = place[3]
    column = own // 4
    tiles = row_sem.shape[0]
    width = terms.shape[2] * terms.shape[0]
    tile = width // tiles
    lanes = terms.shape[2]
    count = terms.shape[0]
    columns = first.shape[0]
    per_tile = tile // lanes
    query_count = gradient.shape[0]
    rerun = scaled.shape[0]
    rank = up.shape[0]
    tokens = narrow.shape[0]
    exact = dict(precision=lax.Precision.HIGHEST, preferred_element_type=f32)
    over_rows = (((0,), (0,)), ((), ()))
    over_lanes = (((1,), (1,)), ((), ()))

    def at(j):
        return pl.ds(pl.multiple_of(j * tile, tile), tile)

    def came_in(j):
        return pltpu.make_async_copy(returned.at[:, at(j)], rows.at[:, at(j)], row_sem.at[j])

    hid_in = pltpu.make_async_copy(hidden, hid, hid_sem)
    ctx_in = pltpu.make_async_copy(context, ctx, ctx_sem)
    mix_here = pltpu.make_async_copy(mix_in, mix, small_sem.at[0])
    small_here = [
        pltpu.make_async_copy(source, target, small_sem.at[1 + k])
        for k, (source, target) in enumerate(
            ((narrow_in, narrow), (hidden_up_in, hidden_up), (inverse_in, inverse))
        )
    ]

    def near_here(j):
        return pltpu.make_async_copy(
            near_in.at[:, at(j)], near_part.at[:, at(j)], near_sem.at[j]
        )

    mix_here.start()
    came_in(0).start()
    near_here(0).start()
    hid_in.start()
    for j in range(1, tiles):
        came_in(j).start()
        near_here(j).start()
    for copy in small_here:
        copy.start()
    ctx_in.start()
    barrier = pltpu.get_barrier_semaphore()

    gathers = column < count
    base = (lanes * column) // 28
    last = (lanes * column + lanes - 1) // 28
    tile0 = (28 * own) // lanes
    tile1 = (28 * own + 27) // lanes

    def of_column(j, b):
        return (j // 8, lax.rem(j // 4, 2), lax.rem(j, 4), b)

    def greet(d, carry):
        to = of_column(lax.rem(column + d, columns), lane_group)
        pl.semaphore_signal(barrier, inc=1, device_id=to, device_id_type=MESH)
        return carry

    lax.fori_loop(1, columns, greet, 0)
    for slot in range(2):
        for b in range(4):
            @pl.when((tile0 + slot <= tile1) & ((tile0 + slot != column) | (lane_group != b)))
            def _():
                to = of_column(tile0 + slot, b)
                pl.semaphore_signal(barrier, inc=1, device_id=to, device_id_type=MESH)

    products[...] = jnp.zeros_like(products)
    scaled_up[...] = jnp.zeros_like(scaled_up)
    mix_here.wait()
    hid_in.wait()

    def mixing(j, carry):
        came_in(j).wait()
        near_here(j).wait()
        both = jnp.dot(mix[...], rows[:, at(j)], preferred_element_type=f32)
        value = gradient_scale * (both[:query_count] + both[query_count:] + near_part[:, at(j)])
        grad[:, at(j)] = value
        spread = norm[:, at(j)] * (value[:rerun] / TQ)
        scaled[:, at(j)] = spread
        products[...] += lax.dot_general(
            hid[:, at(j)], spread.astype(bf16), over_lanes, preferred_element_type=f32
        )
        scaled_up[...] += lax.dot_general(spread, up[:, at(j)].astype(f32), over_lanes, **exact)
        return carry

    lax.fori_loop(0, tiles, mixing, 0)
    gradient_out = pltpu.make_async_copy(grad, gradient, grad_sem)
    gradient_out.start()

    for copy in small_here:
        copy.wait()
    token_query = lax.broadcasted_iota(jnp.int32, (tokens, rerun), 0) // TQ
    of_query = token_query == lax.broadcasted_iota(jnp.int32, (tokens, rerun), 1)
    hot = jnp.where(of_query, 1.0, 0.0)
    mean = jnp.sum(jnp.where(of_query, products[...], 0.0), axis=1, keepdims=True) / width
    rms = inverse[...]
    slope = rms * rms * rms * mean
    spread_up = jnp.dot(hot, scaled_up[...], **exact)
    grad_narrow = (adapter_scale * (rms * spread_up - slope * hidden_up[...])).astype(bf16)
    weighted = (slope * narrow[...]).astype(bf16)
    sums = lax.dot_general(hot, rms * narrow[...], over_rows, **exact)
    ctx_in.wait()

    def products_of(j, carry):
        down = lax.dot_general(
            grad_narrow, ctx[:, at(j)], over_rows, preferred_element_type=f32
        ) / RERUN_QUERIES
        up_part = (adapter_scale / RERUN_QUERIES) * (
            lax.dot_general(sums, scaled[:, at(j)], over_rows, **exact)
            - lax.dot_general(weighted, hid[:, at(j)], over_rows, preferred_element_type=f32)
        )
        for k in range(per_tile):
            terms[j * per_tile + k, :rank, :] = down[:, k * lanes : (k + 1) * lanes]
            terms[j * per_tile + k, rank:, :] = up_part[:, k * lanes : (k + 1) * lanes]
        return carry

    lax.fori_loop(0, tiles, products_of, 0)
    inside = jnp.where((base <= own) & (own <= last), 1, 0)
    pl.semaphore_wait(barrier, columns - 1 + jnp.where(gathers, last - base + 1 - inside, 0))

    def stage1(j):
        to = (j // 8, lax.rem(j // 4, 2), lax.rem(j, 4), lane_group)
        return pltpu.make_async_remote_copy(
            terms.at[j], first.at[column], send1, recv1, device_id=to, device_id_type=MESH
        )

    def start1(j, carry):
        @pl.when(j != column)
        def _():
            stage1(j).start()

        return carry

    lax.fori_loop(0, count, start1, 0)

    def sized(buffer, n, send_sem, recv_sem):
        piece_of = buffer.at[pl.ds(0, n)]
        return pltpu.make_async_remote_copy(
            piece_of, piece_of, send_sem, recv_sem,
            device_id=torus_peer(place, 1), device_id_type=MESH,
        )

    @pl.when(tile0 == tile1)
    def _():
        second[1] = jnp.zeros(second.shape[1:], f32)

    def stage2(i):
        e = base + i
        slot = column - (28 * e) // lanes
        to = (e // 32, lax.rem(e // 16, 2), lax.rem(e // 4, 4), lax.rem(e, 4))
        return pltpu.make_async_remote_copy(
            part, second.at[slot, lane_group], send2.at[i], recv2.at[slot, lane_group],
            device_id=to, device_id_type=MESH,
        )

    @pl.when(gathers)
    def _():
        first[column] = terms[column]
        sized(first, columns - 1, send1, recv1).wait_recv()
        part[...] = jnp.sum(first[...], axis=0)
        for i in range(6):
            e = base + i

            @pl.when((e <= last) & (e != own))
            def _():
                stage2(i).start()

            @pl.when((e <= last) & (e == own))
            def _():
                second[column - tile0, lane_group] = part[...]

        sized(terms, count - 1, send1, recv1).wait_send()

    @pl.when(column >= count)
    def _():
        sized(terms, count, send1, recv1).wait_send()

    for slot in range(2):
        from_tile = tile0 + slot
        for b in range(4):
            @pl.when((from_tile <= tile1) & ((from_tile != column) | (lane_group != b)))
            def _():
                pltpu.make_async_remote_copy(
                    part, second.at[slot, b], send2.at[0], recv2.at[slot, b],
                    device_id=torus_peer(place, 1), device_id_type=MESH,
                ).wait_recv()

    left = jnp.sum(second[0], axis=0)
    right = jnp.sum(second[1], axis=0)
    offset = 28 * own - lanes * tile0
    source = lax.broadcasted_iota(jnp.int32, (lanes, lanes), 0)
    target = lax.broadcasted_iota(jnp.int32, (lanes, lanes), 1) + offset
    piece[...] = jnp.dot(left, jnp.where(source == target, 1.0, 0.0), **exact) + jnp.dot(
        right, jnp.where(source + lanes == target, 1.0, 0.0), **exact
    )

    @pl.when(gathers)
    def _():
        for i in range(6):
            e = base + i

            @pl.when((e <= last) & (e != own))
            def _():
                stage2(i).wait_send()

    gradient_out.wait()


def tail(returned, mix, near_part, norm, hidden, context, up, narrow, hidden_up, inverse, scale):
    all_rows, width = returned.shape
    query_count = near_part.shape[0]
    tokens, rank = narrow.shape
    tiles, lanes, rerun = 7, 128, RERUN_QUERIES
    vmem = pl.BlockSpec(memory_space=pltpu.VMEM)
    hbm = pl.BlockSpec(memory_space=pltpu.HBM)
    dma = pltpu.SemaphoreType.DMA
    return pl.pallas_call(
        functools.partial(tail_kernel, scale),
        out_shape=(
            jax.ShapeDtypeStruct((query_count, width), f32),
            jax.ShapeDtypeStruct((2 * rank, lanes), f32),
        ),
        in_specs=[hbm, hbm, hbm, vmem, hbm, hbm, vmem, hbm, hbm, hbm],
        out_specs=(hbm, vmem),
        scratch_shapes=[
            pltpu.VMEM(mix.shape, bf16),
            pltpu.VMEM(near_part.shape, f32),
            pltpu.VMEM(narrow.shape, f32),
            pltpu.VMEM(hidden_up.shape, f32),
            pltpu.VMEM(inverse.shape, f32),
            dma((4,)),
            dma((tiles,)),
            pltpu.VMEM((all_rows, width), bf16),
            pltpu.VMEM((tokens, width), bf16),
            pltpu.VMEM((tokens, width), bf16),
            pltpu.VMEM((query_count, width), f32),
            pltpu.VMEM((rerun, width), f32),
            pltpu.VMEM((tokens, rerun), f32),
            pltpu.VMEM((rerun, rank), f32),
            pltpu.VMEM((width // lanes, 2 * rank, lanes), f32),
            pltpu.VMEM((32, 2 * rank, lanes), f32),
            pltpu.VMEM((2 * rank, lanes), f32),
            pltpu.VMEM((2, 4, 2 * rank, lanes), f32),
            dma((tiles,)),
            dma(()),
            dma(()),
            dma(()),
            dma(()),
            dma(()),
            dma((6,)),
            dma((2, 4)),
        ],
        compiler_params=pltpu.CompilerParams(
            collective_id=3, has_side_effects=True, vmem_limit_bytes=58 * 1024 * 1024
        ),
        name="tail",
    )(returned, mix, near_part, norm, hidden, context, up, narrow, hidden_up, inverse)


def local(
    queries,
    passages,
    hard_block_offsets,
    positive,
    context,
    residual,
    output_weight,
    adapter_down_weight,
    adapter_up_weight,
    final_norm_weight,
):
    device_count = lax.axis_size(PB_PA)
    block_count, hard_count = hard_block_offsets.shape
    query_count = queries.shape[0]
    block_rows = query_count // block_count
    capacity = 2 * block_count * hard_count // device_count
    slot_rows = capacity * block_rows
    all_rows = device_count * slot_rows
    passage_count = passages.shape[0]
    score_scale = inverse_temp / math.sqrt(MODEL_WIDTH)


    source = lax.axis_index(PB_PA)
    target = ((source + 1 + hard_block_offsets) % device_count).reshape(-1)
    order = jnp.arange(target.shape[0], dtype=jnp.int32)
    earlier = (target[:, None] == target[None, :]) & (order[:, None] > order[None, :])
    slot = target * capacity + jnp.sum(earlier.astype(jnp.int32), axis=1)
    slot_of = slot.reshape(block_count, hard_count).T
    key = jnp.repeat(slot_of, block_rows, axis=1) * block_rows + (
        jnp.arange(query_count, dtype=jnp.int32) % block_rows
    )
    row_ids = jnp.arange(all_rows, dtype=jnp.int32)
    picks = row_ids[:, None] == key[0][None, :]
    for t in range(1, hard_count):
        picks = picks | (row_ids[:, None] == key[t][None, :])
    outgoing = jnp.dot(picks.astype(bf16), queries, preferred_element_type=bf16)
    outgoing, first, second = lax.optimization_barrier(
        (outgoing, *weight_halves_sent(output_weight))
    )
    weight_rows = gather_input(first, second)
    arrived = exchange(outgoing.reshape(device_count, slot_rows, MODEL_WIDTH))
    arrived = arrived.reshape(-1, MODEL_WIDTH)

    half_weight = lax.all_gather(weight_rows, CHIPS, axis=0, tiled=True)
    near_scores = dot(queries, passages.T) * score_scale
    near_peak = jnp.max(near_scores, axis=1)
    near_exp = jnp.exp(near_scores - near_peak[:, None])
    near_sum = jnp.sum(near_exp, axis=1)
    near_mass = near_peak + jnp.log(near_sum)
    positive_hot = positive[:, None] == jnp.arange(passage_count, dtype=jnp.int32)[None, :]
    stacked = dot(
        jnp.concatenate([near_exp.astype(bf16), positive_hot.astype(bf16)], axis=0), passages
    )

    far_mean, far_scores, mix_parts, log_total, log_arrived = far_forward(
        arrived, passages, near_mass, key, device_count, score_scale
    )
    returned = exchange(far_mean.reshape(device_count, slot_rows, MODEL_WIDTH))
    returned = returned.reshape(-1, MODEL_WIDTH)
    log_total = log_total[:, 0]
    near_share = jnp.exp(near_mass - log_total)
    near_part = (near_share / near_sum)[:, None] * stacked[:query_count] - stacked[query_count:]

    product_dims = (((0,), (0,)), ((), ()))
    far_weight = jnp.exp(far_scores - log_arrived).astype(bf16)
    near_weight = (
        jnp.exp(near_scores - log_total[:, None]) - positive_hot.astype(f32)
    ).astype(bf16)
    far_grad = lax.dot_general(far_weight, arrived, product_dims, preferred_element_type=f32)
    near_grad = lax.dot_general(near_weight, queries, product_dims, preferred_element_type=f32)

    hidden_low, narrow, hidden_up, inverse_rms = layer_forward(
        context, half_weight, residual, adapter_down_weight.T, adapter_up_weight
    )
    grad_passages = loss_scale * score_scale * (far_grad + near_grad)

    returned, near_part, hidden_low, grad_passages = lax.optimization_barrier(
        (returned, near_part, hidden_low, grad_passages)
    )
    query_gradient, sums = tail(
        returned,
        mix_parts,
        near_part,
        final_norm_weight.astype(f32)[None, :],
        hidden_low,
        context,
        adapter_up_weight,
        narrow,
        hidden_up,
        inverse_rms,
        loss_scale * score_scale,
    )
    rank = narrow.shape[1]
    columns = MODEL_WIDTH // device_count
    return (
        query_gradient,
        grad_passages,
        sums[:rank, :columns].T,
        sums[rank:, :columns],
    )


def solution(mesh):
    torus = Mesh(mesh.devices.reshape(4, 2, 4, 4), PB_PA)
    in_specs = (
        P(PB_PA, None),
        P(PB_PA, None),
        P(PB_PA, None),
        P(PB_PA),
        P(PB_PA, None),
        P(PB_PA, None),
        P(PB_PA, None),
        P(),
        P(),
        P(),
    )
    out_specs = (P(PB_PA, None), P(PB_PA, None), P(PB_PA, None), P(None, PB_PA))
    return jax.shard_map(local, mesh=torus, in_specs=in_specs, out_specs=out_specs, check_vma=False)
```

```python
import functools
import math

import jax
import jax.numpy as jnp
from jax import lax
from jax.experimental import pallas as pl
from jax.experimental.pallas import tpu as pltpu
from jax.sharding import Mesh
from jax.sharding import PartitionSpec as P

MODEL_WIDTH = 3584
RERUN_QUERIES = 16
TQ = 32
PB_PA = ("pb_0", "pb_1", "pa_0", "pa_1")
CHIPS = ("pb_0", "pa_0", "pa_1")

inverse_temp = 2.0
loss_scale = 32.0
adapter_scale = 2.0
epsilon = 1e-06
absent_mass = 1e30
f32 = jnp.float32
bf16 = jnp.bfloat16
MESH = pl.DeviceIdType.MESH


def dot(a, b, **kw):
    return jnp.dot(a, b, preferred_element_type=f32, **kw)


def two_parts(x):
    high = x.astype(bf16)
    return high, (x - high.astype(f32)).astype(bf16)


def device_of(chip, core, per_plane):
    return (chip // per_plane) * 2 * per_plane + core * per_plane + chip % per_plane


def weight_halves_sent(rows):
    count = lax.axis_size(PB_PA)
    per_plane = lax.axis_size("pa_0") * lax.axis_size("pa_1")
    half = rows.shape[1] // 2
    left, right = rows[:, :half], rows[:, half:]
    odd = lax.axis_index("pa_1") % 2 == 1
    same = [(f, device_of(f // 2, f % 2, per_plane)) for f in range(count)]
    other = [(f, device_of(f // 2, 1 - f % 2, per_plane)) for f in range(count)]
    first = lax.ppermute(jnp.where(odd, right, left), PB_PA, same)
    second = lax.ppermute(jnp.where(odd, left, right), PB_PA, other)
    return first, second


def gather_input(first, second):
    core = lax.axis_index("pb_1")
    low = jnp.where(core == 0, first, second)
    high = jnp.where(core == 0, second, first)
    return jnp.concatenate([low, high], axis=0)


def exchange(array):
    return lax.all_to_all(array, PB_PA, split_axis=0, concat_axis=0, tiled=True)


def layer_forward_kernel(
    context, half_weight, residual, down, up, hidden, narrow, hidden_up, inverse,
    own, other, block, own_sem, send_sem, recv_sem, out_sem, squares,
):
    core = lax.axis_index("pb_1")
    twin = (lax.axis_index("pb_0"), 1 - core, lax.axis_index("pa_0"), lax.axis_index("pa_1"))
    tile = own.shape[2]
    half = half_weight.shape[1]
    tiles = half // tile
    barrier = pltpu.get_barrier_semaphore()
    pl.semaphore_signal(barrier, inc=1, device_id=twin, device_id_type=MESH)
    pl.semaphore_wait(barrier, 1)

    def columns(j):
        return pl.ds(pl.multiple_of(j * tile, tile), tile)

    def sent(j):
        return pltpu.make_async_remote_copy(
            half_weight.at[:, columns(j)], other.at[j], send_sem.at[j], recv_sem.at[j],
            device_id=twin, device_id_type=MESH,
        )

    def fetched(j):
        return pltpu.make_async_copy(
            half_weight.at[:, columns(j)], own.at[lax.rem(j, 2)], own_sem.at[lax.rem(j, 2)]
        )

    fetched(0).start()

    def send(j, carry):
        sent(j).start()
        return carry

    lax.fori_loop(0, tiles, send, 0)
    low = lax.dot_general(
        context[...], down[...], (((1,), (1,)), ((), ())), preferred_element_type=f32
    ).astype(bf16)
    narrow[...] = low.astype(f32)
    squares[...] = jnp.zeros_like(squares)
    hidden_up[...] = jnp.zeros_like(hidden_up)

    def stored(columns, k):
        return pltpu.make_async_copy(
            block.at[:, columns], hidden.at[:, columns], out_sem.at[k]
        )

    def step(weight, start, k):
        at = pl.ds(pl.multiple_of(start, tile), tile)
        up_tile = up[:, at]
        value = (
            residual[:, at].astype(f32)
            + jnp.dot(context[...], weight, preferred_element_type=f32)
            + adapter_scale * jnp.dot(low, up_tile, preferred_element_type=f32)
        )
        squares[...] += jnp.sum(value * value, axis=1, keepdims=True)
        value = value.astype(bf16)
        block[:, at] = value
        stored(at, k).start()
        hidden_up[...] += lax.dot_general(
            value, up_tile, (((1,), (1,)), ((), ())), preferred_element_type=f32
        )

    def own_step(j, carry):
        fetched(j).wait()

        @pl.when(j + 1 < tiles)
        def _():
            fetched(j + 1).start()

        step(own[lax.rem(j, 2)], core * half + j * tile, j)
        return carry

    lax.fori_loop(0, tiles, own_step, 0)

    def other_step(j, carry):
        sent(j).wait_recv()
        step(other[j], (1 - core) * half + j * tile, tiles + j)
        return carry

    lax.fori_loop(0, tiles, other_step, 0)
    inverse[...] = lax.rsqrt(squares[...] / MODEL_WIDTH + epsilon)

    def done(j, carry):
        sent(j).wait_send()
        stored(columns(j), j).wait()
        stored(columns(j), tiles + j).wait()
        return carry

    lax.fori_loop(0, tiles, done, 0)


def layer_forward(context, half_weight, residual, down, up):
    tokens, width = context.shape
    half = half_weight.shape[1]
    tile = 256
    tiles = half // tile
    rank = up.shape[0]
    vmem = pl.BlockSpec(memory_space=pltpu.VMEM)
    return pl.pallas_call(
        layer_forward_kernel,
        out_shape=(
            jax.ShapeDtypeStruct((tokens, width), bf16),
            jax.ShapeDtypeStruct((tokens, rank), f32),
            jax.ShapeDtypeStruct((tokens, rank), f32),
            jax.ShapeDtypeStruct((tokens, 1), f32),
        ),
        in_specs=[vmem, pl.BlockSpec(memory_space=pl.ANY), vmem, vmem, vmem],
        out_specs=(pl.BlockSpec(memory_space=pltpu.HBM), vmem, vmem, vmem),
        scratch_shapes=[
            pltpu.VMEM((2, width, tile), bf16),
            pltpu.VMEM((tiles, width, tile), bf16),
            pltpu.VMEM((tokens, width), bf16),
            pltpu.SemaphoreType.DMA((2,)),
            pltpu.SemaphoreType.DMA((tiles,)),
            pltpu.SemaphoreType.DMA((tiles,)),
            pltpu.SemaphoreType.DMA((2 * tiles,)),
            pltpu.VMEM((tokens, 1), f32),
        ],
        compiler_params=pltpu.CompilerParams(
            collective_id=1, has_side_effects=True, vmem_limit_bytes=58 * 1024 * 1024
        ),
        cost_estimate=pl.CostEstimate(flops=1000, bytes_accessed=1000, transcendentals=0),
        name="layer_forward",
    )(context, half_weight, residual, down, up)


def torus_place():
    return tuple(lax.axis_index(axis) for axis in PB_PA)


def flat_of(place):
    return ((place[0] * 2 + place[1]) * 4 + place[2]) * 4 + place[3]


def torus_peer(place, j):
    return (
        lax.rem(place[0] + lax.rem(j, 4), 4),
        lax.rem(place[1] + j // 64, 2),
        lax.rem(place[2] + lax.rem(j // 4, 4), 4),
        lax.rem(place[3] + lax.rem(j // 16, 4), 4),
    )


def far_kernel(
    score_scale, arrived, passages_in, near_mass, key_column, mean, scores_out, mix_out, log_total,
    log_column, scores, mix, score_sem, mix_sem, rows, passages, weights, inverse, means, mass, log_out, mass1, mass2, mass3, log1,
    log2, log3, row_sem, passage_sem, mean_sem, send_sem, recv_sem,
):
    place = torus_place()
    outer = place[0] * 2 + place[1]
    inner = place[2] * 4 + place[3]
    outers, inners, lanes = mass.shape
    peers = outers * inners
    query_count = near_mass.shape[0]
    hard_count = key_column.shape[0] // query_count
    all_rows, passage_count = scores.shape
    slot_rows = all_rows // peers
    width = passages.shape[1]
    chunks = row_sem.shape[0]
    block = all_rows // chunks
    exact = dict(precision=lax.Precision.HIGHEST, preferred_element_type=f32)

    def along_outer(d):
        to = lax.rem(outer + d, outers)
        return to, (to // 2, lax.rem(to, 2), place[2], place[3])

    def along_inner(d):
        to = lax.rem(inner + d, inners)
        return to, (place[0], place[1], to // 4, lax.rem(to, 4))

    def part(c):
        return pl.ds(pl.multiple_of(c * block, block), block)

    def came_in(c):
        return pltpu.make_async_copy(arrived.at[part(c)], rows.at[part(c)], row_sem.at[c])

    def went_out(c):
        return pltpu.make_async_copy(means.at[part(c)], mean.at[part(c)], mean_sem.at[c])

    def scores_stored(c):
        return pltpu.make_async_copy(
            scores.at[part(c)], scores_out.at[part(c)], score_sem.at[c]
        )

    mix_stored = pltpu.make_async_copy(mix, mix_out, mix_sem)
    passages_here = pltpu.make_async_copy(passages_in, passages, passage_sem)
    passages_here.start()
    for c in range(chunks):
        came_in(c).start()
    barrier = pltpu.get_barrier_semaphore()
    for d in range(1, outers):
        pl.semaphore_signal(barrier, inc=1, device_id=along_outer(d)[1], device_id_type=MESH)
    for d in range(1, inners):
        pl.semaphore_signal(barrier, inc=1, device_id=along_inner(d)[1], device_id_type=MESH)
    passages_here.wait()
    lane_ids = lax.broadcasted_iota(jnp.int32, (block, lanes), 1)
    slot_ids = lax.rem(lax.broadcasted_iota(jnp.int32, (block, lanes), 0), slot_rows)
    block_peers = block // slot_rows
    peer_ids = lax.broadcasted_iota(jnp.int32, (block_peers, block), 0)
    peer_rows = lax.broadcasted_iota(jnp.int32, (block_peers, block), 1) // slot_rows
    gather_rows = jnp.where(peer_ids == peer_rows, 1.0, 0.0)

    def score(c, carry):
        came_in(c).wait()
        value = score_scale * lax.dot_general(
            rows[part(c), :], passages[...], (((1,), (1,)), ((), ())),
            preferred_element_type=f32,
        )
        scores[part(c), :] = value
        scores_stored(c).start()
        peak = jnp.max(value, axis=1, keepdims=True)
        weight = jnp.exp(value - peak)
        total = jnp.sum(weight, axis=1, keepdims=True)
        weights[part(c), :] = weight.astype(bf16)
        inverse[part(c), :] = 1.0 / total
        spread = jnp.where(lane_ids == slot_ids, peak + jnp.log(total), 0.0)
        compact = jnp.dot(gather_rows, spread, **exact)
        step = block_peers // inners
        mass[pl.ds(c * step, step)] = compact.reshape(step, inners, lanes)
        return carry

    lax.fori_loop(0, chunks, score, 0)
    pl.semaphore_wait(barrier, outers - 1 + inners - 1)

    def hop1(source, target, which):
        for d in range(1, outers):
            to, device = along_outer(d)
            pltpu.make_async_remote_copy(
                source.at[to], target.at[outer], send_sem.at[which], recv_sem.at[which],
                device_id=device, device_id_type=MESH,
            ).start()
        target[outer] = source[outer]

    def hop2(source, target, which):
        for d in range(1, inners):
            to, device = along_inner(d)
            pltpu.make_async_remote_copy(
                source.at[to], target.at[inner], send_sem.at[which], recv_sem.at[which],
                device_id=device, device_id_type=MESH,
            ).start()
        target[inner] = source[inner]

    def others(source, target, which):
        rest = pl.ds(0, source.shape[0] - 1)
        return pltpu.make_async_remote_copy(
            source.at[rest], target.at[rest], send_sem.at[which], recv_sem.at[which],
            device_id=along_outer(1)[1], device_id_type=MESH,
        )

    def repack(source, target):
        for r in range(inners):
            target[r] = source[:, r, :]

    def average(c, carry):
        weight = weights[part(c), :]
        scale = inverse[part(c), :]
        tile = 512
        for start in range(0, width, tile):
            value = jnp.dot(
                weight, passages[:, start : start + tile], preferred_element_type=f32
            )
            means[part(c), start : start + tile] = (value * scale).astype(bf16)
        went_out(c).start()
        return carry

    hop1(mass, mass1, 0)
    lax.fori_loop(0, chunks // 2, average, 0)
    others(mass, mass1, 0).wait_recv()
    repack(mass1, mass2)
    hop2(mass2, mass3, 1)
    lax.fori_loop(chunks // 2, chunks, average, 0)

    key = key_column[...]
    peer = key // slot_rows
    slot = lax.rem(key, slot_rows)
    pairs = key.shape[0]
    ids = lax.broadcasted_iota(jnp.int32, (pairs, peers), 1)
    at_slot = lax.broadcasted_iota(jnp.int32, (pairs, lanes), 1) == slot
    to_peer = jnp.where(ids == peer, 1.0, 0.0)
    from_peer = jnp.where(ids == lax.rem(peer, inners) * outers + peer // inners, 1.0, 0.0)
    others(mass2, mass3, 1).wait_recv()
    came = jnp.dot(from_peer, mass3[...].reshape(peers, lanes), **exact)
    came = jnp.sum(jnp.where(at_slot, came, 0.0), axis=1, keepdims=True)
    masses = [near_mass[...]] + [
        came[t * query_count : (t + 1) * query_count] for t in range(hard_count)
    ]
    peak = masses[0]
    for value in masses[1:]:
        peak = jnp.maximum(peak, value)
    total = jnp.exp(masses[0] - peak)
    for value in masses[1:]:
        total = total + jnp.exp(value - peak)
    log_value = peak + jnp.log(total)
    log_total[...] = log_value
    log_pairs = jnp.concatenate([log_value] * hard_count, axis=0)
    over_pairs = (((0,), (0,)), ((), ()))
    outgoing = lax.dot_general(to_peer, jnp.where(at_slot, log_pairs, 0.0), over_pairs, **exact)
    filled = lax.dot_general(to_peer, jnp.where(at_slot, 1.0, 0.0), over_pairs, **exact)
    outgoing = jnp.where(filled > 0.5, outgoing, absent_mass)
    log_out[...] = outgoing.reshape(log_out.shape)
    hop1(log_out, log1, 2)
    row_ids = lax.broadcasted_iota(jnp.int32, (query_count, all_rows), 1)
    shares = jnp.zeros((query_count, all_rows), f32)
    for t in range(hard_count):
        hit = key[t * query_count : (t + 1) * query_count] == row_ids
        shares = jnp.where(hit, jnp.exp(masses[1 + t] - log_value), shares)
    high = shares.astype(bf16)
    mix[:query_count, :] = high
    mix[query_count:, :] = (shares - high.astype(f32)).astype(bf16)
    mix_stored.start()
    others(log_out, log1, 2).wait_recv()
    repack(log1, log2)
    hop2(log2, log3, 3)
    row = lax.broadcasted_iota(jnp.int32, (all_rows, peers), 0)
    row_peer = row // slot_rows
    back = lax.rem(row_peer, inners) * outers + row_peer // inners
    spread = jnp.where(
        lax.broadcasted_iota(jnp.int32, (all_rows, peers), 1) == back, 1.0, 0.0
    )
    mine = lax.broadcasted_iota(jnp.int32, (all_rows, lanes), 1) == lax.rem(
        lax.broadcasted_iota(jnp.int32, (all_rows, lanes), 0), slot_rows
    )
    for c in range(chunks):
        went_out(c).wait()
        scores_stored(c).wait()
    mix_stored.wait()
    others(mass, mass1, 0).wait_send()
    others(mass2, mass3, 1).wait_send()
    others(log_out, log1, 2).wait_send()
    others(log2, log3, 3).wait_recv()
    logs = jnp.dot(spread, log3[...].reshape(peers, lanes), **exact)
    log_column[...] = jnp.sum(jnp.where(mine, logs, 0.0), axis=1, keepdims=True)
    others(log2, log3, 3).wait_send()


def far_forward(arrived, passages, near_mass, key, peers, score_scale):
    all_rows, width = arrived.shape
    passage_count = passages.shape[0]
    hard_count, query_count = key.shape
    lanes, chunks, outers = 128, 4, 8
    inners = peers // outers
    by_outer = pltpu.VMEM((outers, inners, lanes), f32)
    by_inner = pltpu.VMEM((inners, outers, lanes), f32)
    vmem = pl.BlockSpec(memory_space=pltpu.VMEM)
    hbm = pl.BlockSpec(memory_space=pltpu.HBM)
    dma = pltpu.SemaphoreType.DMA
    return pl.pallas_call(
        functools.partial(far_kernel, score_scale),
        out_shape=(
            jax.ShapeDtypeStruct((all_rows, width), bf16),
            jax.ShapeDtypeStruct((all_rows, passage_count), f32),
            jax.ShapeDtypeStruct((2 * query_count, all_rows), bf16),
            jax.ShapeDtypeStruct((query_count, 1), f32),
            jax.ShapeDtypeStruct((all_rows, 1), f32),
        ),
        in_specs=[hbm, hbm, vmem, vmem],
        out_specs=(hbm, hbm, hbm, vmem, vmem),
        scratch_shapes=[
            pltpu.VMEM((all_rows, passage_count), f32),
            pltpu.VMEM((2 * query_count, all_rows), bf16),
            dma((chunks,)),
            dma(()),
            pltpu.VMEM((all_rows, width), bf16),
            pltpu.VMEM((passage_count, width), bf16),
            pltpu.VMEM((all_rows, passage_count), bf16),
            pltpu.VMEM((all_rows, 1), f32),
            pltpu.VMEM((all_rows, width), bf16),
            by_outer,
            by_outer,
            by_outer,
            by_inner,
            by_inner,
            by_outer,
            by_inner,
            by_inner,
            dma((chunks,)),
            dma(()),
            dma((chunks,)),
            dma((4,)),
            dma((4,)),
        ],
        compiler_params=pltpu.CompilerParams(
            collective_id=2, has_side_effects=True, vmem_limit_bytes=58 * 1024 * 1024
        ),
        name="far_forward",
    )(arrived, passages, near_mass[:, None], key.reshape(-1)[:, None])


def tail_kernel(
    gradient_scale, returned, mix_in, near_in, norm, hidden, context, up, narrow_in, hidden_up_in,
    inverse_in, gradient, piece, mix, near_part, narrow, hidden_up, inverse, small_sem, near_sem, rows, hid, ctx, grad, scaled, products, scaled_up, terms, first, part, second,
    row_sem, hid_sem, ctx_sem, grad_sem, send1, recv1, send2, recv2,
):
    place = torus_place()
    own = flat_of(place)
    lane_group = place[3]
    column = own // 4
    tiles = row_sem.shape[0]
    width = terms.shape[2] * terms.shape[0]
    tile = width // tiles
    lanes = terms.shape[2]
    count = terms.shape[0]
    columns = first.shape[0]
    per_tile = tile // lanes
    query_count = gradient.shape[0]
    rerun = scaled.shape[0]
    rank = up.shape[0]
    tokens = narrow.shape[0]
    exact = dict(precision=lax.Precision.HIGHEST, preferred_element_type=f32)
    over_rows = (((0,), (0,)), ((), ()))
    over_lanes = (((1,), (1,)), ((), ()))

    def at(j):
        return pl.ds(pl.multiple_of(j * tile, tile), tile)

    def came_in(j):
        return pltpu.make_async_copy(returned.at[:, at(j)], rows.at[:, at(j)], row_sem.at[j])

    hid_in = pltpu.make_async_copy(hidden, hid, hid_sem)
    ctx_in = pltpu.make_async_copy(context, ctx, ctx_sem)
    mix_here = pltpu.make_async_copy(mix_in, mix, small_sem.at[0])
    small_here = [
        pltpu.make_async_copy(source, target, small_sem.at[1 + k])
        for k, (source, target) in enumerate(
            ((narrow_in, narrow), (hidden_up_in, hidden_up), (inverse_in, inverse))
        )
    ]

    def near_here(j):
        return pltpu.make_async_copy(
            near_in.at[:, at(j)], near_part.at[:, at(j)], near_sem.at[j]
        )

    mix_here.start()
    came_in(0).start()
    near_here(0).start()
    hid_in.start()
    for j in range(1, tiles):
        came_in(j).start()
        near_here(j).start()
    for copy in small_here:
        copy.start()
    ctx_in.start()
    barrier = pltpu.get_barrier_semaphore()

    gathers = column < count
    base = (lanes * column) // 28
    last = (lanes * column + lanes - 1) // 28
    tile0 = (28 * own) // lanes
    tile1 = (28 * own + 27) // lanes

    def of_column(j, b):
        return (j // 8, lax.rem(j // 4, 2), lax.rem(j, 4), b)

    def greet(d, carry):
        to = of_column(lax.rem(column + d, columns), lane_group)
        pl.semaphore_signal(barrier, inc=1, device_id=to, device_id_type=MESH)
        return carry

    lax.fori_loop(1, columns, greet, 0)
    for slot in range(2):
        for b in range(4):
            @pl.when((tile0 + slot <= tile1) & ((tile0 + slot != column) | (lane_group != b)))
            def _():
                to = of_column(tile0 + slot, b)
                pl.semaphore_signal(barrier, inc=1, device_id=to, device_id_type=MESH)

    products[...] = jnp.zeros_like(products)
    scaled_up[...] = jnp.zeros_like(scaled_up)
    mix_here.wait()
    hid_in.wait()

    def mixing(j, carry):
        came_in(j).wait()
        near_here(j).wait()
        both = jnp.dot(mix[...], rows[:, at(j)], preferred_element_type=f32)
        value = gradient_scale * (both[:query_count] + both[query_count:] + near_part[:, at(j)])
        grad[:, at(j)] = value
        spread = norm[:, at(j)] * (value[:rerun] / TQ)
        scaled[:, at(j)] = spread
        products[...] += lax.dot_general(
            hid[:, at(j)], spread.astype(bf16), over_lanes, preferred_element_type=f32
        )
        scaled_up[...] += lax.dot_general(spread, up[:, at(j)].astype(f32), over_lanes, **exact)
        return carry

    lax.fori_loop(0, tiles, mixing, 0)
    gradient_out = pltpu.make_async_copy(grad, gradient, grad_sem)
    gradient_out.start()

    for copy in small_here:
        copy.wait()
    token_query = lax.broadcasted_iota(jnp.int32, (tokens, rerun), 0) // TQ
    of_query = token_query == lax.broadcasted_iota(jnp.int32, (tokens, rerun), 1)
    hot = jnp.where(of_query, 1.0, 0.0)
    mean = jnp.sum(jnp.where(of_query, products[...], 0.0), axis=1, keepdims=True) / width
    rms = inverse[...]
    slope = rms * rms * rms * mean
    spread_up = jnp.dot(hot, scaled_up[...], **exact)
    grad_narrow = (adapter_scale * (rms * spread_up - slope * hidden_up[...])).astype(bf16)
    weighted = (slope * narrow[...]).astype(bf16)
    sums = lax.dot_general(hot, rms * narrow[...], over_rows, **exact)
    ctx_in.wait()

    def products_of(j, carry):
        down = lax.dot_general(
            grad_narrow, ctx[:, at(j)], over_rows, preferred_element_type=f32
        ) / RERUN_QUERIES
        up_part = (adapter_scale / RERUN_QUERIES) * (
            lax.dot_general(sums, scaled[:, at(j)], over_rows, **exact)
            - lax.dot_general(weighted, hid[:, at(j)], over_rows, preferred_element_type=f32)
        )
        for k in range(per_tile):
            terms[j * per_tile + k, :rank, :] = down[:, k * lanes : (k + 1) * lanes]
            terms[j * per_tile + k, rank:, :] = up_part[:, k * lanes : (k + 1) * lanes]
        return carry

    lax.fori_loop(0, tiles, products_of, 0)
    inside = jnp.where((base <= own) & (own <= last), 1, 0)
    pl.semaphore_wait(barrier, columns - 1 + jnp.where(gathers, last - base + 1 - inside, 0))

    def stage1(j):
        to = (j // 8, lax.rem(j // 4, 2), lax.rem(j, 4), lane_group)
        return pltpu.make_async_remote_copy(
            terms.at[j], first.at[column], send1, recv1, device_id=to, device_id_type=MESH
        )

    def start1(j, carry):
        @pl.when(j != column)
        def _():
            stage1(j).start()

        return carry

    lax.fori_loop(0, count, start1, 0)

    def sized(buffer, n, send_sem, recv_sem):
        piece_of = buffer.at[pl.ds(0, n)]
        return pltpu.make_async_remote_copy(
            piece_of, piece_of, send_sem, recv_sem,
            device_id=torus_peer(place, 1), device_id_type=MESH,
        )

    @pl.when(tile0 == tile1)
    def _():
        second[1] = jnp.zeros(second.shape[1:], f32)

    def stage2(i):
        e = base + i
        slot = column - (28 * e) // lanes
        to = (e // 32, lax.rem(e // 16, 2), lax.rem(e // 4, 4), lax.rem(e, 4))
        return pltpu.make_async_remote_copy(
            part, second.at[slot, lane_group], send2.at[i], recv2.at[slot, lane_group],
            device_id=to, device_id_type=MESH,
        )

    @pl.when(gathers)
    def _():
        first[column] = terms[column]
        sized(first, columns - 1, send1, recv1).wait_recv()
        part[...] = jnp.sum(first[...], axis=0)
        for i in range(6):
            e = base + i

            @pl.when((e <= last) & (e != own))
            def _():
                stage2(i).start()

            @pl.when((e <= last) & (e == own))
            def _():
                second[column - tile0, lane_group] = part[...]

        sized(terms, count - 1, send1, recv1).wait_send()

    @pl.when(column >= count)
    def _():
        sized(terms, count, send1, recv1).wait_send()

    for slot in range(2):
        from_tile = tile0 + slot
        for b in range(4):
            @pl.when((from_tile <= tile1) & ((from_tile != column) | (lane_group != b)))
            def _():
                pltpu.make_async_remote_copy(
                    part, second.at[slot, b], send2.at[0], recv2.at[slot, b],
                    device_id=torus_peer(place, 1), device_id_type=MESH,
                ).wait_recv()

    left = jnp.sum(second[0], axis=0)
    right = jnp.sum(second[1], axis=0)
    offset = 28 * own - lanes * tile0
    source = lax.broadcasted_iota(jnp.int32, (lanes, lanes), 0)
    target = lax.broadcasted_iota(jnp.int32, (lanes, lanes), 1) + offset
    piece[...] = jnp.dot(left, jnp.where(source == target, 1.0, 0.0), **exact) + jnp.dot(
        right, jnp.where(source + lanes == target, 1.0, 0.0), **exact
    )

    @pl.when(gathers)
    def _():
        for i in range(6):
            e = base + i

            @pl.when((e <= last) & (e != own))
            def _():
                stage2(i).wait_send()

    gradient_out.wait()


def tail(returned, mix, near_part, norm, hidden, context, up, narrow, hidden_up, inverse, scale):
    all_rows, width = returned.shape
    query_count = near_part.shape[0]
    tokens, rank = narrow.shape
    tiles, lanes, rerun = 7, 128, RERUN_QUERIES
    vmem = pl.BlockSpec(memory_space=pltpu.VMEM)
    hbm = pl.BlockSpec(memory_space=pltpu.HBM)
    dma = pltpu.SemaphoreType.DMA
    return pl.pallas_call(
        functools.partial(tail_kernel, scale),
        out_shape=(
            jax.ShapeDtypeStruct((query_count, width), f32),
            jax.ShapeDtypeStruct((2 * rank, lanes), f32),
        ),
        in_specs=[hbm, hbm, hbm, vmem, hbm, hbm, vmem, hbm, hbm, hbm],
        out_specs=(hbm, vmem),
        scratch_shapes=[
            pltpu.VMEM(mix.shape, bf16),
            pltpu.VMEM(near_part.shape, f32),
            pltpu.VMEM(narrow.shape, f32),
            pltpu.VMEM(hidden_up.shape, f32),
            pltpu.VMEM(inverse.shape, f32),
            dma((4,)),
            dma((tiles,)),
            pltpu.VMEM((all_rows, width), bf16),
            pltpu.VMEM((tokens, width), bf16),
            pltpu.VMEM((tokens, width), bf16),
            pltpu.VMEM((query_count, width), f32),
            pltpu.VMEM((rerun, width), f32),
            pltpu.VMEM((tokens, rerun), f32),
            pltpu.VMEM((rerun, rank), f32),
            pltpu.VMEM((width // lanes, 2 * rank, lanes), f32),
            pltpu.VMEM((32, 2 * rank, lanes), f32),
            pltpu.VMEM((2 * rank, lanes), f32),
            pltpu.VMEM((2, 4, 2 * rank, lanes), f32),
            dma((tiles,)),
            dma(()),
            dma(()),
            dma(()),
            dma(()),
            dma(()),
            dma((6,)),
            dma((2, 4)),
        ],
        compiler_params=pltpu.CompilerParams(
            collective_id=3, has_side_effects=True, vmem_limit_bytes=58 * 1024 * 1024
        ),
        name="tail",
    )(returned, mix, near_part, norm, hidden, context, up, narrow, hidden_up, inverse)


def local(
    queries,
    passages,
    hard_block_offsets,
    positive,
    context,
    residual,
    output_weight,
    adapter_down_weight,
    adapter_up_weight,
    final_norm_weight,
):
    device_count = lax.axis_size(PB_PA)
    block_count, hard_count = hard_block_offsets.shape
    query_count = queries.shape[0]
    block_rows = query_count // block_count
    capacity = 2 * block_count * hard_count // device_count
    slot_rows = capacity * block_rows
    all_rows = device_count * slot_rows
    passage_count = passages.shape[0]
    score_scale = inverse_temp / math.sqrt(MODEL_WIDTH)


    source = lax.axis_index(PB_PA)
    target = ((source + 1 + hard_block_offsets) % device_count).reshape(-1)
    order = jnp.arange(target.shape[0], dtype=jnp.int32)
    earlier = (target[:, None] == target[None, :]) & (order[:, None] > order[None, :])
    slot = target * capacity + jnp.sum(earlier.astype(jnp.int32), axis=1)
    slot_of = slot.reshape(block_count, hard_count).T
    key = jnp.repeat(slot_of, block_rows, axis=1) * block_rows + (
        jnp.arange(query_count, dtype=jnp.int32) % block_rows
    )
    row_ids = jnp.arange(all_rows, dtype=jnp.int32)
    key, first, second = lax.optimization_barrier((key, *weight_halves_sent(output_weight)))
    weight_rows = gather_input(first, second)
    picks = row_ids[:, None] == key[0][None, :]
    for t in range(1, hard_count):
        picks = picks | (row_ids[:, None] == key[t][None, :])
    outgoing = jnp.dot(picks.astype(bf16), queries, preferred_element_type=bf16)
    arrived = exchange(outgoing.reshape(device_count, slot_rows, MODEL_WIDTH))
    arrived = arrived.reshape(-1, MODEL_WIDTH)

    half_weight = lax.all_gather(weight_rows, CHIPS, axis=0, tiled=True)
    near_scores = dot(queries, passages.T) * score_scale
    near_peak = jnp.max(near_scores, axis=1)
    near_exp = jnp.exp(near_scores - near_peak[:, None])
    near_sum = jnp.sum(near_exp, axis=1)
    near_mass = near_peak + jnp.log(near_sum)
    positive_hot = positive[:, None] == jnp.arange(passage_count, dtype=jnp.int32)[None, :]
    stacked = dot(
        jnp.concatenate([near_exp.astype(bf16), positive_hot.astype(bf16)], axis=0), passages
    )

    far_mean, far_scores, mix_parts, log_total, log_arrived = far_forward(
        arrived, passages, near_mass, key, device_count, score_scale
    )
    returned = exchange(far_mean.reshape(device_count, slot_rows, MODEL_WIDTH))
    returned = returned.reshape(-1, MODEL_WIDTH)
    log_total = log_total[:, 0]
    near_share = jnp.exp(near_mass - log_total)
    near_part = (near_share / near_sum)[:, None] * stacked[:query_count] - stacked[query_count:]

    product_dims = (((0,), (0,)), ((), ()))
    far_weight = jnp.exp(far_scores - log_arrived).astype(bf16)
    near_weight = (
        jnp.exp(near_scores - log_total[:, None]) - positive_hot.astype(f32)
    ).astype(bf16)
    far_grad = lax.dot_general(far_weight, arrived, product_dims, preferred_element_type=f32)
    near_grad = lax.dot_general(near_weight, queries, product_dims, preferred_element_type=f32)

    hidden_low, narrow, hidden_up, inverse_rms = layer_forward(
        context, half_weight, residual, adapter_down_weight.T, adapter_up_weight
    )
    grad_passages = loss_scale * score_scale * (far_grad + near_grad)

    returned, near_part, hidden_low, grad_passages = lax.optimization_barrier(
        (returned, near_part, hidden_low, grad_passages)
    )
    query_gradient, sums = tail(
        returned,
        mix_parts,
        near_part,
        final_norm_weight.astype(f32)[None, :],
        hidden_low,
        context,
        adapter_up_weight,
        narrow,
        hidden_up,
        inverse_rms,
        loss_scale * score_scale,
    )
    rank = narrow.shape[1]
    columns = MODEL_WIDTH // device_count
    return (
        query_gradient,
        grad_passages,
        sums[:rank, :columns].T,
        sums[rank:, :columns],
    )


def solution(mesh):
    torus = Mesh(mesh.devices.reshape(4, 2, 4, 4), PB_PA)
    in_specs = (
        P(PB_PA, None),
        P(PB_PA, None),
        P(PB_PA, None),
        P(PB_PA),
        P(PB_PA, None),
        P(PB_PA, None),
        P(PB_PA, None),
        P(),
        P(),
        P(),
    )
    out_specs = (P(PB_PA, None), P(PB_PA, None), P(PB_PA, None), P(None, PB_PA))
    return jax.shard_map(local, mesh=torus, in_specs=in_specs, out_specs=out_specs, check_vma=False)
```
